32 devices in a mesh: shot: 2 (over x), gx: 16 (over z, y, core).
Axes of the slice: x: 2, y: 2, z: 4, core: 2. Of those that a mesh axis runs over, the one named last changes fastest.
Arguments:
- source_field: float32 [512, 16, 128], P(('shot', 'gx')), parts along dimension 0, may hold values from -6 to 6
- source_prior: float32 [512, 16, 128], P(('shot', 'gx')), parts along dimension 0, may hold values from -6 to 6
- receiver_field: float32 [512, 16, 128], P(('shot', 'gx')), parts along dimension 0, may hold values from -6 to 6
- receiver_prior: float32 [512, 16, 128], P(('shot', 'gx')), parts along dimension 0, may hold values from -6 to 6
- stiffness: float32 [256, 16, 128], P('gx'), may hold values from 0.02 to 0.085
- buoyancy: float32 [256, 16, 128], P('gx'), may hold values from 0.5 to 2
- wavelet: float32 [32, 8], P('shot'), parts along dimension 0, may hold values from -6 to 6
- fire_step: int32 [32], P('shot'), parts along dimension 0, may hold values from 0 to 7
- shot_cell: int32 [32], P('shot'), parts along dimension 0, may hold values from 0 to 4095
- receiver_cell: int32 [4096], P('shot'), parts along dimension 0, may hold values from 0 to 4095
- traces: float32 [16, 2048], P('shot', 'gx'), parts along dimension 0, may hold values from -6 to 6
Outputs:
- image_sum: float32 [66, 256, 16, 128], P('shot', 'gx'), parts along dimension 0
The draws below stay inside these ranges and needn't reach their ends.
There are 2 independent parts, one for each index of `shot`. The reference program is written for one: setup_inputs(seed, part) draws one part's arguments, and reference() takes and returns one part's arrays. A program takes and returns all parts, laid end to end along the dimension named above; an argument that names none is the same for every part. Nothing has to cross between parts.
All inputs are finite; a program needn't handle non-finite values.
Results may differ from the reference program's by a relative error of at most 0.0003.
Values sent between devices are 32-bit elements; how exact they have to be, the bound alone decides.
No kernel may reach another device: no remote copies, remote signals or barrier semaphores. Data moves between devices by JAX's collectives and lax.ppermute only.
A program may use at most 64 MiB of HBM per device.

```python
import math
import jax
import jax.numpy as jnp

NY = 16
NZ = 128
STEPS = 8
IMG_EVERY = 4
NOFF = 33
SURFACE = 4
NSRC = 16
HALF = 16
NX = 256
NREC = 2048


def set_ends(array, key, smallest, top_value):
    longest = array.shape.index(max(array.shape))
    spots = []
    for shift in (0, 1):
        where = [jax.random.randint(jax.random.fold_in(key, axis), (), 0, length) for axis, length in enumerate(array.shape)]
        where[longest] = (where[longest] + shift) % array.shape[longest]
        spots.append(tuple(where))
    return array.at[spots[0]].set(smallest).at[spots[1]].set(top_value)


def block_levels(stream_key, shape, split, smallest, largest):
    def one(axis_at, blocks):
        steps = jax.random.uniform(jax.random.fold_in(jax.random.fold_in(stream_key, 6), axis_at), (blocks,), jnp.float32, smallest / len(split), largest / len(split))
        return jnp.repeat(jnp.exp(steps), shape[axis_at] // blocks).reshape((-1,) + (1,) * (len(shape) - axis_at - 1))

    gain = one(*split[0])
    for cut in split[1:]:
        gain = gain * one(*cut)
    return gain


def gaussian(stream_key, dims, deviation, limit, cuts=(), kind=jnp.bfloat16):
    loudness = block_levels(stream_key, dims, cuts, -0.22, 0.18) if cuts else 1.0
    entries = jax.random.normal(stream_key, dims, jnp.float32) * deviation * loudness
    return jnp.minimum(jnp.maximum(entries, -limit), limit).astype(kind)


def setup_inputs(seed: int = 0, part: int = 0) -> dict:
    key_list = jax.random.split(jax.random.key(seed), 12)
    part_keys = jax.random.split(jax.random.fold_in(key_list[11], part), 12)
    return {
        "source_field": gaussian(part_keys[0], (NX, NY, NZ), 1.0, 6.0, ((0, 16),), jnp.float32),
        "source_prior": gaussian(part_keys[1], (NX, NY, NZ), 1.0, 6.0, ((0, 16),), jnp.float32),
        "receiver_field": gaussian(part_keys[2], (NX, NY, NZ), 1.0, 6.0, ((0, 16),), jnp.float32),
        "receiver_prior": gaussian(part_keys[3], (NX, NY, NZ), 1.0, 6.0, ((0, 16),), jnp.float32),
        "stiffness": jnp.clip(jnp.exp(math.log(0.085) - 1.446919 * jax.random.uniform(key_list[4], (NX, NY, NZ), jnp.float32) ** block_levels(key_list[4], (NX, NY, NZ), ((0, 16),), -0.2, 0.2)), 0.02, 0.085),
        "buoyancy": jnp.clip(jnp.exp(math.log(2.0) - 1.3862944 * jax.random.uniform(key_list[5], (NX, NY, NZ), jnp.float32) ** block_levels(key_list[5], (NX, NY, NZ), ((0, 16),), -0.2, 0.2)), 0.5, 2.0),
        "wavelet": gaussian(part_keys[6], (NSRC, STEPS), 1.0, 6.0, (), jnp.float32),
        "fire_step": set_ends(jax.random.randint(part_keys[7], (NSRC,), 0, STEPS), jax.random.fold_in(part_keys[7], 1), 0, STEPS - 1).astype(jnp.int32),
        "shot_cell": set_ends(jax.random.randint(part_keys[8], (NSRC,), 0, NX * NY), jax.random.fold_in(part_keys[8], 1), 0, (NX * NY) - 1).astype(jnp.int32),
        "receiver_cell": set_ends(jax.random.randint(part_keys[9], (NREC,), 0, NX * NY), jax.random.fold_in(part_keys[9], 1), 0, (NX * NY) - 1).astype(jnp.int32),
        "traces": gaussian(part_keys[10], (STEPS, NREC), 1.0, 6.0, ((1, 16),), jnp.float32),
    }


stencil_weights = (1.6, -0.2, 8.0 / 315.0, -1.0 / 560.0)


def window(padded, direction, offset, extent):
    starts = [4, 4, 4]
    starts[direction] = starts[direction] + offset
    return padded[starts[0]:starts[0] + extent[0], starts[1]:starts[1] + extent[1], starts[2]:starts[2] + extent[2]]


def laplace(wavefield, buoyant):
    extent = (wavefield.shape[0] - 8, wavefield.shape[1], wavefield.shape[2])
    padded_field = jnp.pad(wavefield, ((0, 0), (4, 4), (4, 4)))
    padded_buoyant = jnp.pad(buoyant, ((0, 0), (4, 4), (4, 4)))
    centre_field = window(padded_field, 0, 0, extent)
    centre_buoyant = window(padded_buoyant, 0, 0, extent)
    accumulated = jnp.zeros(extent, jnp.float32)
    for direction in range(3):
        for distance in range(4):
            for orientation in (1, -1):
                other_field = window(padded_field, direction, orientation * (distance + 1), extent)
                other_buoyant = window(padded_buoyant, direction, orientation * (distance + 1), extent)
                accumulated = accumulated + stencil_weights[distance] * (0.5 * (centre_buoyant + other_buoyant)) * (other_field - centre_field)
    return accumulated


def inject_plane(cell_index, amounts, start_row, span_rows, lateral):
    inline = cell_index // lateral
    crossline = cell_index % lateral
    relative = inline - start_row
    inside = (relative >= 0) & (relative < span_rows)
    target = jnp.where(inside, relative * lateral + crossline, span_rows * lateral)
    summed = jax.ops.segment_sum(jnp.where(inside, amounts, 0.0), target, num_segments=span_rows * lateral + 1)
    return summed[:span_rows * lateral].reshape(span_rows, lateral)


def wavelet_amounts(wavelet, fire_step, moment):
    delays = moment - fire_step
    choose = jnp.arange(wavelet.shape[1], dtype=jnp.int32)[None, :] == delays[:, None]
    return jnp.sum(jnp.where(choose, wavelet, 0.0), axis=1)


def advance(current, prior_field, buoyant, stiff_cells, source_term):
    centre_cells = current[4:current.shape[0] - 4]
    updated = 2.0 * centre_cells - prior_field + stiff_cells * laplace(current, buoyant)
    return updated.at[:, :, SURFACE].add(source_term)


def correlate(lag_source, lag_receiver, span_rows):
    pieces = []
    for offset_index in range(NOFF):
        lag_shift = offset_index - HALF
        pieces.append(lag_source[HALF - lag_shift:HALF - lag_shift + span_rows] * lag_receiver[HALF + lag_shift:HALF + lag_shift + span_rows])
    return jnp.stack(pieces, 0)


def reference(source_field, source_prior, receiver_field, receiver_prior, stiffness, buoyancy, wavelet, fire_step, shot_cell, receiver_cell, traces):
    pad_stencil = ((4, 4), (0, 0), (0, 0))
    pad_lag = ((HALF, HALF), (0, 0), (0, 0))
    padded_buoyant = jnp.pad(buoyancy, pad_stencil)
    source_now, source_before = source_field, source_prior
    receiver_now, receiver_before = receiver_field, receiver_prior
    image_sum = None
    for moment in range(STEPS + 1):
        if moment % IMG_EVERY == 0:
            product = correlate(jnp.pad(source_now, pad_lag), jnp.pad(receiver_now, pad_lag), NX)
            image_sum = product if moment == 0 else image_sum + product
        if moment < STEPS:
            source_term = inject_plane(shot_cell, wavelet_amounts(wavelet, fire_step, moment), 0, NX, NY)
            receiver_term = inject_plane(receiver_cell, traces[STEPS - 1 - moment], 0, NX, NY)
            source_next = advance(jnp.pad(source_now, pad_stencil), source_before, padded_buoyant, stiffness, source_term)
            receiver_next = advance(jnp.pad(receiver_now, pad_stencil), receiver_before, padded_buoyant, stiffness, receiver_term)
            source_before, source_now = source_now, source_next
            receiver_before, receiver_now = receiver_now, receiver_next
    return image_sum
```

```python
import functools

import jax
import jax.numpy as jnp
from jax import lax
from jax.experimental import pallas as pl
from jax.experimental.pallas import tpu as pltpu
from jax.sharding import PartitionSpec as P

STEPS = 8
IMG_EVERY = 4
NOFF = 33
SURFACE = 4
HALF = 16
REACH = 4
TRIM = HALF - REACH
PAD = 8

SCALE = 5040.0
WHOLE = (8064.0, -1008.0, 128.0, -9.0)
CENTRE = 6.0 * sum(WHOLE)

f32 = jnp.float32
bf16 = jnp.bfloat16


def vmem_specs(count):
    return [pl.BlockSpec(memory_space=pltpu.VMEM)] * count


def params(megabytes):
    return pltpu.CompilerParams(vmem_limit_bytes=megabytes * 1024 * 1024)


def shape(*dims):
    return jax.ShapeDtypeStruct(dims, f32)


def parity():
    return lax.rem(lax.axis_index("gx"), 2)


def split2(value):
    high = value.astype(bf16)
    low = (value - high.astype(f32)).astype(bf16)
    return high, low


def split3(value):
    high = value.astype(bf16)
    rest = value - high.astype(f32)
    mid = rest.astype(bf16)
    low = (rest - mid.astype(f32)).astype(bf16)
    return high, mid, low


def depth_matrix(nz):
    row = lax.broadcasted_iota(jnp.int32, (nz, nz), 0)
    col = lax.broadcasted_iota(jnp.int32, (nz, nz), 1)
    gap = jnp.abs(row - col)
    band = jnp.zeros((nz, nz), f32)
    for k, weight in enumerate(WHOLE):
        band = jnp.where(gap == k + 1, weight, band)
    band = band.astype(bf16)
    return jnp.concatenate([band, band], axis=0)


def weighted_sum(ref, r0, depth):
    ny = ref.shape[1] - 2 * PAD
    nz = ref.shape[2]
    tiles = ny // 8
    block = ref[pl.ds(r0, 8), PAD : PAD + ny, :].reshape(8 * ny, nz)
    high, low = split2(block)
    along = jnp.dot(jnp.concatenate([high, low], axis=1), depth, preferred_element_type=f32)
    out = {}
    for t in range(tiles):
        at = PAD + 8 * t
        column = [ref[r0 - REACH + m, at : at + 8, :] for m in range(8 + 2 * REACH)]
        for i in range(8):
            row = i * ny + 8 * t
            total = along[row : row + 8]
            for k in range(1, REACH + 1):
                four = (column[i + REACH + k] + column[i + REACH - k]) + (
                    ref[r0 + i, at + k : at + k + 8, :] + ref[r0 + i, at - k : at - k + 8, :]
                )
                total = total + WHOLE[k - 1] * four
            out[i, t] = total
    return out


def clear_pads(ref):
    zero = jnp.zeros((ref.shape[0], PAD, ref.shape[2]), f32)
    ref[:, 0:PAD, :] = zero
    ref[:, ref.shape[1] - PAD :, :] = zero


def pack_kernel(s0, sp, r0, rp, stiff, buoy, od1, od2, ev1, ev2):
    p = parity()
    n = s0.shape[0]
    for full, trimmed, first in ((od1, od2, p), (ev1, ev2, 1 - p)):
        cut = pl.ds(REACH * first, TRIM)
        full[0:n] = buoy[...]
        full[n : n + TRIM] = stiff[cut]
        full[n + TRIM : 2 * n + TRIM] = s0[...]
        full[2 * n + TRIM :] = sp[cut]
        trimmed[0:n] = r0[...]
        trimmed[n:] = rp[cut]


def planes_kernel(cells, traces, shots, fire, wavelet, ps, pr, lhs, acc):
    groups, width = cells.shape
    span, lateral, nz = ps.shape
    nt = traces.shape[1]
    ns = shots.shape[1]
    me = lax.axis_index("gx")
    first_cell = (me * HALF - TRIM) * lateral
    chunk = 8 * lateral
    spread = jnp.broadcast_to(fire[...], (ns, ns))
    same = lax.broadcasted_iota(jnp.int32, (ns, ns), 0) == lax.broadcasted_iota(jnp.int32, (ns, ns), 1)
    fire_col = jnp.sum(jnp.where(same, spread.astype(f32), 0.0), axis=1, keepdims=True)
    lane = lax.broadcasted_iota(jnp.int32, (ns, nz), 1).astype(f32)
    amounts = jnp.zeros((ns, nz), f32)
    for d in range(wavelet.shape[1]):
        amounts = amounts + jnp.where(lane == fire_col + float(d), wavelet[:, d : d + 1], 0.0)
    parts = split3(amounts)
    shot_row = shots[...] - first_cell
    for c in range(span // 8):
        spot = lax.broadcasted_iota(jnp.int32, (chunk, ns), 0) + c * chunk
        hot = jnp.where(spot == shot_row, 1.0, 0.0).astype(bf16)
        total = jnp.zeros((chunk, nz), f32)
        for part in parts:
            total = total + jnp.dot(hot, part, preferred_element_type=f32)
        ps[8 * c : 8 * c + 8] = total.reshape(8, lateral, nz)
    def stage(j, carry):
        for half in range(2):
            block = traces[2 * j + half]
            back = jnp.concatenate([block[nt - 1 - t : nt - t] for t in range(nt)], axis=0)
            for q, part in enumerate(split3(back)):
                lhs[j, q * nt : (q + 1) * nt, half * width : (half + 1) * width] = part.astype(f32)
        return carry

    lax.fori_loop(0, groups // 2, stage, 0)
    acc[...] = jnp.zeros(acc.shape, f32)

    def gather(j, carry):
        a = jnp.bitwise_xor(me, 2 * j)
        b = jnp.bitwise_xor(me, 2 * j + 1)
        row = jnp.concatenate([cells[pl.ds(a, 1), :], cells[pl.ds(b, 1), :]], axis=1) - first_cell
        amounts_j = lhs[j].astype(bf16)
        for c in range(span // 8):
            spot = lax.broadcasted_iota(jnp.int32, (chunk, 2 * width), 0) + c * chunk
            hot = jnp.where(spot == row, 1.0, 0.0).astype(bf16)
            acc[c * chunk : (c + 1) * chunk, 0 : 3 * nt] += lax.dot_general(
                hot, amounts_j, (((1,), (1,)), ((), ())), preferred_element_type=f32
            )
        return carry

    lax.fori_loop(0, groups // 2, gather, 0)
    for c in range(span // 8):
        part = acc[c * chunk : (c + 1) * chunk]
        part = part + pltpu.roll(part, nz - nt, axis=1) + pltpu.roll(part, nz - 2 * nt, axis=1)
        pr[8 * c : 8 * c + 8] = part.reshape(8, lateral, nz)


def load_field(dst, own, od, ev, lo, n, full, p):
    rows = own.shape[0]
    inner = slice(PAD, PAD + own.shape[1])
    dst[rows : 2 * rows, inner, :] = own[...]
    skip = 0 if full else REACH
    dst[pl.ds(2 * rows * p + skip * (1 - p), n), inner, :] = od[lo : lo + n]
    dst[pl.ds(2 * rows * (1 - p) + skip * p, n), inner, :] = ev[lo : lo + n]


def run_steps(field, product, coefs, planes, depth, base, ny):
    buoy, kb, kk, gg = coefs
    wide = field.shape[1]
    nz = field.shape[3]
    surface = lax.broadcasted_iota(jnp.int32, (8, nz), 1) == SURFACE
    for step in range(IMG_EVERY):
        now, new = step % 2, 1 - step % 2
        first = REACH * (step + 1)
        shift = (SURFACE - (base + step)) % nz

        def chunk(c, carry, now=now, new=new, first=first, shift=shift, step=step):
            r0 = first + 8 * c
            plain = weighted_sum(field.at[now], r0, depth)
            scaled = weighted_sum(product.at[now], r0, depth)
            for (i, t), value in plain.items():
                at = PAD + 8 * t
                tile = slice(8 * t, 8 * t + 8)
                r = r0 + i
                term = planes[r - REACH, tile, :]
                if shift:
                    term = pltpu.roll(term, shift, axis=1)
                term = jnp.where(surface, term, 0.0)
                fresh = (
                    (gg[r, tile, :] * field[now, r, at : at + 8, :] - field[new, r, at : at + 8, :])
                    + (kb[r, tile, :] * value + kk[r, tile, :] * scaled[i, t])
                    + term
                )
                field[new, r, at : at + 8, :] = fresh
                if step < IMG_EVERY - 1:
                    product[new, r, at : at + 8, :] = buoy[r, tile, :] * fresh
            return carry

        lax.fori_loop(0, (wide - 2 * first) // 8, chunk, 0)


def start_products(field, product, buoy, ny):
    inner = slice(PAD, PAD + ny)
    for which in range(2):
        clear_pads(field.at[which])
        clear_pads(product.at[which])
    product[0, :, inner, :] = buoy[...] * field[0, :, inner, :]


def first_kernel(own, prior, stiff, buoy_own, od, ev, planes, now_out, before_out, od_out, ev_out, buoy, kb, kk, gg, field, product, base):
    p = parity()
    n, ny, nz = own.shape
    inner = slice(PAD, PAD + ny)
    depth = depth_matrix(nz)
    pad_buoy = product.at[1]
    clear_pads(pad_buoy)
    load_field(pad_buoy, buoy_own, od, ev, 0, n, True, p)
    load_field(field.at[1], stiff, od, ev, n, TRIM, False, p)
    buoy[...] = pad_buoy[:, inner, :]

    def coefficients(c, carry):
        r0 = REACH + 8 * c
        total = weighted_sum(pad_buoy, r0, depth)
        for (i, t), value in total.items():
            tile = slice(8 * t, 8 * t + 8)
            r = r0 + i
            at = PAD + 8 * t
            b = pad_buoy[r, at : at + 8, :]
            k = field[1, r, at : at + 8, :] * (0.5 / SCALE)
            kk[r, tile, :] = k
            kb[r, tile, :] = k * b
            gg[r, tile, :] = 2.0 - k * (CENTRE * b + value)
        return carry

    lax.fori_loop(0, (3 * n - 2 * REACH) // 8, coefficients, 0)
    load_field(field.at[0], own, od, ev, n + TRIM, n, True, p)
    load_field(field.at[1], prior, od, ev, 2 * n + TRIM, TRIM, False, p)
    start_products(field, product, buoy, ny)
    run_steps(field, product, (buoy, kb, kk, gg), planes, depth, base, ny)
    finish(field, now_out, before_out, od_out, ev_out, p, n, inner)


def finish(field, now_out, before_out, od_out, ev_out, p, n, inner):
    last, earlier = IMG_EVERY % 2, 1 - IMG_EVERY % 2
    value = field[last, n : 2 * n, inner, :]
    now_out[...] = value
    before_out[...] = field[earlier, n : 2 * n, inner, :]
    od_out[0:n] = value
    ev_out[0:n] = value
    od_out[n:] = field[earlier, pl.ds(n + REACH * p, TRIM), inner, :]
    ev_out[n:] = field[earlier, pl.ds(n + REACH * (1 - p), TRIM), inner, :]


def block_kernel(own, prior, od, ev, planes, buoy, kb, kk, gg, now_out, before_out, od_out, ev_out, field, product, base):
    p = parity()
    n, ny, nz = own.shape
    inner = slice(PAD, PAD + ny)
    depth = depth_matrix(nz)
    load_field(field.at[0], own, od, ev, 0, n, True, p)
    load_field(field.at[1], prior, od, ev, n, TRIM, False, p)
    start_products(field, product, buoy, ny)
    run_steps(field, product, (buoy, kb, kk, gg), planes, depth, base, ny)
    finish(field, now_out, before_out, od_out, ev_out, p, n, inner)


def last_kernel(own, prior, od, ev, planes, buoy, kb, kk, gg, now_out, field, product, base):
    p = parity()
    n, ny, nz = own.shape
    inner = slice(PAD, PAD + ny)
    depth = depth_matrix(nz)
    load_field(field.at[0], own, od, ev, 0, n, True, p)
    load_field(field.at[1], prior, od, ev, n, TRIM, False, p)
    start_products(field, product, buoy, ny)
    run_steps(field, product, (buoy, kb, kk, gg), planes, depth, base, ny)
    now_out[...] = field[IMG_EVERY % 2, n : 2 * n, inner, :]


def image_kernel(s0, s4, s8, r0, r4, r8, od1, ev1, od2, ev2, ods, evs, odr, evr, ods8, evs8, odr8, evr8, out, lag_s, lag_r, block, sems):
    p = parity()
    n, ny, nz = s0.shape
    left, right = 2 * n * p, 2 * n * (1 - p)
    groups = (
        (lag_s, 0, s0, od1, ev1, n + TRIM),
        (lag_r, 0, r0, od2, ev2, 0),
        (lag_s, 1, s4, ods, evs, 0),
        (lag_r, 1, r4, odr, evr, 0),
        (lag_s, 2, s8, ods8, evs8, 0),
        (lag_r, 2, r8, odr8, evr8, 0),
    )
    for dst, level, own, od, ev, lo in groups:
        dst[level, n : 2 * n] = own[...]
        dst[level, pl.ds(left, n)] = od[lo : lo + n]
        dst[level, pl.ds(right, n)] = ev[lo : lo + n]

    def one(j, carry):
        lag = j - HALF
        for x in range(n):
            total = lag_s[0, HALF + x - lag] * lag_r[0, HALF + x + lag]
            for level in (1, 2):
                total = total + lag_s[level, HALF + x - lag] * lag_r[level, HALF + x + lag]
            block[j, x] = total
        pltpu.make_async_copy(block.at[j], out.at[j], sems.at[j]).start()
        return carry

    lax.fori_loop(0, NOFF, one, 0)

    def drain(j, carry):
        pltpu.make_async_copy(block.at[j], out.at[j], sems.at[j]).wait()
        return carry

    lax.fori_loop(0, NOFF, drain, 0)


def estimate(flops, nbytes):
    return pl.CostEstimate(flops=flops, bytes_accessed=nbytes, transcendentals=0)


def local(source_field, source_prior, receiver_field, receiver_prior, stiffness, buoyancy, wavelet, fire_step, shot_cell, receiver_cell, traces):
    n, ny, nz = source_field.shape
    count = lax.axis_size("gx")
    near = [(i, i ^ 1) for i in range(count)]
    far = [(i, i + 1) for i in range(1, count - 1, 2)] + [(i + 1, i) for i in range(1, count - 1, 2)]
    swap_near = lambda x: lax.ppermute(x, "gx", near)
    swap_far = lambda x: lax.ppermute(x, "gx", far)

    big, small = 2 * n + 2 * TRIM + 0, n + TRIM
    od1, od2, ev1, ev2 = pl.pallas_call(
        pack_kernel,
        out_shape=[shape(big, ny, nz), shape(small, ny, nz)] * 2,
        in_specs=vmem_specs(6),
        out_specs=vmem_specs(4),
        compiler_params=params(8),
        name="pack",
    )(source_field, source_prior, receiver_field, receiver_prior, stiffness, buoyancy)
    od1 = swap_far(od1)
    ev1 = swap_near(ev1)
    od2 = swap_far(od2)
    ev2 = swap_near(ev2)

    gathered = traces[None]
    hop = 1
    while hop < count:
        gathered = jnp.concatenate([gathered, lax.ppermute(gathered, "gx", [(i, i ^ hop) for i in range(count)])], axis=0)
        hop *= 2

    span = n + 2 * TRIM
    width = traces.shape[1]
    ns = shot_cell.shape[0]
    plane_s, plane_r = pl.pallas_call(
        planes_kernel,
        out_shape=[shape(span, ny, nz)] * 2,
        in_specs=vmem_specs(5),
        out_specs=vmem_specs(2),
        scratch_shapes=[
            pltpu.VMEM((count // 2, 3 * traces.shape[0], 2 * width), f32),
            pltpu.VMEM((span * ny, nz), f32),
        ],
        compiler_params=params(8),
        cost_estimate=estimate(2 * span * ny * 24 * 2048, 1000000),
        name="planes",
    )(receiver_cell.reshape(count, width), gathered, shot_cell.reshape(1, ns), fire_step.reshape(1, ns), wavelet)

    wide = 3 * n
    scratch = [pltpu.VMEM((2, wide, ny + 2 * PAD, nz), f32)] * 2
    cost = estimate(224 * 8 * 128 * 60, 6000000)
    own = shape(n, ny, nz)
    s4, s3, ods, evs, buoy, kb, kk, gg = pl.pallas_call(
        functools.partial(first_kernel, base=0),
        out_shape=[own, own, shape(small, ny, nz), shape(small, ny, nz)] + [shape(wide, ny, nz)] * 4,
        in_specs=vmem_specs(7),
        out_specs=vmem_specs(8),
        scratch_shapes=scratch,
        compiler_params=params(16),
        cost_estimate=cost,
        name="first_s",
    )(source_field, source_prior, stiffness, buoyancy, od1, ev1, plane_s)
    coefs = (buoy, kb, kk, gg)
    ods = swap_far(ods)
    evs = swap_near(evs)
    block = pl.pallas_call(
        functools.partial(block_kernel, base=0),
        out_shape=[own, own, shape(small, ny, nz), shape(small, ny, nz)],
        in_specs=vmem_specs(9),
        out_specs=vmem_specs(4),
        scratch_shapes=scratch,
        compiler_params=params(16),
        cost_estimate=cost,
        name="first_r",
    )
    r4, r3, odr, evr = block(receiver_field, receiver_prior, od2, ev2, plane_r, *coefs)
    odr = swap_far(odr)
    evr = swap_near(evr)

    def last(name):
        return pl.pallas_call(
            functools.partial(last_kernel, base=IMG_EVERY),
            out_shape=own,
            in_specs=vmem_specs(9),
            out_specs=pl.BlockSpec(memory_space=pltpu.VMEM),
            scratch_shapes=scratch,
            compiler_params=params(16),
            cost_estimate=cost,
            name=name,
        )

    s8 = last("last_s")(s4, s3, ods, evs, plane_s, *coefs)
    ods8 = swap_far(s8)
    evs8 = swap_near(s8)
    r8 = last("last_r")(r4, r3, odr, evr, plane_r, *coefs)
    odr8 = swap_far(r8)
    evr8 = swap_near(r8)
    return pl.pallas_call(
        image_kernel,
        out_shape=shape(NOFF, n, ny, nz),
        in_specs=vmem_specs(18),
        out_specs=pl.BlockSpec(memory_space=pl.ANY),
        scratch_shapes=[
            pltpu.VMEM((3, wide, ny, nz), f32),
            pltpu.VMEM((3, wide, ny, nz), f32),
            pltpu.VMEM((NOFF, n, ny, nz), f32),
            pltpu.SemaphoreType.DMA((NOFF,)),
        ],
        compiler_params=params(24),
        cost_estimate=estimate(NOFF * n * ny * nz * 5, 4400000),
        name="image",
    )(source_field, s4, s8, receiver_field, r4, r8, od1, ev1, od2, ev2, ods, evs, odr, evr, ods8, evs8, odr8, evr8)


def solution(mesh):
    placed = (
        P(("shot", "gx"), None, None),
        P(("shot", "gx"), None, None),
        P(("shot", "gx"), None, None),
        P(("shot", "gx"), None, None),
        P("gx", None, None),
        P("gx", None, None),
        P("shot", None),
        P("shot"),
        P("shot"),
        P("shot"),
        P("shot", "gx"),
    )
    return jax.shard_map(local, mesh=mesh, in_specs=placed, out_specs=P("shot", "gx", None, None), check_vma=False)
```

```python
import functools

import jax
import jax.numpy as jnp
from jax import lax
from jax.experimental import pallas as pl
from jax.experimental.pallas import tpu as pltpu
from jax.sharding import PartitionSpec as P


STEPS = 8
IMG_EVERY = 4
NOFF = 33
SURFACE = 4
HALF = 16
REACH = 4
TRIM = HALF - REACH
PAD = 8

SCALE = 5040.0
WHOLE = (8064.0, -1008.0, 128.0, -9.0)
CENTRE = 6.0 * sum(WHOLE)

f32 = jnp.float32
bf16 = jnp.bfloat16


def vmem_specs(count):
    return [pl.BlockSpec(memory_space=pltpu.VMEM)] * count


def params(megabytes):
    return pltpu.CompilerParams(vmem_limit_bytes=megabytes * 1024 * 1024)


def shape(*dims):
    return jax.ShapeDtypeStruct(dims, f32)


def place():
    me = lax.axis_index("gx")
    return lax.rem(me, 2), (me > 0) & (me < lax.axis_size("gx") - 1)


def split2(value):
    high = value.astype(bf16)
    low = (value - high.astype(f32)).astype(bf16)
    return high, low


def split3(value):
    high = value.astype(bf16)
    rest = value - high.astype(f32)
    mid = rest.astype(bf16)
    low = (rest - mid.astype(f32)).astype(bf16)
    return high, mid, low


def depth_matrix(nz):
    row = lax.broadcasted_iota(jnp.int32, (nz, nz), 0)
    col = lax.broadcasted_iota(jnp.int32, (nz, nz), 1)
    gap = jnp.abs(row - col)
    band = jnp.zeros((nz, nz), f32)
    for k, weight in enumerate(WHOLE):
        band = jnp.where(gap == k + 1, weight, band)
    band = band.astype(bf16)
    return jnp.concatenate([band, band], axis=0)


def along_depth(refs, r0, at, depth):
    nz = refs[0].shape[2]
    high, low = split2(jnp.concatenate([ref[pl.ds(r0, 8), pl.ds(at, 8), :].reshape(64, nz) for ref in refs], axis=0))
    return jnp.dot(jnp.concatenate([high, low], axis=1), depth, preferred_element_type=f32)


def across(ref, r0, at, i):
    total = None
    for k in range(1, REACH + 1):
        four = (ref[r0 + i + k, pl.ds(at, 8), :] + ref[r0 + i - k, pl.ds(at, 8), :]) + (
            ref[r0 + i, pl.ds(at + k, 8), :] + ref[r0 + i, pl.ds(at - k, 8), :]
        )
        total = WHOLE[k - 1] * four if total is None else total + WHOLE[k - 1] * four
    return total


def clear_pads(ref):
    zero = jnp.zeros((ref.shape[0], PAD, ref.shape[2]), f32)
    ref[:, 0:PAD, :] = zero
    ref[:, ref.shape[1] - PAD :, :] = zero


def pack_kernel(*refs):
    count = (len(refs) - 5) // 2
    args, copies, (od1, od2, ev1, ev2), sems = refs[:count], refs[count : 2 * count], refs[2 * count : -1], refs[-1]
    moves = [pltpu.make_async_copy(a, b, sems.at[i]) for i, (a, b) in enumerate(zip(args, copies))]
    for move in moves:
        move.start()
    for move in moves:
        move.wait()
    s0, sp, r0, rp, stiff, buoy = copies[:6]
    p, _ = place()
    n = s0.shape[0]
    for full, trimmed, first in ((od1, od2, p), (ev1, ev2, 1 - p)):
        cut = pl.ds(REACH * first, TRIM)
        full[0:n] = buoy[...]
        full[n : n + TRIM] = stiff[cut]
        full[n + TRIM : 2 * n + TRIM] = s0[...]
        full[2 * n + TRIM :] = sp[cut]
        trimmed[0:n] = r0[...]
        trimmed[n:] = rp[cut]


def first_plane_cell(lateral):
    return (lax.axis_index("gx") * HALF - TRIM) * lateral


def collect(acc, nt):
    nz = acc.shape[1]
    return acc + pltpu.roll(acc, nz - nt, axis=1) + pltpu.roll(acc, nz - 2 * nt, axis=1)


def hot_cells(base, row, rows):
    spot = lax.broadcasted_iota(jnp.int32, (rows, row.shape[1]), 0) + base
    return jnp.where(spot == row, 1.0, 0.0).astype(bf16)


def shots_kernel(shots, fire, wavelet, planes, acc):
    span, lateral, nz = planes.shape
    taps, ns = wavelet.shape
    delay = lax.broadcasted_iota(jnp.int32, (STEPS, ns), 0) - fire[...]
    amounts = jnp.zeros((STEPS, ns), f32)
    for d in range(taps):
        amounts = amounts + jnp.where(delay == d, wavelet[d : d + 1, :], 0.0)
    parts = jnp.concatenate([x.astype(f32) for x in split3(amounts)], axis=0).astype(bf16)
    row = shots[...] - first_plane_cell(lateral)
    chunk = 8 * lateral
    for c in range(span // 8):
        acc[:, 0 : 3 * STEPS] = lax.dot_general(
            hot_cells(c * chunk, row, chunk), parts, (((1,), (1,)), ((), ())), preferred_element_type=f32
        )
        planes[8 * c : 8 * c + 8] = collect(acc[...], STEPS).reshape(8, lateral, nz)


def receivers_kernel(cells, traces, planes, amounts, acc, hops):
    groups, width = cells.shape
    span, lateral, nz = planes.shape
    nt = traces.shape[1]
    me = lax.axis_index("gx")
    chunk = 8 * lateral

    def owner(q):
        other = me
        for bit, hop in enumerate(hops):
            other = jnp.bitwise_xor(other, hop * jnp.bitwise_and(lax.shift_right_logical(q, bit), 1))
        return other

    def stage(j, carry):
        for half in range(2):
            block = traces[2 * j + half]
            back = jnp.concatenate([block[nt - 1 - t : nt - t] for t in range(nt)], axis=0)
            for q, part in enumerate(split3(back)):
                amounts[j, q * nt : (q + 1) * nt, half * width : (half + 1) * width] = part.astype(f32)
        return carry

    lax.fori_loop(0, groups // 2, stage, 0)
    acc[...] = jnp.zeros(acc.shape, f32)

    def gather(j, carry):
        pair = [cells[pl.ds(owner(2 * j + half), 1), :] for half in range(2)]
        row = jnp.concatenate(pair, axis=1) - first_plane_cell(lateral)
        amounts_j = amounts[j].astype(bf16)
        for c in range(span // 8):
            acc[c * chunk : (c + 1) * chunk, 0 : 3 * nt] += lax.dot_general(
                hot_cells(c * chunk, row, chunk), amounts_j, (((1,), (1,)), ((), ())), preferred_element_type=f32
            )
        return carry

    lax.fori_loop(0, groups // 2, gather, 0)
    for c in range(span // 8):
        planes[8 * c : 8 * c + 8] = collect(acc[c * chunk : (c + 1) * chunk], nt).reshape(8, lateral, nz)


def load_field(dst, own, od, ev, lo, n, full):
    p, there = place()
    rows = own.shape[0]
    inner = slice(PAD, PAD + own.shape[1])
    dst[rows : 2 * rows, inner, :] = own[...]
    skip = 0 if full else REACH
    dst[pl.ds(2 * rows * p + skip * (1 - p), n), inner, :] = jnp.where(there, od[lo : lo + n], 0.0)
    dst[pl.ds(2 * rows * (1 - p) + skip * p, n), inner, :] = ev[lo : lo + n]


def run_steps(field, product, along, coefs, planes, depth, base):
    buoy, kb, kk, gg = coefs
    wide, tall, nz = field[0].shape
    tiles = (tall - 2 * PAD) // 8
    surface = lax.broadcasted_iota(jnp.int32, (8, nz), 1) == SURFACE
    for step in range(IMG_EVERY):
        old, new = field[step % 2], field[1 - step % 2]
        flux, flux_new = product[step % 2], product[1 - step % 2]
        first = REACH * (step + 1)
        shift = (SURFACE - (base + step)) % nz
        count = tiles * (wide - 2 * first) // 8

        def spot(q, first=first):
            y0 = pl.multiple_of(8 * lax.rem(q, tiles), 8)
            return first + 8 * lax.div(q, tiles), y0, pl.multiple_of(PAD + y0, 8)

        def chunk(q, carry, old=old, new=new, flux=flux, flux_new=flux_new, shift=shift, step=step, count=count, spot=spot):
            r0, y0, at = spot(q)
            slot = lax.rem(q, 2)
            later = spot(jnp.minimum(q + 1, count - 1))
            following = along_depth((old, flux), later[0], later[2], depth)
            tile = pl.ds(y0, 8)
            for i in range(8):
                r = r0 + i
                term = planes[r - REACH, tile, :]
                if shift:
                    term = pltpu.roll(term, shift, axis=1)
                part = gg[r, tile, :] * old[r, pl.ds(at, 8), :] - new[r, pl.ds(at, 8), :] + jnp.where(surface, term, 0.0)
                part = part + kb[r, tile, :] * (across(old, r0, at, i) + along[slot, 8 * i : 8 * i + 8, :])
                part = part + kk[r, tile, :] * (across(flux, r0, at, i) + along[slot, 64 + 8 * i : 72 + 8 * i, :])
                new[r, pl.ds(at, 8), :] = part
                if step < IMG_EVERY - 1:
                    flux_new[r, pl.ds(at, 8), :] = buoy[r, tile, :] * part
            along[1 - slot] = following
            return carry

        begin = spot(0)
        along[0] = along_depth((old, flux), begin[0], begin[2], depth)
        lax.fori_loop(0, count, chunk, 0)


def start_products(field, product, buoy):
    for ref in (*field, *product):
        clear_pads(ref)
    inner = slice(PAD, field[0].shape[1] - PAD)
    product[0][:, inner, :] = buoy[...] * field[0][:, inner, :]


def finish(field, n, now_out, before_out, od_out, ev_out):
    p, _ = place()
    last, earlier = field[IMG_EVERY % 2], field[1 - IMG_EVERY % 2]
    inner = slice(PAD, last.shape[1] - PAD)
    value = last[n : 2 * n, inner, :]
    now_out[...] = value
    before_out[...] = earlier[n : 2 * n, inner, :]
    od_out[0:n] = value
    ev_out[0:n] = value
    od_out[n:] = earlier[pl.ds(n + REACH * p, TRIM), inner, :]
    ev_out[n:] = earlier[pl.ds(n + REACH * (1 - p), TRIM), inner, :]


def first_kernel(own, prior, stiff, buoy_own, od, ev, planes, now_out, before_out, od_out, ev_out, buoy, kb, kk, gg, f0, f1, p0, p1, along):
    n, ny, nz = own.shape
    tiles = ny // 8
    inner = slice(PAD, PAD + ny)
    depth = depth_matrix(nz)
    clear_pads(p1)
    load_field(p1, buoy_own, od, ev, 0, n, True)
    load_field(f1, stiff, od, ev, n, TRIM, False)
    buoy[...] = p1[:, inner, :]

    def coefficients(q, carry):
        r0 = REACH + 8 * lax.div(q, tiles)
        y0 = pl.multiple_of(8 * lax.rem(q, tiles), 8)
        at = pl.multiple_of(PAD + y0, 8)
        tile = pl.ds(y0, 8)
        deep = along_depth((p1,), r0, at, depth)
        for i in range(8):
            r = r0 + i
            b = p1[r, pl.ds(at, 8), :]
            k = f1[r, pl.ds(at, 8), :] * (0.5 / SCALE)
            kk[r, tile, :] = k
            kb[r, tile, :] = k * b
            gg[r, tile, :] = 2.0 - k * (CENTRE * b + (across(p1, r0, at, i) + deep[8 * i : 8 * i + 8]))
        return carry

    lax.fori_loop(0, tiles * (3 * n - 2 * REACH) // 8, coefficients, 0)
    load_field(f0, own, od, ev, n + TRIM, n, True)
    load_field(f1, prior, od, ev, 2 * n + TRIM, TRIM, False)
    start_products((f0, f1), (p0, p1), buoy)
    run_steps((f0, f1), (p0, p1), along, (buoy, kb, kk, gg), planes, depth, 0)
    finish((f0, f1), n, now_out, before_out, od_out, ev_out)


def block_steps(own, prior, od, ev, planes, coefs, field, product, along, base):
    n, _, nz = own.shape
    depth = depth_matrix(nz)
    load_field(field[0], own, od, ev, 0, n, True)
    load_field(field[1], prior, od, ev, n, TRIM, False)
    start_products(field, product, coefs[0])
    run_steps(field, product, along, coefs, planes, depth, base)


def block_kernel(own, prior, od, ev, planes, buoy, kb, kk, gg, now_out, before_out, od_out, ev_out, f0, f1, p0, p1, along, base):
    block_steps(own, prior, od, ev, planes, (buoy, kb, kk, gg), (f0, f1), (p0, p1), along, base)
    finish((f0, f1), own.shape[0], now_out, before_out, od_out, ev_out)


def last_kernel(own, prior, od, ev, planes, buoy, kb, kk, gg, now_out, f0, f1, p0, p1, along, base):
    block_steps(own, prior, od, ev, planes, (buoy, kb, kk, gg), (f0, f1), (p0, p1), along, base)
    n, ny, _ = own.shape
    now_out[...] = (f0, f1)[IMG_EVERY % 2][n : 2 * n, PAD : PAD + ny, :]


def image_kernel(s0, s4, s8, r0, r4, r8, od1, ev1, od2, ev2, ods, evs, odr, evr, ods8, evs8, odr8, evr8, out, lag_s, lag_r, block, sems):
    p, there = place()
    n, _, _ = s0.shape
    left, right = 2 * n * p, 2 * n * (1 - p)
    groups = (
        (lag_s, 0, s0, od1, ev1, n + TRIM),
        (lag_r, 0, r0, od2, ev2, 0),
        (lag_s, 1, s4, ods, evs, 0),
        (lag_r, 1, r4, odr, evr, 0),
        (lag_s, 2, s8, ods8, evs8, 0),
        (lag_r, 2, r8, odr8, evr8, 0),
    )
    for dst, level, own, od, ev, lo in groups:
        dst[level, n : 2 * n] = own[...]
        dst[level, pl.ds(left, n)] = jnp.where(there, od[lo : lo + n], 0.0)
        dst[level, pl.ds(right, n)] = ev[lo : lo + n]

    def one(j, carry):
        lag = j - HALF
        for x in range(n):
            total = lag_s[0, HALF + x - lag] * lag_r[0, HALF + x + lag]
            for level in (1, 2):
                total = total + lag_s[level, HALF + x - lag] * lag_r[level, HALF + x + lag]
            block[j, x] = total
        pltpu.make_async_copy(block.at[j], out.at[j], sems.at[j]).start()
        return carry

    lax.fori_loop(0, NOFF, one, 0)

    def drain(j, carry):
        pltpu.make_async_copy(block.at[j], out.at[j], sems.at[j]).wait()
        return carry

    lax.fori_loop(0, NOFF, drain, 0)


def estimate(flops, nbytes):
    return pl.CostEstimate(flops=flops, bytes_accessed=nbytes, transcendentals=0)


def local(source_field, source_prior, receiver_field, receiver_prior, stiffness, buoyancy, wavelet, fire_step, shot_cell, receiver_cell, traces):
    n, ny, nz = source_field.shape
    shots, count = lax.axis_size("shot"), lax.axis_size("gx")
    near = [(i, i ^ 1) for i in range(count)]
    far = [(s * count + i, s * count + i + 1) for s in range(shots) for i in range(1, count - 1, 2)]
    far = far + [(b, a) for a, b in far]
    if shots % 2 == 0:
        far += [(s * count + e, (s ^ 1) * count + e) for s in range(shots) for e in (0, count - 1)]

    def swap_near(x):
        return lax.ppermute(x, "gx", near)

    def swap_far(x):
        return lax.ppermute(x, ("shot", "gx"), far)

    hops = []
    hop = 2
    while hop < count:
        hops.append(hop)
        hop *= 2
    hops.append(1)

    def exchange(x, which):
        return lax.ppermute(x, "gx", [(i, i ^ hops[which]) for i in range(count)])

    received = exchange(traces[None], 0)

    big, small = 2 * n + 2 * TRIM, n + TRIM
    width = traces.shape[1]
    ns = shot_cell.shape[0]
    args = (
        source_field,
        source_prior,
        receiver_field,
        receiver_prior,
        stiffness,
        buoyancy,
        traces[None],
        receiver_cell.reshape(count, width),
        shot_cell.reshape(1, ns),
        fire_step.reshape(1, ns),
        wavelet.T,
    )
    packed = pl.pallas_call(
        pack_kernel,
        out_shape=[jax.ShapeDtypeStruct(a.shape, a.dtype) for a in args] + [shape(big, ny, nz), shape(small, ny, nz)] * 2,
        in_specs=[pl.BlockSpec(memory_space=pltpu.MemorySpace.HBM)] * len(args),
        out_specs=vmem_specs(len(args) + 4),
        scratch_shapes=[pltpu.SemaphoreType.DMA((len(args),))],
        compiler_params=params(8),
        name="pack",
    )(*(pltpu.with_memory_space_constraint(a, pltpu.MemorySpace.HBM) for a in args))
    source_field, source_prior, receiver_field, receiver_prior, stiffness, buoyancy, gathered, cells, shot_row, fire_row, wave = packed[: len(args)]
    od1, od2, ev1, ev2 = packed[len(args) :]
    od1 = swap_far(od1)
    ev1 = swap_near(ev1)
    od2 = swap_far(od2)
    ev2 = swap_near(ev2)

    gathered = jnp.concatenate([gathered, received], axis=0)
    for which in range(1, len(hops)):
        gathered = jnp.concatenate([gathered, exchange(gathered, which)], axis=0)

    span = n + 2 * TRIM
    chunk = pltpu.VMEM((8 * ny, nz), f32)
    plane_s = pl.pallas_call(
        shots_kernel,
        out_shape=shape(span, ny, nz),
        in_specs=vmem_specs(3),
        out_specs=pl.BlockSpec(memory_space=pltpu.VMEM),
        scratch_shapes=[chunk],
        compiler_params=params(8),
        cost_estimate=estimate(1000000, 100000),
        name="shots",
    )(shot_row, fire_row, wave)
    plane_r = pl.pallas_call(
        functools.partial(receivers_kernel, hops=tuple(hops)),
        out_shape=shape(span, ny, nz),
        in_specs=vmem_specs(2),
        out_specs=pl.BlockSpec(memory_space=pltpu.VMEM),
        scratch_shapes=[pltpu.VMEM((count // 2, 3 * traces.shape[0], 2 * width), f32), pltpu.VMEM((span * ny, nz), f32)],
        compiler_params=params(8),
        cost_estimate=estimate(2 * span * ny * 24 * 2048, 1000000),
        name="receivers",
    )(cells, gathered)

    wide = 3 * n
    scratch = [pltpu.VMEM((wide, ny + 2 * PAD, nz), f32)] * 4 + [pltpu.VMEM((2, 128, nz), f32)]
    cost = estimate(224 * 8 * 128 * 60, 6000000)
    own = shape(n, ny, nz)
    s4, s3, ods, evs, buoy, kb, kk, gg = pl.pallas_call(
        first_kernel,
        out_shape=[own, own, shape(small, ny, nz), shape(small, ny, nz)] + [shape(wide, ny, nz)] * 4,
        in_specs=vmem_specs(7),
        out_specs=vmem_specs(8),
        scratch_shapes=scratch,
        compiler_params=params(16),
        cost_estimate=cost,
        name="first_s",
    )(source_field, source_prior, stiffness, buoyancy, od1, ev1, plane_s)
    coefs = (buoy, kb, kk, gg)
    ods = swap_far(ods)
    evs = swap_near(evs)
    r4, r3, odr, evr = pl.pallas_call(
        functools.partial(block_kernel, base=0),
        out_shape=[own, own, shape(small, ny, nz), shape(small, ny, nz)],
        in_specs=vmem_specs(9),
        out_specs=vmem_specs(4),
        scratch_shapes=scratch,
        compiler_params=params(16),
        cost_estimate=cost,
        name="first_r",
    )(receiver_field, receiver_prior, od2, ev2, plane_r, *coefs)
    odr = swap_far(odr)
    evr = swap_near(evr)

    def last():
        return pl.pallas_call(
            functools.partial(last_kernel, base=IMG_EVERY),
            out_shape=own,
            in_specs=vmem_specs(9),
            out_specs=pl.BlockSpec(memory_space=pltpu.VMEM),
            scratch_shapes=scratch,
            compiler_params=params(16),
            cost_estimate=cost,
        )

    s8 = last()(s4, s3, ods, evs, plane_s, *coefs)
    ods8 = swap_far(s8)
    evs8 = swap_near(s8)
    r8 = last()(r4, r3, odr, evr, plane_r, *coefs)
    odr8 = swap_far(r8)
    evr8 = swap_near(r8)
    return pl.pallas_call(
        image_kernel,
        out_shape=shape(NOFF, n, ny, nz),
        in_specs=vmem_specs(18),
        out_specs=pl.BlockSpec(memory_space=pl.ANY),
        scratch_shapes=[
            pltpu.VMEM((3, wide, ny, nz), f32),
            pltpu.VMEM((3, wide, ny, nz), f32),
            pltpu.VMEM((NOFF, n, ny, nz), f32),
            pltpu.SemaphoreType.DMA((NOFF,)),
        ],
        compiler_params=params(24),
        cost_estimate=estimate(NOFF * n * ny * nz * 5, 4400000),
        name="image",
    )(source_field, s4, s8, receiver_field, r4, r8, od1, ev1, od2, ev2, ods, evs, odr, evr, ods8, evs8, odr8, evr8)


def solution(mesh):
    placed = (
        P(("shot", "gx"), None, None),
        P(("shot", "gx"), None, None),
        P(("shot", "gx"), None, None),
        P(("shot", "gx"), None, None),
        P("gx", None, None),
        P("gx", None, None),
        P("shot", None),
        P("shot"),
        P("shot"),
        P("shot"),
        P("shot", "gx"),
    )
    return jax.shard_map(local, mesh=mesh, in_specs=placed, out_specs=P("shot", "gx", None, None), check_vma=False)
```

```python
import functools

import jax
import jax.numpy as jnp
from jax import lax
from jax.experimental import pallas as pl
from jax.experimental.pallas import tpu as pltpu
from jax.sharding import PartitionSpec as P


STEPS = 8
IMG_EVERY = 4
NOFF = 33
SURFACE = 4
HALF = 16
REACH = 4
TRIM = HALF - REACH
LANES = 48
PAD = 8

SCALE = 5040.0
WHOLE = (8064.0, -1008.0, 128.0, -9.0)
CENTRE = 6.0 * sum(WHOLE)

f32 = jnp.float32
bf16 = jnp.bfloat16


def vmem_specs(count):
    return [pl.BlockSpec(memory_space=pltpu.VMEM)] * count


def params(megabytes):
    return pltpu.CompilerParams(vmem_limit_bytes=megabytes * 1024 * 1024)


def shape(*dims):
    return jax.ShapeDtypeStruct(dims, f32)


def place():
    me = lax.axis_index("gx")
    return lax.rem(me, 2), (me > 0) & (me < lax.axis_size("gx") - 1)


def split2(value):
    high = value.astype(bf16)
    low = (value - high.astype(f32)).astype(bf16)
    return high, low


def split3(value):
    high = value.astype(bf16)
    rest = value - high.astype(f32)
    mid = rest.astype(bf16)
    low = (rest - mid.astype(f32)).astype(bf16)
    return high, mid, low


def depth_matrix(nz):
    row = lax.broadcasted_iota(jnp.int32, (nz, nz), 0)
    col = lax.broadcasted_iota(jnp.int32, (nz, nz), 1)
    gap = jnp.abs(row - col)
    band = jnp.zeros((nz, nz), f32)
    for k, weight in enumerate(WHOLE):
        band = jnp.where(gap == k + 1, weight, band)
    band = band.astype(bf16)
    return jnp.concatenate([band, band], axis=0)


def along_depth(refs, r0, depth):
    _, tall, nz = refs[0].shape
    ny = tall - 2 * PAD
    rows = [ref[r0 : r0 + 8, PAD : PAD + ny, :].reshape(8 * ny, nz) for ref in refs]
    high, low = split2(jnp.concatenate(rows, axis=0))
    return jnp.dot(jnp.concatenate([high, low], axis=1), depth, preferred_element_type=f32)


def across(ref, r0, at, i):
    total = None
    for k in range(1, REACH + 1):
        four = (ref[r0 + i + k, pl.ds(at, 8), :] + ref[r0 + i - k, pl.ds(at, 8), :]) + (
            ref[r0 + i, pl.ds(at + k, 8), :] + ref[r0 + i, pl.ds(at - k, 8), :]
        )
        total = WHOLE[k - 1] * four if total is None else total + WHOLE[k - 1] * four
    return total


def clear_pads(ref):
    zero = jnp.zeros((ref.shape[0], PAD, ref.shape[2]), f32)
    ref[:, 0:PAD, :] = zero
    ref[:, ref.shape[1] - PAD :, :] = zero


def pack_kernel(*refs, count):
    args, copies, sems = refs[:count], refs[count : 2 * count], refs[-1]
    far_coef, far_prior, far_r, near_s, near_r = refs[2 * count : -1]
    moves = [pltpu.make_async_copy(a, b, sems.at[i]) for i, (a, b) in enumerate(zip(args, copies))]
    for move in moves:
        move.start()
    for move in moves:
        move.wait()
    s0, sp, r0, rp, stiff, buoy = copies[:6]
    p, _ = place()
    n = s0.shape[0]
    far_cut, near_cut = pl.ds(REACH * p, TRIM), pl.ds(REACH * (1 - p), TRIM)
    far_coef[0:n] = buoy[...]
    far_coef[n:] = stiff[far_cut]
    far_prior[...] = sp[far_cut]
    far_r[0:n] = r0[...]
    far_r[n:] = rp[far_cut]
    near_s[0:n] = buoy[...]
    near_s[n : n + TRIM] = stiff[near_cut]
    near_s[n + TRIM : 2 * n + TRIM] = s0[...]
    near_s[2 * n + TRIM :] = sp[near_cut]
    near_r[0:n] = r0[...]
    near_r[n:] = rp[near_cut]


def spread(cells, parts, lateral, steps):
    width = cells.shape[1]
    bits = lateral.bit_length() - 1
    crossline = jnp.bitwise_and(cells, lateral - 1)
    inline = lax.shift_right_arithmetic(cells, bits) - (lax.axis_index("gx") * HALF - TRIM)
    here = lax.broadcasted_iota(jnp.int32, (lateral, width), 0) == crossline
    hot = jnp.where(lax.broadcasted_iota(jnp.int32, (LANES, width), 0) == inline, 1.0, 0.0).astype(bf16)
    total = None
    for part in parts:
        part = part.astype(f32)
        rows = [jnp.where(here, part[t : t + 1], 0.0) for t in range(steps)]
        term = lax.dot_general(
            jnp.concatenate(rows, axis=0).astype(bf16), hot, (((1,), (1,)), ((), ())), preferred_element_type=f32
        )
        total = term if total is None else total + term
    return total


def shots_kernel(shots, fire, wavelet, planes):
    steps, lateral, _ = planes.shape
    taps, ns = wavelet.shape
    delay = lax.broadcasted_iota(jnp.int32, (steps, ns), 0) - fire[...]
    amounts = jnp.zeros((steps, ns), f32)
    for d in range(taps):
        amounts = amounts + jnp.where(delay == d, wavelet[d : d + 1, :], 0.0)
    total = spread(shots[...], split3(amounts), lateral, steps)
    planes[:, :, 0:LANES] = total.reshape(steps, lateral, LANES)


def receivers_kernel(cells, traces, planes, acc, hops):
    groups = cells.shape[0]
    steps, lateral, _ = planes.shape
    me = lax.axis_index("gx")

    def owner(q):
        other = me
        for bit, hop in enumerate(hops):
            other = jnp.bitwise_xor(other, hop * jnp.bitwise_and(lax.shift_right_logical(q, bit), 1))
        return other

    acc[...] = jnp.zeros(acc.shape, f32)

    def gather(j, carry):
        row = jnp.concatenate([cells[pl.ds(owner(2 * j + half), 1), :] for half in range(2)], axis=1)
        block = jnp.concatenate([traces[2 * j], traces[2 * j + 1]], axis=1)
        back = jnp.concatenate([block[steps - 1 - t : steps - t] for t in range(steps)], axis=0)
        acc[:, 0:LANES] += spread(row, split3(back), lateral, steps)
        return carry

    lax.fori_loop(0, groups // 2, gather, 0)
    planes[:, :, 0:LANES] = acc[:, 0:LANES].reshape(steps, lateral, LANES)


def load_field(dst, own, od, od_lo, ev, ev_lo, n, full):
    p, there = place()
    rows = own.shape[0]
    inner = slice(PAD, PAD + own.shape[1])
    dst[rows : 2 * rows, inner, :] = own[...]
    skip = 0 if full else REACH
    dst[pl.ds(2 * rows * p + skip * (1 - p), n), inner, :] = jnp.where(there, od[od_lo : od_lo + n], 0.0)
    dst[pl.ds(2 * rows * (1 - p) + skip * p, n), inner, :] = ev[ev_lo : ev_lo + n]


def tiles_of(q, first, tiles):
    y0 = pl.multiple_of(8 * lax.rem(q, tiles), 8)
    return first + 8 * lax.div(q, tiles), y0, pl.multiple_of(PAD + y0, 8)


def run_steps(field, product, coefs, planes, depth, base):
    buoy, kb, kk, gg = coefs
    wide, tall, nz = field[0].shape
    ny = tall - 2 * PAD
    tiles = ny // 8
    surface = lax.broadcasted_iota(jnp.int32, (8, nz), 1) == SURFACE
    for step in range(IMG_EVERY):
        old, new = field[step % 2], field[1 - step % 2]
        flux, flux_new = product[step % 2], product[1 - step % 2]
        first = REACH * (step + 1)
        for r0 in range(first, wide - first, 8):
            deep = along_depth((old, flux), r0, depth)
            for i in range(8):
                r = r0 + i
                for t in range(tiles):
                    tile = slice(8 * t, 8 * t + 8)
                    at = slice(PAD + 8 * t, PAD + 8 * t + 8)
                    row = ny * i + 8 * t
                    term = pltpu.roll(planes[base + step, tile, :], (SURFACE - (r - REACH)) % nz, axis=1)
                    part = gg[r, tile, :] * old[r, at, :] - new[r, at, :] + jnp.where(surface, term, 0.0)
                    part = part + kb[r, tile, :] * deep[row : row + 8]
                    new[r, at, :] = part + kk[r, tile, :] * deep[8 * ny + row : 8 * ny + row + 8]

        def chunk(q, carry, old=old, new=new, flux=flux, flux_new=flux_new, step=step, first=first):
            r0, y0, at = tiles_of(q, first, tiles)
            tile = pl.ds(y0, 8)
            for i in range(8):
                r = r0 + i
                part = new[r, pl.ds(at, 8), :] + kb[r, tile, :] * across(old, r0, at, i)
                part = part + kk[r, tile, :] * across(flux, r0, at, i)
                new[r, pl.ds(at, 8), :] = part
                if step < IMG_EVERY - 1:
                    flux_new[r, pl.ds(at, 8), :] = buoy[r, tile, :] * part
            return carry

        lax.fori_loop(0, tiles * (wide - 2 * first) // 8, chunk, 0)


def start_products(field, product, buoy):
    for ref in (*field, *product):
        clear_pads(ref)
    inner = slice(PAD, field[0].shape[1] - PAD)
    product[0][:, inner, :] = buoy[...] * field[0][:, inner, :]


def finish(field, n, now_out, before_out, od_out, ev_out):
    p, _ = place()
    last, earlier = field[IMG_EVERY % 2], field[1 - IMG_EVERY % 2]
    inner = slice(PAD, last.shape[1] - PAD)
    value = last[n : 2 * n, inner, :]
    now_out[...] = value
    before_out[...] = earlier[n : 2 * n, inner, :]
    od_out[0:n] = value
    ev_out[0:n] = value
    od_out[n:] = earlier[pl.ds(n + REACH * p, TRIM), inner, :]
    ev_out[n:] = earlier[pl.ds(n + REACH * (1 - p), TRIM), inner, :]


def first_kernel(own, prior, stiff, buoy_own, far_own, far_coef, far_prior, ev, planes, now_out, before_out, od_out, ev_out, buoy, kb, kk, gg, f0, f1, p0, p1):
    n, ny, nz = own.shape
    tiles = ny // 8
    inner = slice(PAD, PAD + ny)
    depth = depth_matrix(nz)
    clear_pads(p1)
    load_field(p1, buoy_own, far_coef, 0, ev, 0, n, True)
    load_field(f1, stiff, far_coef, n, ev, n, TRIM, False)
    buoy[...] = p1[:, inner, :]

    for r0 in range(REACH, 3 * n - REACH, 8):
        gg[r0 : r0 + 8] = along_depth((p1,), r0, depth).reshape(8, ny, nz)

    def coefficients(q, carry):
        r0, y0, at = tiles_of(q, REACH, tiles)
        tile = pl.ds(y0, 8)
        for i in range(8):
            r = r0 + i
            b = p1[r, pl.ds(at, 8), :]
            k = f1[r, pl.ds(at, 8), :] * (0.5 / SCALE)
            kk[r, tile, :] = k
            kb[r, tile, :] = k * b
            gg[r, tile, :] = 2.0 - k * (CENTRE * b + (across(p1, r0, at, i) + gg[r, tile, :]))
        return carry

    lax.fori_loop(0, tiles * (3 * n - 2 * REACH) // 8, coefficients, 0)
    load_field(f0, own, far_own, 0, ev, n + TRIM, n, True)
    load_field(f1, prior, far_prior, 0, ev, 2 * n + TRIM, TRIM, False)
    start_products((f0, f1), (p0, p1), buoy)
    run_steps((f0, f1), (p0, p1), (buoy, kb, kk, gg), planes, depth, 0)
    finish((f0, f1), n, now_out, before_out, od_out, ev_out)


def block_steps(own, prior, od, ev, planes, coefs, field, product, base):
    n, _, nz = own.shape
    depth = depth_matrix(nz)
    load_field(field[0], own, od, 0, ev, 0, n, True)
    load_field(field[1], prior, od, n, ev, n, TRIM, False)
    start_products(field, product, coefs[0])
    run_steps(field, product, coefs, planes, depth, base)


def block_kernel(own, prior, od, ev, planes, buoy, kb, kk, gg, now_out, before_out, od_out, ev_out, f0, f1, p0, p1, base):
    block_steps(own, prior, od, ev, planes, (buoy, kb, kk, gg), (f0, f1), (p0, p1), base)
    finish((f0, f1), own.shape[0], now_out, before_out, od_out, ev_out)


def last_kernel(own, prior, od, ev, planes, buoy, kb, kk, gg, now_out, f0, f1, p0, p1, base):
    block_steps(own, prior, od, ev, planes, (buoy, kb, kk, gg), (f0, f1), (p0, p1), base)
    n, ny, _ = own.shape
    now_out[...] = (f0, f1)[IMG_EVERY % 2][n : 2 * n, PAD : PAD + ny, :]


def lagged(lag_s, lag_r, levels, x, lag):
    total = None
    for level in levels:
        term = lag_s[level, HALF + x - lag] * lag_r[level, HALF + x + lag]
        total = term if total is None else total + term
    return total


def write_out(block, out, sems, count, target):
    def drain(j, carry):
        pltpu.make_async_copy(block.at[j], out.at[target(j)], sems.at[j]).wait()
        return carry

    lax.fori_loop(0, count, drain, 0)


def image_kernel(s0, s4, s8, r0, r4, r8, far_s0, ev1, far_r, ev2, ods, evs, odr, evr, ods8, evs8, evr8, out, rest, lag_s, lag_r, block, sems):
    p, there = place()
    n = s0.shape[0]
    left, right = pl.ds(2 * n * p, n), pl.ds(2 * n * (1 - p), n)
    groups = (
        (lag_s, 0, s0, far_s0, 0, ev1, n + TRIM),
        (lag_r, 0, r0, far_r, 0, ev2, 0),
        (lag_s, 1, s4, ods, 0, evs, 0),
        (lag_r, 1, r4, odr, 0, evr, 0),
        (lag_s, 2, s8, ods8, 0, evs8, 0),
        (lag_r, 2, r8, None, 0, evr8, 0),
    )
    for dst, level, own, od, od_lo, ev, ev_lo in groups:
        dst[level, n : 2 * n] = own[...]
        if od is not None:
            dst[level, left] = jnp.where(there, od[od_lo : od_lo + n], 0.0)
        dst[level, right] = ev[ev_lo : ev_lo + n]
    sign = 1 - 2 * p
    target = lambda j: HALF + sign * j

    def whole(j, carry):
        for x in range(n):
            block[j, x] = lagged(lag_s, lag_r, (0, 1, 2), x, sign * j)
        pltpu.make_async_copy(block.at[j], out.at[target(j)], sems.at[j]).start()
        return carry

    lax.fori_loop(0, HALF + 1, whole, 0)

    def partial(j, carry):
        for x in range(n):
            rest[j, x] = lagged(lag_s, lag_r, (0, 1), x, -sign * (j + 1))
        return carry

    lax.fori_loop(0, HALF, partial, 0)
    write_out(block, out, sems, HALF + 1, target)


def last_image_kernel(s8, r8, evs8, odr8, rest, before, out, lag_s, lag_r, block, sems):
    p, there = place()
    n = s8.shape[0]
    lag_s[0, n : 2 * n] = s8[...]
    lag_s[0, pl.ds(2 * n * (1 - p), n)] = evs8[...]
    lag_r[0, n : 2 * n] = r8[...]
    lag_r[0, pl.ds(2 * n * p, n)] = jnp.where(there, odr8[...], 0.0)
    sign = 1 - 2 * p
    target = lambda j: HALF - sign * (j + 1)

    def one(j, carry):
        for x in range(n):
            block[j, x] = rest[j, x] + lagged(lag_s, lag_r, (0,), x, -sign * (j + 1))
        pltpu.make_async_copy(block.at[j], out.at[target(j)], sems.at[j]).start()
        return carry

    lax.fori_loop(0, HALF, one, 0)
    write_out(block, out, sems, HALF, target)


def estimate(flops, nbytes):
    return pl.CostEstimate(flops=flops, bytes_accessed=nbytes, transcendentals=0)


def local(source_field, source_prior, receiver_field, receiver_prior, stiffness, buoyancy, wavelet, fire_step, shot_cell, receiver_cell, traces):
    n, ny, nz = source_field.shape
    shots, count = lax.axis_size("shot"), lax.axis_size("gx")
    near = [(i, i ^ 1) for i in range(count)]
    far = [(s * count + i, s * count + i + 1) for s in range(shots) for i in range(1, count - 1, 2)]
    far = far + [(b, a) for a, b in far]
    if shots % 2 == 0:
        far += [(s * count + e, (s ^ 1) * count + e) for s in range(shots) for e in (0, count - 1)]

    def swap_near(x):
        return lax.ppermute(x, "gx", near)

    def swap_far(x):
        return lax.ppermute(x, ("shot", "gx"), far)

    hops = []
    hop = 2
    while hop < count:
        hops.append(hop)
        hop *= 2
    hops.append(1)

    def exchange(x, which):
        return lax.ppermute(x, "gx", [(i, i ^ hops[which]) for i in range(count)])

    received = exchange(traces[None], 0)
    far_s0 = swap_far(source_field)

    small = n + TRIM
    width = traces.shape[1]
    ns = shot_cell.shape[0]
    args = (
        source_field,
        source_prior,
        receiver_field,
        receiver_prior,
        stiffness,
        buoyancy,
        traces[None],
        receiver_cell.reshape(count, width),
        shot_cell.reshape(1, ns),
        fire_step.reshape(1, ns),
        wavelet.T,
    )
    packed = pl.pallas_call(
        functools.partial(pack_kernel, count=len(args)),
        out_shape=[jax.ShapeDtypeStruct(a.shape, a.dtype) for a in args]
        + [shape(small, ny, nz), shape(TRIM, ny, nz), shape(small, ny, nz), shape(2 * small, ny, nz), shape(small, ny, nz)],
        in_specs=[pl.BlockSpec(memory_space=pltpu.MemorySpace.HBM)] * len(args),
        out_specs=vmem_specs(len(args) + 5),
        scratch_shapes=[pltpu.SemaphoreType.DMA((len(args),))],
        compiler_params=params(8),
        cost_estimate=estimate(1000, 3000000),
        name="pack",
    )(*(pltpu.with_memory_space_constraint(a, pltpu.MemorySpace.HBM) for a in args))
    source_field, source_prior, receiver_field, receiver_prior, stiffness, buoyancy, gathered, cells, shot_row, fire_row, wave = packed[: len(args)]
    far_coef, far_prior, far_r, ev1, ev2 = packed[len(args) :]
    far_coef = swap_far(far_coef)
    far_prior = swap_far(far_prior)
    far_r = swap_far(far_r)
    ev1 = swap_near(ev1)
    ev2 = swap_near(ev2)

    gathered = jnp.concatenate([gathered, received], axis=0)
    for which in range(1, len(hops)):
        gathered = jnp.concatenate([gathered, exchange(gathered, which)], axis=0)

    plane = shape(STEPS, ny, nz)
    plane_s = pl.pallas_call(
        shots_kernel,
        out_shape=plane,
        in_specs=vmem_specs(3),
        out_specs=pl.BlockSpec(memory_space=pltpu.VMEM),
        compiler_params=params(8),
        cost_estimate=estimate(1000000, 100000),
        name="shots",
    )(shot_row, fire_row, wave)
    plane_r = pl.pallas_call(
        functools.partial(receivers_kernel, hops=tuple(hops)),
        out_shape=plane,
        in_specs=vmem_specs(2),
        out_specs=pl.BlockSpec(memory_space=pltpu.VMEM),
        scratch_shapes=[pltpu.VMEM((STEPS * ny, nz), f32)],
        compiler_params=params(8),
        cost_estimate=estimate(2 * LANES * STEPS * ny * 2048, 1000000),
        name="receivers",
    )(cells, gathered)

    wide = 3 * n
    scratch = [pltpu.VMEM((wide, ny + 2 * PAD, nz), f32)] * 4
    cost = estimate(224 * 8 * 128 * 60, 6000000)
    own = shape(n, ny, nz)
    s4, s3, ods, evs, buoy, kb, kk, gg = pl.pallas_call(
        first_kernel,
        out_shape=[own, own, shape(small, ny, nz), shape(small, ny, nz)] + [shape(wide, ny, nz)] * 4,
        in_specs=vmem_specs(9),
        out_specs=vmem_specs(8),
        scratch_shapes=scratch,
        compiler_params=params(16),
        cost_estimate=cost,
        name="first_s",
    )(source_field, source_prior, stiffness, buoyancy, far_s0, far_coef, far_prior, ev1, plane_s)
    coefs = (buoy, kb, kk, gg)
    ods = swap_far(ods)
    evs = swap_near(evs)
    r4, r3, odr, evr = pl.pallas_call(
        functools.partial(block_kernel, base=0),
        out_shape=[own, own, shape(small, ny, nz), shape(small, ny, nz)],
        in_specs=vmem_specs(9),
        out_specs=vmem_specs(4),
        scratch_shapes=scratch,
        compiler_params=params(16),
        cost_estimate=cost,
        name="first_r",
    )(receiver_field, receiver_prior, far_r, ev2, plane_r, *coefs)
    odr = swap_far(odr)
    evr = swap_near(evr)

    def last():
        return pl.pallas_call(
            functools.partial(last_kernel, base=IMG_EVERY),
            out_shape=own,
            in_specs=vmem_specs(9),
            out_specs=pl.BlockSpec(memory_space=pltpu.VMEM),
            scratch_shapes=scratch,
            compiler_params=params(16),
            cost_estimate=cost,
        )

    s8 = last()(s4, s3, ods, evs, plane_s, *coefs)
    ods8 = swap_far(s8)
    evs8 = swap_near(s8)
    r8 = last()(r4, r3, odr, evr, plane_r, *coefs)
    odr8 = swap_far(r8)
    evr8 = swap_near(r8)
    lags = lambda levels, blocks: [
        pltpu.VMEM((levels, wide, ny, nz), f32),
        pltpu.VMEM((levels, wide, ny, nz), f32),
        pltpu.VMEM((blocks, n, ny, nz), f32),
        pltpu.SemaphoreType.DMA((blocks,)),
    ]
    hbm = pl.BlockSpec(memory_space=pltpu.MemorySpace.HBM)
    image, rest = pl.pallas_call(
        image_kernel,
        out_shape=[shape(NOFF, n, ny, nz), shape(HALF, n, ny, nz)],
        in_specs=vmem_specs(17),
        out_specs=[hbm, pl.BlockSpec(memory_space=pltpu.VMEM)],
        scratch_shapes=lags(3, HALF + 1),
        compiler_params=params(16),
        cost_estimate=estimate(NOFF * n * ny * nz * 4, 4400000),
        name="image",
    )(source_field, s4, s8, receiver_field, r4, r8, far_s0, ev1, far_r, ev2, ods, evs, odr, evr, ods8, evs8, evr8)
    return pl.pallas_call(
        last_image_kernel,
        out_shape=shape(NOFF, n, ny, nz),
        in_specs=vmem_specs(5) + [hbm],
        out_specs=hbm,
        scratch_shapes=lags(1, HALF),
        input_output_aliases={5: 0},
        compiler_params=params(16),
        cost_estimate=estimate(HALF * n * ny * nz * 2, 2200000),
        name="last_image",
    )(s8, r8, evs8, odr8, rest, image)


def solution(mesh):
    placed = (
        P(("shot", "gx"), None, None),
        P(("shot", "gx"), None, None),
        P(("shot", "gx"), None, None),
        P(("shot", "gx"), None, None),
        P("gx", None, None),
        P("gx", None, None),
        P("shot", None),
        P("shot"),
        P("shot"),
        P("shot"),
        P("shot", "gx"),
    )
    return jax.shard_map(local, mesh=mesh, in_specs=placed, out_specs=P("shot", "gx", None, None), check_vma=False)
```

```python
import functools

import jax
import jax.numpy as jnp
from jax import lax
from jax.experimental import pallas as pl
from jax.experimental.pallas import tpu as pltpu
from jax.sharding import PartitionSpec as P


STEPS = 8
IMG_EVERY = 4
NOFF = 33
SURFACE = 4
HALF = 16
REACH = 4
TRIM = HALF - REACH
LANES = 48

SCALE = 5040.0
WHOLE = (8064.0, -1008.0, 128.0, -9.0)
CENTRE = 6.0 * sum(WHOLE)

f32 = jnp.float32
bf16 = jnp.bfloat16


def vmem_specs(count):
    return [pl.BlockSpec(memory_space=pltpu.VMEM)] * count


def params(megabytes):
    return pltpu.CompilerParams(vmem_limit_bytes=megabytes * 1024 * 1024)


def shape(*dims):
    return jax.ShapeDtypeStruct(dims, f32)


def place():
    me = lax.axis_index("gx")
    return lax.rem(me, 2), (me > 0) & (me < lax.axis_size("gx") - 1)


def split2(value):
    high = value.astype(bf16)
    low = (value - high.astype(f32)).astype(bf16)
    return high, low


def split3(value):
    high = value.astype(bf16)
    rest = value - high.astype(f32)
    mid = rest.astype(bf16)
    low = (rest - mid.astype(f32)).astype(bf16)
    return high, mid, low


def weights_of(gap):
    value = jnp.zeros(gap.shape, f32)
    for k, weight in enumerate(WHOLE):
        value = jnp.where(gap == k + 1, weight, value)
    return value


def depth_matrix(nz):
    row = lax.broadcasted_iota(jnp.int32, (nz, nz), 0)
    col = lax.broadcasted_iota(jnp.int32, (nz, nz), 1)
    band = weights_of(jnp.abs(row - col)).astype(bf16)
    return jnp.concatenate([band, band], axis=0)


def cross_matrix(ny):
    bits = ny.bit_length() - 1
    row = lax.broadcasted_iota(jnp.int32, (8 * ny, 16 * ny), 0)
    col = lax.broadcasted_iota(jnp.int32, (8 * ny, 16 * ny), 1)
    along = jnp.abs(lax.shift_right_logical(col, bits) - lax.shift_right_logical(row, bits) - REACH)
    aside = jnp.abs(jnp.bitwise_and(col, ny - 1) - jnp.bitwise_and(row, ny - 1))
    band = jnp.where(aside == 0, weights_of(along), 0.0) + jnp.where(along == 0, weights_of(aside), 0.0)
    band = band.astype(bf16)
    return jnp.concatenate([band, band], axis=1)


def neighbours(high, low, r0, depth, cross):
    _, ny, both = high.shape
    nz = both // 2
    h, l = high[r0 : r0 + 8].reshape(8 * ny, both), low[r0 : r0 + 8].reshape(8 * ny, both)
    split = [jnp.concatenate([h[:, cut], l[:, cut]], axis=1) for cut in (slice(0, nz), slice(nz, both))]
    deep = jnp.dot(jnp.concatenate(split, axis=0), depth, preferred_element_type=f32)
    rows = slice(r0 - REACH, r0 + 8 + REACH)
    around = jnp.concatenate([high[rows].reshape(16 * ny, both), low[rows].reshape(16 * ny, both)], axis=0)
    wide = jnp.dot(cross, around, preferred_element_type=f32)
    return wide[:, 0:nz] + deep[0 : 8 * ny], wide[:, nz:] + deep[8 * ny :]


def keep(high, low, rows, plain, scaled):
    pair = jnp.concatenate([plain, scaled], axis=plain.ndim - 1)
    h, l = split2(pair)
    high[rows] = h
    low[rows] = l


def pack_kernel(*refs, count):
    args, copies, sems = refs[:count], refs[count : 2 * count], refs[-1]
    far_coef, far_prior, far_r, near_s, near_r = refs[2 * count : -1]
    moves = [pltpu.make_async_copy(a, b, sems.at[i]) for i, (a, b) in enumerate(zip(args, copies))]
    for move in moves:
        move.start()
    for move in moves:
        move.wait()
    s0, sp, r0, rp, stiff, buoy = copies[:6]
    p, _ = place()
    n = s0.shape[0]
    far_cut, near_cut = pl.ds(REACH * p, TRIM), pl.ds(REACH * (1 - p), TRIM)
    far_coef[0:n] = buoy[...]
    far_coef[n:] = stiff[far_cut]
    far_prior[...] = sp[far_cut]
    far_r[0:n] = r0[...]
    far_r[n:] = rp[far_cut]
    near_s[0:n] = buoy[...]
    near_s[n : n + TRIM] = stiff[near_cut]
    near_s[n + TRIM : 2 * n + TRIM] = s0[...]
    near_s[2 * n + TRIM :] = sp[near_cut]
    near_r[0:n] = r0[...]
    near_r[n:] = rp[near_cut]


def spread(cells, parts, lateral, steps):
    width = cells.shape[1]
    bits = lateral.bit_length() - 1
    crossline = jnp.bitwise_and(cells, lateral - 1)
    inline = lax.shift_right_arithmetic(cells, bits) - (lax.axis_index("gx") * HALF - TRIM)
    here = lax.broadcasted_iota(jnp.int32, (lateral, width), 0) == crossline
    hot = jnp.where(lax.broadcasted_iota(jnp.int32, (LANES, width), 0) == inline, 1.0, 0.0).astype(bf16)
    total = None
    for part in parts:
        part = part.astype(f32)
        rows = [jnp.where(here, part[t : t + 1], 0.0) for t in range(steps)]
        term = lax.dot_general(
            jnp.concatenate(rows, axis=0).astype(bf16), hot, (((1,), (1,)), ((), ())), preferred_element_type=f32
        )
        total = term if total is None else total + term
    return total


def shots_kernel(shots, fire, wavelet, planes, depth, cross):
    steps, lateral, _ = planes.shape
    taps, ns = wavelet.shape
    delay = lax.broadcasted_iota(jnp.int32, (steps, ns), 0) - fire[...]
    amounts = jnp.zeros((steps, ns), f32)
    for d in range(taps):
        amounts = amounts + jnp.where(delay == d, wavelet[d : d + 1, :], 0.0)
    depth[...] = depth_matrix(depth.shape[1])
    cross[...] = cross_matrix(lateral)
    total = spread(shots[...], split3(amounts), lateral, steps)
    planes[:, :, 0:LANES] = total.reshape(steps, lateral, LANES)


def receivers_kernel(cells, traces, planes, acc, hops):
    groups = cells.shape[0]
    steps, lateral, _ = planes.shape
    me = lax.axis_index("gx")

    def owner(q):
        other = me
        for bit, hop in enumerate(hops):
            other = jnp.bitwise_xor(other, hop * jnp.bitwise_and(lax.shift_right_logical(q, bit), 1))
        return other

    acc[...] = jnp.zeros(acc.shape, f32)

    def gather(j, carry):
        row = jnp.concatenate([cells[pl.ds(owner(2 * j + half), 1), :] for half in range(2)], axis=1)
        block = jnp.concatenate([traces[2 * j], traces[2 * j + 1]], axis=1)
        back = jnp.concatenate([block[steps - 1 - t : steps - t] for t in range(steps)], axis=0)
        acc[:, 0:LANES] += spread(row, split3(back), lateral, steps)
        return carry

    lax.fori_loop(0, groups // 2, gather, 0)
    planes[:, :, 0:LANES] = acc[:, 0:LANES].reshape(steps, lateral, LANES)


def load_field(dst, own, od, od_lo, ev, ev_lo, n, full):
    p, there = place()
    rows = own.shape[0]
    dst[rows : 2 * rows] = own[...]
    skip = 0 if full else REACH
    dst[pl.ds(2 * rows * p + skip * (1 - p), n)] = jnp.where(there, od[od_lo : od_lo + n], 0.0)
    dst[pl.ds(2 * rows * (1 - p) + skip * p, n)] = ev[ev_lo : ev_lo + n]


def run_steps(field, parts, coefs, planes, depth, cross, base):
    buoy, kb, kk, gg = coefs
    wide, ny, nz = field[0].shape
    surface = lax.broadcasted_iota(jnp.int32, (8, nz), 1) == SURFACE
    band = depth[...], cross[...]
    for r0 in range(0, wide, 8):
        rows = slice(r0, r0 + 8)
        keep(*parts[0], rows, field[0][rows], buoy[rows] * field[0][rows])
    for step in range(IMG_EVERY):
        old, new = field[step % 2], field[1 - step % 2]
        first = REACH * (step + 1)
        for r0 in range(first, wide - first, 8):
            rows = slice(r0, r0 + 8)
            plain, scaled = neighbours(*parts[step % 2], r0, *band)
            terms = []
            for i in range(8):
                for t in range(ny // 8):
                    term = pltpu.roll(planes[base + step, 8 * t : 8 * t + 8, :], (SURFACE - (r0 + i - REACH)) % nz, axis=1)
                    terms.append(jnp.where(surface, term, 0.0))
            fresh = gg[rows] * old[rows] - new[rows] + jnp.concatenate(terms, axis=0).reshape(8, ny, nz)
            fresh = fresh + kb[rows] * plain.reshape(8, ny, nz) + kk[rows] * scaled.reshape(8, ny, nz)
            new[rows] = fresh
            if step < IMG_EVERY - 1:
                keep(*parts[1 - step % 2], rows, fresh, buoy[rows] * fresh)


def finish(field, n, now_out, before_out, od_out, ev_out):
    p, _ = place()
    last, earlier = field[IMG_EVERY % 2], field[1 - IMG_EVERY % 2]
    value = last[n : 2 * n]
    now_out[...] = value
    before_out[...] = earlier[n : 2 * n]
    od_out[0:n] = value
    ev_out[0:n] = value
    od_out[n:] = earlier[pl.ds(n + REACH * p, TRIM)]
    ev_out[n:] = earlier[pl.ds(n + REACH * (1 - p), TRIM)]


def first_kernel(own, prior, stiff, buoy_own, far_own, far_coef, far_prior, ev, planes, depth, cross, now_out, before_out, od_out, ev_out, buoy, kb, kk, gg, f0, f1, h0, l0, h1, l1):
    n, ny, nz = own.shape
    band = depth[...], cross[...]
    load_field(buoy, buoy_own, far_coef, 0, ev, 0, n, True)
    load_field(f1, stiff, far_coef, n, ev, n, TRIM, False)
    load_field(f0, own, far_own, 0, ev, n + TRIM, n, True)
    for r0 in range(0, 3 * n, 8):
        rows = slice(r0, r0 + 8)
        keep(h1, l1, rows, buoy[rows], f0[rows])
    for r0 in range(REACH, 3 * n - REACH, 8):
        rows = slice(r0, r0 + 8)
        around, _ = neighbours(h1, l1, r0, *band)
        b = buoy[rows]
        k = f1[rows] * (0.5 / SCALE)
        kk[rows] = k
        kb[rows] = k * b
        gg[rows] = 2.0 - k * (CENTRE * b + around.reshape(8, ny, nz))
    load_field(f1, prior, far_prior, 0, ev, 2 * n + TRIM, TRIM, False)
    run_steps((f0, f1), ((h0, l0), (h1, l1)), (buoy, kb, kk, gg), planes, depth, cross, 0)
    finish((f0, f1), n, now_out, before_out, od_out, ev_out)


def block_steps(own, prior, od, ev, planes, depth, cross, coefs, field, parts, base):
    n = own.shape[0]
    load_field(field[0], own, od, 0, ev, 0, n, True)
    load_field(field[1], prior, od, n, ev, n, TRIM, False)
    run_steps(field, parts, coefs, planes, depth, cross, base)


def block_kernel(own, prior, od, ev, planes, depth, cross, buoy, kb, kk, gg, now_out, before_out, od_out, ev_out, f0, f1, h0, l0, h1, l1, base):
    block_steps(own, prior, od, ev, planes, depth, cross, (buoy, kb, kk, gg), (f0, f1), ((h0, l0), (h1, l1)), base)
    finish((f0, f1), own.shape[0], now_out, before_out, od_out, ev_out)


def last_kernel(own, prior, od, ev, planes, depth, cross, buoy, kb, kk, gg, now_out, f0, f1, h0, l0, h1, l1, base):
    block_steps(own, prior, od, ev, planes, depth, cross, (buoy, kb, kk, gg), (f0, f1), ((h0, l0), (h1, l1)), base)
    n = own.shape[0]
    now_out[...] = (f0, f1)[IMG_EVERY % 2][n : 2 * n]


def lagged(lag_s, lag_r, levels, x, lag):
    total = None
    for level in levels:
        term = lag_s[level, HALF + x - lag] * lag_r[level, HALF + x + lag]
        total = term if total is None else total + term
    return total


def write_out(block, out, sems, count, target):
    def drain(j, carry):
        pltpu.make_async_copy(block.at[j], out.at[target(j)], sems.at[j]).wait()
        return carry

    lax.fori_loop(0, count, drain, 0)


def image_kernel(s0, s4, s8, r0, r4, r8, far_s0, ev1, far_r, ev2, ods, evs, odr, evr, ods8, evs8, evr8, out, rest, lag_s, lag_r, block, sems):
    p, there = place()
    n = s0.shape[0]
    left, right = pl.ds(2 * n * p, n), pl.ds(2 * n * (1 - p), n)
    groups = (
        (lag_s, 0, s0, far_s0, 0, ev1, n + TRIM),
        (lag_r, 0, r0, far_r, 0, ev2, 0),
        (lag_s, 1, s4, ods, 0, evs, 0),
        (lag_r, 1, r4, odr, 0, evr, 0),
        (lag_s, 2, s8, ods8, 0, evs8, 0),
        (lag_r, 2, r8, None, 0, evr8, 0),
    )
    for dst, level, own, od, od_lo, ev, ev_lo in groups:
        dst[level, n : 2 * n] = own[...]
        if od is not None:
            dst[level, left] = jnp.where(there, od[od_lo : od_lo + n], 0.0)
        dst[level, right] = ev[ev_lo : ev_lo + n]
    sign = 1 - 2 * p
    target = lambda j: HALF + sign * j

    def whole(j, carry):
        for x in range(n):
            block[j, x] = lagged(lag_s, lag_r, (0, 1, 2), x, sign * j)
        pltpu.make_async_copy(block.at[j], out.at[target(j)], sems.at[j]).start()
        return carry

    lax.fori_loop(0, HALF + 1, whole, 0)

    def partial(j, carry):
        for x in range(n):
            rest[j, x] = lagged(lag_s, lag_r, (0, 1), x, -sign * (j + 1))
        return carry

    lax.fori_loop(0, HALF, partial, 0)
    write_out(block, out, sems, HALF + 1, target)


def last_image_kernel(s8, r8, evs8, odr8, rest, before, out, lag_s, lag_r, block, sems):
    p, there = place()
    n = s8.shape[0]
    lag_s[0, n : 2 * n] = s8[...]
    lag_s[0, pl.ds(2 * n * (1 - p), n)] = evs8[...]
    lag_r[0, n : 2 * n] = r8[...]
    lag_r[0, pl.ds(2 * n * p, n)] = jnp.where(there, odr8[...], 0.0)
    sign = 1 - 2 * p
    target = lambda j: HALF - sign * (j + 1)

    def one(j, carry):
        for x in range(n):
            block[j, x] = rest[j, x] + lagged(lag_s, lag_r, (0,), x, -sign * (j + 1))
        pltpu.make_async_copy(block.at[j], out.at[target(j)], sems.at[j]).start()
        return carry

    lax.fori_loop(0, HALF, one, 0)
    write_out(block, out, sems, HALF, target)


def estimate(flops, nbytes):
    return pl.CostEstimate(flops=flops, bytes_accessed=nbytes, transcendentals=0)


def local(source_field, source_prior, receiver_field, receiver_prior, stiffness, buoyancy, wavelet, fire_step, shot_cell, receiver_cell, traces):
    n, ny, nz = source_field.shape
    shots, count = lax.axis_size("shot"), lax.axis_size("gx")
    near = [(i, i ^ 1) for i in range(count)]
    far = [(s * count + i, s * count + i + 1) for s in range(shots) for i in range(1, count - 1, 2)]
    far = far + [(b, a) for a, b in far]
    if shots % 2 == 0:
        far += [(s * count + e, (s ^ 1) * count + e) for s in range(shots) for e in (0, count - 1)]

    def swap_near(x):
        return lax.ppermute(x, "gx", near)

    def swap_far(x):
        return lax.ppermute(x, ("shot", "gx"), far)

    hops = []
    hop = 2
    while hop < count:
        hops.append(hop)
        hop *= 2
    hops.append(1)

    def exchange(x, which):
        return lax.ppermute(x, "gx", [(i, i ^ hops[which]) for i in range(count)])

    received = exchange(traces[None], 0)
    far_s0 = swap_far(source_field)

    small = n + TRIM
    width = traces.shape[1]
    ns = shot_cell.shape[0]
    args = (
        source_field,
        source_prior,
        receiver_field,
        receiver_prior,
        stiffness,
        buoyancy,
        traces[None],
        receiver_cell.reshape(count, width),
        shot_cell.reshape(1, ns),
        fire_step.reshape(1, ns),
        wavelet.T,
    )
    packed = pl.pallas_call(
        functools.partial(pack_kernel, count=len(args)),
        out_shape=[jax.ShapeDtypeStruct(a.shape, a.dtype) for a in args]
        + [shape(small, ny, nz), shape(TRIM, ny, nz), shape(small, ny, nz), shape(2 * small, ny, nz), shape(small, ny, nz)],
        in_specs=[pl.BlockSpec(memory_space=pltpu.MemorySpace.HBM)] * len(args),
        out_specs=vmem_specs(len(args) + 5),
        scratch_shapes=[pltpu.SemaphoreType.DMA((len(args),))],
        compiler_params=params(8),
        cost_estimate=estimate(1000, 3000000),
        name="pack",
    )(*(pltpu.with_memory_space_constraint(a, pltpu.MemorySpace.HBM) for a in args))
    source_field, source_prior, receiver_field, receiver_prior, stiffness, buoyancy, gathered, cells, shot_row, fire_row, wave = packed[: len(args)]
    far_coef, far_prior, far_r, ev1, ev2 = packed[len(args) :]
    far_coef = swap_far(far_coef)
    far_prior = swap_far(far_prior)
    far_r = swap_far(far_r)
    ev1 = swap_near(ev1)
    ev2 = swap_near(ev2)

    gathered = jnp.concatenate([gathered, received], axis=0)
    for which in range(1, len(hops)):
        gathered = jnp.concatenate([gathered, exchange(gathered, which)], axis=0)

    plane = shape(STEPS, ny, nz)
    plane_s, *band = pl.pallas_call(
        shots_kernel,
        out_shape=[plane, jax.ShapeDtypeStruct((2 * nz, nz), bf16), jax.ShapeDtypeStruct((8 * ny, 32 * ny), bf16)],
        in_specs=vmem_specs(3),
        out_specs=vmem_specs(3),
        compiler_params=params(8),
        cost_estimate=estimate(1000000, 100000),
        name="shots",
    )(shot_row, fire_row, wave)
    plane_r = pl.pallas_call(
        functools.partial(receivers_kernel, hops=tuple(hops)),
        out_shape=plane,
        in_specs=vmem_specs(2),
        out_specs=pl.BlockSpec(memory_space=pltpu.VMEM),
        scratch_shapes=[pltpu.VMEM((STEPS * ny, nz), f32)],
        compiler_params=params(8),
        cost_estimate=estimate(2 * LANES * STEPS * ny * 2048, 1000000),
        name="receivers",
    )(cells, gathered)

    wide = 3 * n
    scratch = [pltpu.VMEM((wide, ny, nz), f32)] * 2 + [pltpu.VMEM((wide, ny, 2 * nz), bf16)] * 4
    cost = estimate(224 * 8 * 128 * 60, 6000000)
    own = shape(n, ny, nz)
    s4, s3, ods, evs, buoy, kb, kk, gg = pl.pallas_call(
        first_kernel,
        out_shape=[own, own, shape(small, ny, nz), shape(small, ny, nz)] + [shape(wide, ny, nz)] * 4,
        in_specs=vmem_specs(11),
        out_specs=vmem_specs(8),
        scratch_shapes=scratch,
        compiler_params=params(16),
        cost_estimate=cost,
        name="first_s",
    )(source_field, source_prior, stiffness, buoyancy, far_s0, far_coef, far_prior, ev1, plane_s, *band)
    coefs = (buoy, kb, kk, gg)
    ods = swap_far(ods)
    evs = swap_near(evs)
    r4, r3, odr, evr = pl.pallas_call(
        functools.partial(block_kernel, base=0),
        out_shape=[own, own, shape(small, ny, nz), shape(small, ny, nz)],
        in_specs=vmem_specs(11),
        out_specs=vmem_specs(4),
        scratch_shapes=scratch,
        compiler_params=params(16),
        cost_estimate=cost,
        name="first_r",
    )(receiver_field, receiver_prior, far_r, ev2, plane_r, *band, *coefs)
    odr = swap_far(odr)
    evr = swap_near(evr)

    def last():
        return pl.pallas_call(
            functools.partial(last_kernel, base=IMG_EVERY),
            out_shape=own,
            in_specs=vmem_specs(11),
            out_specs=pl.BlockSpec(memory_space=pltpu.VMEM),
            scratch_shapes=scratch,
            compiler_params=params(16),
            cost_estimate=cost,
        )

    s8 = last()(s4, s3, ods, evs, plane_s, *band, *coefs)
    ods8 = swap_far(s8)
    evs8 = swap_near(s8)
    r8 = last()(r4, r3, odr, evr, plane_r, *band, *coefs)
    odr8 = swap_far(r8)
    evr8 = swap_near(r8)
    lags = lambda levels, blocks: [
        pltpu.VMEM((levels, wide, ny, nz), f32),
        pltpu.VMEM((levels, wide, ny, nz), f32),
        pltpu.VMEM((blocks, n, ny, nz), f32),
        pltpu.SemaphoreType.DMA((blocks,)),
    ]
    hbm = pl.BlockSpec(memory_space=pltpu.MemorySpace.HBM)
    image, rest = pl.pallas_call(
        image_kernel,
        out_shape=[shape(NOFF, n, ny, nz), shape(HALF, n, ny, nz)],
        in_specs=vmem_specs(17),
        out_specs=[hbm, pl.BlockSpec(memory_space=pltpu.VMEM)],
        scratch_shapes=lags(3, HALF + 1),
        compiler_params=params(16),
        cost_estimate=estimate(NOFF * n * ny * nz * 4, 4400000),
        name="image",
    )(source_field, s4, s8, receiver_field, r4, r8, far_s0, ev1, far_r, ev2, ods, evs, odr, evr, ods8, evs8, evr8)
    return pl.pallas_call(
        last_image_kernel,
        out_shape=shape(NOFF, n, ny, nz),
        in_specs=vmem_specs(5) + [hbm],
        out_specs=hbm,
        scratch_shapes=lags(1, HALF),
        input_output_aliases={5: 0},
        compiler_params=params(16),
        cost_estimate=estimate(HALF * n * ny * nz * 2, 2200000),
        name="last_image",
    )(s8, r8, evs8, odr8, rest, image)


def solution(mesh):
    placed = (
        P(("shot", "gx"), None, None),
        P(("shot", "gx"), None, None),
        P(("shot", "gx"), None, None),
        P(("shot", "gx"), None, None),
        P("gx", None, None),
        P("gx", None, None),
        P("shot", None),
        P("shot"),
        P("shot"),
        P("shot"),
        P("shot", "gx"),
    )
    return jax.shard_map(local, mesh=mesh, in_specs=placed, out_specs=P("shot", "gx", None, None), check_vma=False)
```

```python
import functools

import jax
import jax.numpy as jnp
from jax import lax
from jax.experimental import pallas as pl
from jax.experimental.pallas import tpu as pltpu
from jax.sharding import PartitionSpec as P


STEPS = 8
IMG_EVERY = 4
NOFF = 33
SURFACE = 4
HALF = 16
REACH = 4
TRIM = HALF - REACH
LANES = 48

SCALE = 5040.0
WHOLE = (8064.0, -1008.0, 128.0, -9.0)
CENTRE = 6.0 * sum(WHOLE)

f32 = jnp.float32
bf16 = jnp.bfloat16


def vmem_specs(count):
    return [pl.BlockSpec(memory_space=pltpu.VMEM)] * count


def params(megabytes):
    return pltpu.CompilerParams(vmem_limit_bytes=megabytes * 1024 * 1024)


def shape(*dims):
    return jax.ShapeDtypeStruct(dims, f32)


def place():
    me = lax.axis_index("gx")
    return lax.rem(me, 2), (me > 0) & (me < lax.axis_size("gx") - 1)


def split2(value):
    high = value.astype(bf16)
    low = (value - high.astype(f32)).astype(bf16)
    return high, low


def split3(value):
    high = value.astype(bf16)
    rest = value - high.astype(f32)
    mid = rest.astype(bf16)
    low = (rest - mid.astype(f32)).astype(bf16)
    return high, mid, low


def weights_of(gap):
    value = jnp.zeros(gap.shape, f32)
    for k, weight in enumerate(WHOLE):
        value = jnp.where(gap == k + 1, weight, value)
    return value


def depth_matrix(nz):
    row = lax.broadcasted_iota(jnp.int32, (nz, nz), 0)
    col = lax.broadcasted_iota(jnp.int32, (nz, nz), 1)
    band = weights_of(jnp.abs(row - col)).astype(bf16)
    return jnp.concatenate([band, band], axis=0)


def cross_matrix(ny):
    bits = ny.bit_length() - 1
    row = lax.broadcasted_iota(jnp.int32, (8 * ny, 16 * ny), 0)
    col = lax.broadcasted_iota(jnp.int32, (8 * ny, 16 * ny), 1)
    along = jnp.abs(lax.shift_right_logical(col, bits) - lax.shift_right_logical(row, bits) - REACH)
    aside = jnp.abs(jnp.bitwise_and(col, ny - 1) - jnp.bitwise_and(row, ny - 1))
    band = jnp.where(aside == 0, weights_of(along), 0.0) + jnp.where(along == 0, weights_of(aside), 0.0)
    band = band.astype(bf16)
    return jnp.concatenate([band, band], axis=1)


def neighbours(high, low, r0, depth, cross):
    _, ny, both = high.shape
    nz = both // 2
    h, l = high[r0 : r0 + 8].reshape(8 * ny, both), low[r0 : r0 + 8].reshape(8 * ny, both)
    split = [jnp.concatenate([h[:, cut], l[:, cut]], axis=1) for cut in (slice(0, nz), slice(nz, both))]
    deep = jnp.dot(jnp.concatenate(split, axis=0), depth, preferred_element_type=f32)
    rows = slice(r0 - REACH, r0 + 8 + REACH)
    around = jnp.concatenate([high[rows].reshape(16 * ny, both), low[rows].reshape(16 * ny, both)], axis=0)
    wide = jnp.dot(cross, around, preferred_element_type=f32)
    return wide[:, 0:nz] + deep[0 : 8 * ny], wide[:, nz:] + deep[8 * ny :]


def keep(high, low, rows, plain, scaled):
    pair = jnp.concatenate([plain, scaled], axis=plain.ndim - 1)
    h, l = split2(pair)
    high[rows] = h
    low[rows] = l


def pack_kernel(*refs, count):
    args, copies, sems = refs[:count], refs[count : 2 * count], refs[-1]
    far_coef, far_prior, far_r, near_s, near_r = refs[2 * count : -1]
    moves = [pltpu.make_async_copy(a, b, sems.at[i]) for i, (a, b) in enumerate(zip(args, copies))]
    for move in moves:
        move.start()
    for move in moves:
        move.wait()
    s0, sp, r0, rp, stiff, buoy = copies[:6]
    p, _ = place()
    n = s0.shape[0]
    far_cut, near_cut = pl.ds(REACH * p, TRIM), pl.ds(REACH * (1 - p), TRIM)
    far_coef[0:n] = buoy[...]
    far_coef[n:] = stiff[far_cut]
    far_prior[...] = sp[far_cut]
    far_r[0:n] = r0[...]
    far_r[n:] = rp[far_cut]
    near_s[0:n] = buoy[...]
    near_s[n : n + TRIM] = stiff[near_cut]
    near_s[n + TRIM : 2 * n + TRIM] = s0[...]
    near_s[2 * n + TRIM :] = sp[near_cut]
    near_r[0:n] = r0[...]
    near_r[n:] = rp[near_cut]


def spread(cells, parts, lateral, steps):
    width = cells.shape[1]
    bits = lateral.bit_length() - 1
    crossline = jnp.bitwise_and(cells, lateral - 1)
    inline = lax.shift_right_arithmetic(cells, bits) - (lax.axis_index("gx") * HALF - TRIM)
    here = lax.broadcasted_iota(jnp.int32, (lateral, width), 0) == crossline
    hot = jnp.where(lax.broadcasted_iota(jnp.int32, (LANES, width), 0) == inline, 1.0, 0.0).astype(bf16)
    total = None
    for part in parts:
        part = part.astype(f32)
        rows = [jnp.where(here, part[t : t + 1], 0.0) for t in range(steps)]
        term = lax.dot_general(
            jnp.concatenate(rows, axis=0).astype(bf16), hot, (((1,), (1,)), ((), ())), preferred_element_type=f32
        )
        total = term if total is None else total + term
    return total


def shots_kernel(shots, fire, wavelet, planes, depth, cross):
    steps, lateral, _ = planes.shape
    taps, ns = wavelet.shape
    delay = lax.broadcasted_iota(jnp.int32, (steps, ns), 0) - fire[...]
    amounts = jnp.zeros((steps, ns), f32)
    for d in range(taps):
        amounts = amounts + jnp.where(delay == d, wavelet[d : d + 1, :], 0.0)
    depth[...] = depth_matrix(depth.shape[1])
    cross[...] = cross_matrix(lateral)
    total = spread(shots[...], split3(amounts), lateral, steps)
    planes[:, :, 0:LANES] = total.reshape(steps, lateral, LANES)


def receivers_kernel(cells, traces, planes, acc, hops):
    groups = cells.shape[0]
    steps, lateral, _ = planes.shape
    me = lax.axis_index("gx")

    def owner(q):
        other = me
        for bit, hop in enumerate(hops):
            other = jnp.bitwise_xor(other, hop * jnp.bitwise_and(lax.shift_right_logical(q, bit), 1))
        return other

    acc[...] = jnp.zeros(acc.shape, f32)

    def gather(j, carry):
        row = jnp.concatenate([cells[pl.ds(owner(2 * j + half), 1), :] for half in range(2)], axis=1)
        block = jnp.concatenate([traces[2 * j], traces[2 * j + 1]], axis=1)
        back = jnp.concatenate([block[steps - 1 - t : steps - t] for t in range(steps)], axis=0)
        acc[:, 0:LANES] += spread(row, split3(back), lateral, steps)
        return carry

    lax.fori_loop(0, groups // 2, gather, 0)
    planes[:, :, 0:LANES] = acc[:, 0:LANES].reshape(steps, lateral, LANES)


def load_field(dst, own, od, od_lo, ev, ev_lo, n, full):
    p, there = place()
    rows = own.shape[0]
    dst[rows : 2 * rows] = own[...]
    skip = 0 if full else REACH
    dst[pl.ds(2 * rows * p + skip * (1 - p), n)] = jnp.where(there, od[od_lo : od_lo + n], 0.0)
    dst[pl.ds(2 * rows * (1 - p) + skip * p, n)] = ev[ev_lo : ev_lo + n]


def run_steps(field, parts, coefs, planes, depth, cross, base):
    buoy, kb, kk, gg = coefs
    wide, ny, nz = field[0].shape
    surface = lax.broadcasted_iota(jnp.int32, (8, nz), 1) == SURFACE
    band = depth[...], cross[...]
    for r0 in range(0, wide, 8):
        rows = slice(r0, r0 + 8)
        keep(*parts[0], rows, field[0][rows], buoy[rows] * field[0][rows])
    for step in range(IMG_EVERY):
        old, new = field[step % 2], field[1 - step % 2]
        first = REACH * (step + 1)
        for r0 in range(first, wide - first, 8):
            rows = slice(r0, r0 + 8)
            plain, scaled = neighbours(*parts[step % 2], r0, *band)
            terms = []
            for i in range(8):
                for t in range(ny // 8):
                    term = pltpu.roll(planes[base + step, 8 * t : 8 * t + 8, :], (SURFACE - (r0 + i - REACH)) % nz, axis=1)
                    terms.append(jnp.where(surface, term, 0.0))
            fresh = gg[rows] * old[rows] - new[rows] + jnp.concatenate(terms, axis=0).reshape(8, ny, nz)
            fresh = fresh + kb[rows] * plain.reshape(8, ny, nz) + kk[rows] * scaled.reshape(8, ny, nz)
            new[rows] = fresh
            if step < IMG_EVERY - 1:
                keep(*parts[1 - step % 2], rows, fresh, buoy[rows] * fresh)


def finish(field, n, now_out, before_out, od_out, ev_out):
    p, _ = place()
    last, earlier = field[IMG_EVERY % 2], field[1 - IMG_EVERY % 2]
    value = last[n : 2 * n]
    now_out[...] = value
    before_out[...] = earlier[n : 2 * n]
    od_out[0:n] = value
    ev_out[0:n] = value
    od_out[n:] = earlier[pl.ds(n + REACH * p, TRIM)]
    ev_out[n:] = earlier[pl.ds(n + REACH * (1 - p), TRIM)]


def first_kernel(own, prior, stiff, buoy_own, far_own, far_coef, far_prior, ev, planes, depth, cross, now_out, before_out, od_out, ev_out, buoy, kb, kk, gg, f0, f1, h0, l0, h1, l1):
    n, ny, nz = own.shape
    band = depth[...], cross[...]
    load_field(buoy, buoy_own, far_coef, 0, ev, 0, n, True)
    load_field(f1, stiff, far_coef, n, ev, n, TRIM, False)
    load_field(f0, own, far_own, 0, ev, n + TRIM, n, True)
    for r0 in range(0, 3 * n, 8):
        rows = slice(r0, r0 + 8)
        keep(h1, l1, rows, buoy[rows], f0[rows])
    for r0 in range(REACH, 3 * n - REACH, 8):
        rows = slice(r0, r0 + 8)
        around, _ = neighbours(h1, l1, r0, *band)
        b = buoy[rows]
        k = f1[rows] * (0.5 / SCALE)
        kk[rows] = k
        kb[rows] = k * b
        gg[rows] = 2.0 - k * (CENTRE * b + around.reshape(8, ny, nz))
    load_field(f1, prior, far_prior, 0, ev, 2 * n + TRIM, TRIM, False)
    run_steps((f0, f1), ((h0, l0), (h1, l1)), (buoy, kb, kk, gg), planes, depth, cross, 0)
    finish((f0, f1), n, now_out, before_out, od_out, ev_out)


def block_steps(own, prior, od, ev, planes, depth, cross, coefs, field, parts, base):
    n = own.shape[0]
    load_field(field[0], own, od, 0, ev, 0, n, True)
    load_field(field[1], prior, od, n, ev, n, TRIM, False)
    run_steps(field, parts, coefs, planes, depth, cross, base)


def block_kernel(own, prior, od, ev, planes, depth, cross, buoy, kb, kk, gg, now_out, before_out, od_out, ev_out, f0, f1, h0, l0, h1, l1, base):
    block_steps(own, prior, od, ev, planes, depth, cross, (buoy, kb, kk, gg), (f0, f1), ((h0, l0), (h1, l1)), base)
    finish((f0, f1), own.shape[0], now_out, before_out, od_out, ev_out)


def last_kernel(own, prior, od, ev, planes, depth, cross, buoy, kb, kk, gg, now_out, f0, f1, h0, l0, h1, l1, base):
    block_steps(own, prior, od, ev, planes, depth, cross, (buoy, kb, kk, gg), (f0, f1), ((h0, l0), (h1, l1)), base)
    n = own.shape[0]
    now_out[...] = (f0, f1)[IMG_EVERY % 2][n : 2 * n]


def lagged(lag_s, lag_r, levels, x, lag):
    total = None
    for level in levels:
        term = lag_s[level, HALF + x - lag] * lag_r[level, HALF + x + lag]
        total = term if total is None else total + term
    return total


def sides():
    p, there = place()
    return p, there, 1 - 2 * p, lambda reach: (HALF - reach) * p, lambda reach: reach * (1 - p)


def image_kernel(s0, s4, s8, r0, r4, r8, far_s0, ev1, far_r, ev2, ods, evs, odr, evr, ods8, evs8, evr8, out, rest, lag_s, lag_r, block, sems):
    p, there, sign, far_start, own_start = sides()
    n = s0.shape[0]
    left, right = pl.ds(2 * n * p, n), pl.ds(2 * n * (1 - p), n)
    groups = (
        (lag_s, 0, s0, far_s0, 0, ev1, n + TRIM),
        (lag_r, 0, r0, far_r, 0, ev2, 0),
        (lag_s, 1, s4, ods, 0, evs, 0),
        (lag_r, 1, r4, odr, 0, evr, 0),
        (lag_s, 2, s8, ods8, 0, evs8, 0),
        (lag_r, 2, r8, None, 0, evr8, 0),
    )
    for dst, level, own, od, od_lo, ev, ev_lo in groups:
        dst[level, n : 2 * n] = own[...]
        if od is not None:
            dst[level, left] = jnp.where(there, od[od_lo : od_lo + n], 0.0)
        dst[level, right] = ev[ev_lo : ev_lo + n]
    move = lambda j: pltpu.make_async_copy(block.at[j], out.at[HALF + sign * j], sems.at[j])

    def whole(j, carry):
        for x in range(n):
            block[j, x] = lagged(lag_s, lag_r, (0, 1, 2), x, sign * j)
        move(j).start()
        return carry

    lax.fori_loop(0, HALF + 1, whole, 0)
    moves = []
    for reach in range(1, HALF):
        for i in range(n - reach):
            block[HALF + reach, i] = lagged(lag_s, lag_r, (0, 1, 2), own_start(reach) + i, -sign * reach)
        target = out.at[HALF - sign * reach, pl.ds(own_start(reach), n - reach)]
        moves.append(pltpu.make_async_copy(block.at[HALF + reach, 0 : n - reach], target, sems.at[HALF + reach]))
        moves[-1].start()
    for reach in range(1, HALF + 1):
        for i in range(reach):
            rest[reach * (reach - 1) // 2 + i] = lagged(lag_s, lag_r, (0, 1), far_start(reach) + i, -sign * reach)

    def drain(j, carry):
        move(j).wait()
        return carry

    lax.fori_loop(0, HALF + 1, drain, 0)
    for each in moves:
        each.wait()


def last_image_kernel(s8, r8, evs8, odr8, rest, before, out, lag_s, lag_r, block, sems):
    p, there, sign, far_start, _ = sides()
    n = s8.shape[0]
    lag_s[0, n : 2 * n] = s8[...]
    lag_s[0, pl.ds(2 * n * (1 - p), n)] = evs8[...]
    lag_r[0, n : 2 * n] = r8[...]
    lag_r[0, pl.ds(2 * n * p, n)] = jnp.where(there, odr8[...], 0.0)
    moves = []
    for reach in range(HALF, 0, -1):
        base = reach * (reach - 1) // 2
        for i in range(reach):
            block[base + i] = rest[base + i] + lagged(lag_s, lag_r, (0,), far_start(reach) + i, -sign * reach)
        target = out.at[HALF - sign * reach, pl.ds(far_start(reach), reach)]
        moves.append(pltpu.make_async_copy(block.at[base : base + reach], target, sems.at[reach - 1]))
        moves[-1].start()
    for each in moves:
        each.wait()


def estimate(flops, nbytes):
    return pl.CostEstimate(flops=flops, bytes_accessed=nbytes, transcendentals=0)


def local(source_field, source_prior, receiver_field, receiver_prior, stiffness, buoyancy, wavelet, fire_step, shot_cell, receiver_cell, traces):
    n, ny, nz = source_field.shape
    shots, count = lax.axis_size("shot"), lax.axis_size("gx")
    near = [(i, i ^ 1) for i in range(count)]
    far = [(s * count + i, s * count + i + 1) for s in range(shots) for i in range(1, count - 1, 2)]
    far = far + [(b, a) for a, b in far]
    if shots % 2 == 0:
        far += [(s * count + e, (s ^ 1) * count + e) for s in range(shots) for e in (0, count - 1)]

    def swap_near(x):
        return lax.ppermute(x, "gx", near)

    def swap_far(x):
        return lax.ppermute(x, ("shot", "gx"), far)

    hops = []
    hop = 2
    while hop < count:
        hops.append(hop)
        hop *= 2
    hops.append(1)

    def exchange(x, which):
        return lax.ppermute(x, "gx", [(i, i ^ hops[which]) for i in range(count)])

    far_s0 = swap_far(source_field)
    received = exchange(traces[None], 0)

    small = n + TRIM
    width = traces.shape[1]
    ns = shot_cell.shape[0]
    args = (
        source_field,
        source_prior,
        receiver_field,
        receiver_prior,
        stiffness,
        buoyancy,
        traces[None],
        receiver_cell.reshape(count, width),
        shot_cell.reshape(1, ns),
        fire_step.reshape(1, ns),
        wavelet.T,
    )
    packed = pl.pallas_call(
        functools.partial(pack_kernel, count=len(args)),
        out_shape=[jax.ShapeDtypeStruct(a.shape, a.dtype) for a in args]
        + [shape(small, ny, nz), shape(TRIM, ny, nz), shape(small, ny, nz), shape(2 * small, ny, nz), shape(small, ny, nz)],
        in_specs=[pl.BlockSpec(memory_space=pltpu.MemorySpace.HBM)] * len(args),
        out_specs=vmem_specs(len(args) + 5),
        scratch_shapes=[pltpu.SemaphoreType.DMA((len(args),))],
        compiler_params=params(8),
        cost_estimate=estimate(1000, 3000000),
        name="pack",
    )(*(pltpu.with_memory_space_constraint(a, pltpu.MemorySpace.HBM) for a in args))
    source_field, source_prior, receiver_field, receiver_prior, stiffness, buoyancy, gathered, cells, shot_row, fire_row, wave = packed[: len(args)]
    far_coef, far_prior, far_r, ev1, ev2 = packed[len(args) :]
    far_coef = swap_far(far_coef)
    far_prior = swap_far(far_prior)
    far_r = swap_far(far_r)
    ev1 = swap_near(ev1)
    ev2 = swap_near(ev2)

    gathered = jnp.concatenate([gathered, received], axis=0)
    for which in range(1, len(hops)):
        gathered = jnp.concatenate([gathered, exchange(gathered, which)], axis=0)

    plane = shape(STEPS, ny, nz)
    plane_s, *band = pl.pallas_call(
        shots_kernel,
        out_shape=[plane, jax.ShapeDtypeStruct((2 * nz, nz), bf16), jax.ShapeDtypeStruct((8 * ny, 32 * ny), bf16)],
        in_specs=vmem_specs(3),
        out_specs=vmem_specs(3),
        compiler_params=params(8),
        cost_estimate=estimate(1000000, 100000),
        name="shots",
    )(shot_row, fire_row, wave)
    plane_r = pl.pallas_call(
        functools.partial(receivers_kernel, hops=tuple(hops)),
        out_shape=plane,
        in_specs=vmem_specs(2),
        out_specs=pl.BlockSpec(memory_space=pltpu.VMEM),
        scratch_shapes=[pltpu.VMEM((STEPS * ny, nz), f32)],
        compiler_params=params(8),
        cost_estimate=estimate(2 * LANES * STEPS * ny * 2048, 1000000),
        name="receivers",
    )(cells, gathered)

    wide = 3 * n
    scratch = [pltpu.VMEM((wide, ny, nz), f32)] * 2 + [pltpu.VMEM((wide, ny, 2 * nz), bf16)] * 4
    cost = estimate(224 * 8 * 128 * 60, 6000000)
    own = shape(n, ny, nz)
    s4, s3, ods, evs, buoy, kb, kk, gg = pl.pallas_call(
        first_kernel,
        out_shape=[own, own, shape(small, ny, nz), shape(small, ny, nz)] + [shape(wide, ny, nz)] * 4,
        in_specs=vmem_specs(11),
        out_specs=vmem_specs(8),
        scratch_shapes=scratch,
        compiler_params=params(16),
        cost_estimate=cost,
        name="first_s",
    )(source_field, source_prior, stiffness, buoyancy, far_s0, far_coef, far_prior, ev1, plane_s, *band)
    coefs = (buoy, kb, kk, gg)
    ods = swap_far(ods)
    evs = swap_near(evs)
    r4, r3, odr, evr = pl.pallas_call(
        functools.partial(block_kernel, base=0),
        out_shape=[own, own, shape(small, ny, nz), shape(small, ny, nz)],
        in_specs=vmem_specs(11),
        out_specs=vmem_specs(4),
        scratch_shapes=scratch,
        compiler_params=params(16),
        cost_estimate=cost,
        name="first_r",
    )(receiver_field, receiver_prior, far_r, ev2, plane_r, *band, *coefs)
    odr = swap_far(odr)
    evr = swap_near(evr)

    def last():
        return pl.pallas_call(
            functools.partial(last_kernel, base=IMG_EVERY),
            out_shape=own,
            in_specs=vmem_specs(11),
            out_specs=pl.BlockSpec(memory_space=pltpu.VMEM),
            scratch_shapes=scratch,
            compiler_params=params(16),
            cost_estimate=cost,
        )

    s8 = last()(s4, s3, ods, evs, plane_s, *band, *coefs)
    ods8 = swap_far(s8)
    evs8 = swap_near(s8)
    r8 = last()(r4, r3, odr, evr, plane_r, *band, *coefs)
    odr8 = swap_far(r8)
    evr8 = swap_near(r8)
    lags = lambda levels: [pltpu.VMEM((levels, wide, ny, nz), f32)] * 2
    corner = HALF * (HALF + 1) // 2
    hbm = pl.BlockSpec(memory_space=pltpu.MemorySpace.HBM)
    image, rest = pl.pallas_call(
        image_kernel,
        out_shape=[shape(NOFF, n, ny, nz), shape(corner, ny, nz)],
        in_specs=vmem_specs(17),
        out_specs=[hbm, pl.BlockSpec(memory_space=pltpu.VMEM)],
        scratch_shapes=lags(3) + [pltpu.VMEM((2 * HALF, n, ny, nz), f32), pltpu.SemaphoreType.DMA((2 * HALF,))],
        compiler_params=params(16),
        cost_estimate=estimate(NOFF * n * ny * nz * 4, 4400000),
        name="image",
    )(source_field, s4, s8, receiver_field, r4, r8, far_s0, ev1, far_r, ev2, ods, evs, odr, evr, ods8, evs8, evr8)
    return pl.pallas_call(
        last_image_kernel,
        out_shape=shape(NOFF, n, ny, nz),
        in_specs=vmem_specs(5) + [hbm],
        out_specs=hbm,
        scratch_shapes=lags(1) + [pltpu.VMEM((corner, ny, nz), f32), pltpu.SemaphoreType.DMA((HALF,))],
        input_output_aliases={5: 0},
        compiler_params=params(16),
        cost_estimate=estimate(HALF * n * ny * nz * 2, 2200000),
        name="last_image",
    )(s8, r8, evs8, odr8, rest, image)


def solution(mesh):
    placed = (
        P(("shot", "gx"), None, None),
        P(("shot", "gx"), None, None),
        P(("shot", "gx"), None, None),
        P(("shot", "gx"), None, None),
        P("gx", None, None),
        P("gx", None, None),
        P("shot", None),
        P("shot"),
        P("shot"),
        P("shot"),
        P("shot", "gx"),
    )
    return jax.shard_map(local, mesh=mesh, in_specs=placed, out_specs=P("shot", "gx", None, None), check_vma=False)
```

```python
import functools

import jax
import jax.numpy as jnp
from jax import lax
from jax.experimental import pallas as pl
from jax.experimental.pallas import tpu as pltpu
from jax.sharding import PartitionSpec as P


STEPS = 8
IMG_EVERY = 4
NOFF = 33
SURFACE = 4
HALF = 16
REACH = 4
TRIM = HALF - REACH
THIN = TRIM - REACH
LANES = 48

SCALE = 5040.0
WHOLE = (8064.0, -1008.0, 128.0, -9.0)
CENTRE = 6.0 * sum(WHOLE)

f32 = jnp.float32
bf16 = jnp.bfloat16


def vmem_specs(count):
    return [pl.BlockSpec(memory_space=pltpu.VMEM)] * count


def params(megabytes):
    return pltpu.CompilerParams(vmem_limit_bytes=megabytes * 1024 * 1024)


def shape(*dims):
    return jax.ShapeDtypeStruct(dims, f32)


def place():
    me = lax.axis_index("gx")
    return lax.rem(me, 2), (me > 0) & (me < lax.axis_size("gx") - 1)


def split2(value):
    high = value.astype(bf16)
    low = (value - high.astype(f32)).astype(bf16)
    return high, low


def split3(value):
    high = value.astype(bf16)
    rest = value - high.astype(f32)
    mid = rest.astype(bf16)
    low = (rest - mid.astype(f32)).astype(bf16)
    return high, mid, low


def weights_of(gap):
    value = jnp.zeros(gap.shape, f32)
    for k, weight in enumerate(WHOLE):
        value = jnp.where(gap == k + 1, weight, value)
    return value


def depth_matrix(nz):
    row = lax.broadcasted_iota(jnp.int32, (nz, nz), 0)
    col = lax.broadcasted_iota(jnp.int32, (nz, nz), 1)
    band = weights_of(jnp.abs(row - col)).astype(bf16)
    return jnp.concatenate([band, band], axis=0)


def cross_matrix(ny):
    bits = ny.bit_length() - 1
    row = lax.broadcasted_iota(jnp.int32, (8 * ny, 16 * ny), 0)
    col = lax.broadcasted_iota(jnp.int32, (8 * ny, 16 * ny), 1)
    along = jnp.abs(lax.shift_right_logical(col, bits) - lax.shift_right_logical(row, bits) - REACH)
    aside = jnp.abs(jnp.bitwise_and(col, ny - 1) - jnp.bitwise_and(row, ny - 1))
    band = jnp.where(aside == 0, weights_of(along), 0.0) + jnp.where(along == 0, weights_of(aside), 0.0)
    band = band.astype(bf16)
    return jnp.concatenate([band, band], axis=1)


def neighbours(high, low, r0, depth, cross):
    _, ny, both = high.shape
    nz = both // 2
    h, l = high[r0 : r0 + 8].reshape(8 * ny, both), low[r0 : r0 + 8].reshape(8 * ny, both)
    split = [jnp.concatenate([h[:, cut], l[:, cut]], axis=1) for cut in (slice(0, nz), slice(nz, both))]
    deep = jnp.dot(jnp.concatenate(split, axis=0), depth, preferred_element_type=f32)
    rows = slice(r0 - REACH, r0 + 8 + REACH)
    around = jnp.concatenate([high[rows].reshape(16 * ny, both), low[rows].reshape(16 * ny, both)], axis=0)
    wide = jnp.dot(cross, around, preferred_element_type=f32)
    return wide[:, 0:nz] + deep[0 : 8 * ny], wide[:, nz:] + deep[8 * ny :]


def keep(high, low, rows, plain, scaled):
    pair = jnp.concatenate([plain, scaled], axis=plain.ndim - 1)
    h, l = split2(pair)
    high[rows] = h
    low[rows] = l


def pack_kernel(*refs, count):
    args, copies, sems = refs[:count], refs[count : 2 * count], refs[-1]
    far_coef, far_r, near = refs[2 * count : -1]
    moves = [pltpu.make_async_copy(a, b, sems.at[i]) for i, (a, b) in enumerate(zip(args, copies))]
    for move in moves:
        move.start()
    for move in moves:
        move.wait()
    s0, sp, r0, rp, stiff, buoy = copies[:6]
    p, _ = place()
    n = s0.shape[0]
    far_cut, near_cut = pl.ds(REACH * p, TRIM), pl.ds(REACH * (1 - p), TRIM)
    far_coef[0:n] = buoy[...]
    far_coef[n : n + TRIM] = stiff[far_cut]
    far_coef[n + TRIM :] = sp[far_cut]
    far_r[0:n] = r0[...]
    far_r[n:] = rp[far_cut]
    near[0:n] = buoy[...]
    near[n : n + TRIM] = stiff[near_cut]
    near[n + TRIM : 2 * n + TRIM] = s0[...]
    near[2 * n + TRIM : 2 * (n + TRIM)] = sp[near_cut]
    near[2 * (n + TRIM) : 3 * n + 2 * TRIM] = r0[...]
    near[3 * n + 2 * TRIM :] = rp[near_cut]


def spread(cells, parts, lateral, steps):
    width = cells.shape[1]
    bits = lateral.bit_length() - 1
    crossline = jnp.bitwise_and(cells, lateral - 1)
    inline = lax.shift_right_arithmetic(cells, bits) - (lax.axis_index("gx") * HALF - TRIM)
    here = lax.broadcasted_iota(jnp.int32, (lateral, width), 0) == crossline
    hot = jnp.where(lax.broadcasted_iota(jnp.int32, (LANES, width), 0) == inline, 1.0, 0.0).astype(bf16)
    total = None
    for part in parts:
        part = part.astype(f32)
        rows = [jnp.where(here, part[t : t + 1], 0.0) for t in range(steps)]
        term = lax.dot_general(
            jnp.concatenate(rows, axis=0).astype(bf16), hot, (((1,), (1,)), ((), ())), preferred_element_type=f32
        )
        total = term if total is None else total + term
    return total


def shots_kernel(shots, fire, wavelet, planes, depth, cross):
    steps, lateral, _ = planes.shape
    taps, ns = wavelet.shape
    delay = lax.broadcasted_iota(jnp.int32, (steps, ns), 0) - fire[...]
    amounts = jnp.zeros((steps, ns), f32)
    for d in range(taps):
        amounts = amounts + jnp.where(delay == d, wavelet[d : d + 1, :], 0.0)
    depth[...] = depth_matrix(depth.shape[1])
    cross[...] = cross_matrix(lateral)
    total = spread(shots[...], split3(amounts), lateral, steps)
    planes[:, :, 0:LANES] = total.reshape(steps, lateral, LANES)


def receivers_kernel(cells, traces, planes, acc, hops):
    groups = cells.shape[0]
    steps, lateral, _ = planes.shape
    me = lax.axis_index("gx")

    def owner(q):
        other = me
        for bit, hop in enumerate(hops):
            other = jnp.bitwise_xor(other, hop * jnp.bitwise_and(lax.shift_right_logical(q, bit), 1))
        return other

    acc[...] = jnp.zeros(acc.shape, f32)

    def gather(j, carry):
        row = jnp.concatenate([cells[pl.ds(owner(2 * j + half), 1), :] for half in range(2)], axis=1)
        block = jnp.concatenate([traces[2 * j], traces[2 * j + 1]], axis=1)
        back = jnp.concatenate([block[steps - 1 - t : steps - t] for t in range(steps)], axis=0)
        acc[:, 0:LANES] += spread(row, split3(back), lateral, steps)
        return carry

    lax.fori_loop(0, groups // 2, gather, 0, unroll=8)
    planes[:, :, 0:LANES] = acc[:, 0:LANES].reshape(steps, lateral, LANES)


def load_field(dst, own, od, od_lo, ev, ev_lo, n, full):
    p, there = place()
    rows = own.shape[0]
    dst[rows : 2 * rows] = own[...]
    skip = 0 if full else REACH
    dst[pl.ds(2 * rows * p + skip * (1 - p), n)] = jnp.where(there, od[od_lo : od_lo + n], 0.0)
    dst[pl.ds(2 * rows * (1 - p) + skip * p, n)] = ev[ev_lo : ev_lo + n]


def run_steps(field, parts, coefs, planes, depth, cross, base):
    buoy, kb, kk, gg = coefs
    wide, ny, nz = field[0].shape
    surface = lax.broadcasted_iota(jnp.int32, (8, nz), 1) == SURFACE
    band = depth[...], cross[...]
    for r0 in range(0, wide, 8):
        rows = slice(r0, r0 + 8)
        keep(*parts[0], rows, field[0][rows], buoy[rows] * field[0][rows])
    for step in range(IMG_EVERY):
        old, new = field[step % 2], field[1 - step % 2]
        first = REACH * (step + 1)
        for r0 in range(first, wide - first, 8):
            rows = slice(r0, r0 + 8)
            plain, scaled = neighbours(*parts[step % 2], r0, *band)
            terms = []
            for i in range(8):
                for t in range(ny // 8):
                    term = pltpu.roll(planes[base + step, 8 * t : 8 * t + 8, :], (SURFACE - (r0 + i - REACH)) % nz, axis=1)
                    terms.append(jnp.where(surface, term, 0.0))
            fresh = gg[rows] * old[rows] - new[rows] + jnp.concatenate(terms, axis=0).reshape(8, ny, nz)
            fresh = fresh + kb[rows] * plain.reshape(8, ny, nz) + kk[rows] * scaled.reshape(8, ny, nz)
            new[rows] = fresh
            if step < IMG_EVERY - 1:
                keep(*parts[1 - step % 2], rows, fresh, buoy[rows] * fresh)


def finish(field, n, now_out, before_out, od_out, ev_out):
    last, earlier = field[IMG_EVERY % 2], field[1 - IMG_EVERY % 2]
    value, thin = last[n : 2 * n], earlier[n + REACH : n + REACH + THIN]
    now_out[...] = value
    before_out[...] = earlier[n - REACH : 2 * n + REACH]
    for out in (od_out, ev_out):
        out[0:n] = value
        out[n:] = thin


def first_kernel(own, prior, stiff, buoy_own, far_own, far_coef, ev, planes, depth, cross, now_out, before_out, od_out, ev_out, buoy, kb, kk, gg, f0, f1, h0, l0, h1, l1):
    n, ny, nz = own.shape
    band = depth[...], cross[...]
    load_field(buoy, buoy_own, far_coef, 0, ev, 0, n, True)
    load_field(f1, stiff, far_coef, n, ev, n, TRIM, False)
    load_field(f0, own, far_own, 0, ev, n + TRIM, n, True)
    for r0 in range(0, 3 * n, 8):
        rows = slice(r0, r0 + 8)
        keep(h1, l1, rows, buoy[rows], f0[rows])
    for r0 in range(REACH, 3 * n - REACH, 8):
        rows = slice(r0, r0 + 8)
        around, _ = neighbours(h1, l1, r0, *band)
        b = buoy[rows]
        k = f1[rows] * (0.5 / SCALE)
        kk[rows] = k
        kb[rows] = k * b
        gg[rows] = 2.0 - k * (CENTRE * b + around.reshape(8, ny, nz))
    load_field(f1, prior, far_coef, n + TRIM, ev, 2 * n + TRIM, TRIM, False)
    run_steps((f0, f1), ((h0, l0), (h1, l1)), (buoy, kb, kk, gg), planes, depth, cross, 0)
    finish((f0, f1), n, now_out, before_out, od_out, ev_out)


def block_steps(own, prior, od, ev, planes, depth, cross, coefs, field, parts, base, near=0):
    n = own.shape[0]
    load_field(field[0], own, od, 0, ev, near, n, True)
    if prior.shape[0] == n:
        load_field(field[1], prior, od, n, ev, near + n, TRIM, False)
    else:
        p, there = place()
        field[1][n - REACH : 2 * n + REACH] = prior[...]
        field[1][pl.ds(2 * n * p + REACH, THIN)] = jnp.where(there, od[n:], 0.0)
        field[1][pl.ds(2 * n * (1 - p) + REACH, THIN)] = ev[n:]
    run_steps(field, parts, coefs, planes, depth, cross, base)


def block_kernel(own, prior, od, ev, planes, depth, cross, buoy, kb, kk, gg, now_out, before_out, od_out, ev_out, f0, f1, h0, l0, h1, l1, base, near):
    block_steps(own, prior, od, ev, planes, depth, cross, (buoy, kb, kk, gg), (f0, f1), ((h0, l0), (h1, l1)), base, near)
    finish((f0, f1), own.shape[0], now_out, before_out, od_out, ev_out)


def last_kernel(own, prior, od, ev, planes, depth, cross, buoy, kb, kk, gg, now_out, f0, f1, h0, l0, h1, l1, base):
    block_steps(own, prior, od, ev, planes, depth, cross, (buoy, kb, kk, gg), (f0, f1), ((h0, l0), (h1, l1)), base)
    n = own.shape[0]
    now_out[...] = (f0, f1)[IMG_EVERY % 2][n : 2 * n]


def lagged(lag_s, lag_r, levels, x, lag):
    total = None
    for level in levels:
        term = lag_s[level, HALF + x - lag] * lag_r[level, HALF + x + lag]
        total = term if total is None else total + term
    return total


def sides():
    p, there = place()
    return p, there, 1 - 2 * p, lambda reach: (HALF - reach) * p, lambda reach: reach * (1 - p)


def place_rows(dst, level, own, od, od_lo, ev, ev_lo):
    p, there = place()
    n = own.shape[0]
    dst[level, n : 2 * n] = own[...]
    if od is not None:
        dst[level, pl.ds(2 * n * p, n)] = jnp.where(there, od[od_lo : od_lo + n], 0.0)
    dst[level, pl.ds(2 * n * (1 - p), n)] = ev[ev_lo : ev_lo + n]


def early_image_kernel(s0, s4, r0, r4, far_s0, ev1, ods, evs, evr, block, lag_s, lag_r):
    _, _, sign, _, own_start = sides()
    n = s0.shape[0]
    place_rows(lag_s, 0, s0, far_s0, 0, ev1, n + TRIM)
    place_rows(lag_r, 0, r0, None, 0, ev1, 2 * (n + TRIM))
    place_rows(lag_s, 1, s4, ods, 0, evs, 0)
    place_rows(lag_r, 1, r4, None, 0, evr, 0)

    def whole(j, carry):
        for x in range(n):
            block[j, x] = lagged(lag_s, lag_r, (0, 1), x, sign * j)
        return carry

    lax.fori_loop(0, HALF + 1, whole, 0)
    for reach in range(1, HALF):
        for i in range(n - reach):
            block[HALF + reach, i] = lagged(lag_s, lag_r, (0, 1), own_start(reach) + i, -sign * reach)


def image_kernel(s0, s4, s8, r0, r4, r8, ev1, far_r, evs, odr, evr, ods8, evs8, evr8, early, out, rest, lag_s, lag_r, block, sems):
    _, _, sign, far_start, own_start = sides()
    n = s0.shape[0]
    place_rows(lag_s, 2, s8, ods8, 0, evs8, 0)
    place_rows(lag_r, 2, r8, None, 0, evr8, 0)
    move = lambda j: pltpu.make_async_copy(block.at[j], out.at[HALF + sign * j], sems.at[j])

    def whole(j, carry):
        for x in range(n):
            block[j, x] = early[j, x] + lagged(lag_s, lag_r, (2,), x, sign * j)
        move(j).start()
        return carry

    lax.fori_loop(0, HALF + 1, whole, 0)
    moves = []
    for reach in range(1, HALF):
        for i in range(n - reach):
            block[HALF + reach, i] = early[HALF + reach, i] + lagged(lag_s, lag_r, (2,), own_start(reach) + i, -sign * reach)
        target = out.at[HALF - sign * reach, pl.ds(own_start(reach), n - reach)]
        moves.append(pltpu.make_async_copy(block.at[HALF + reach, 0 : n - reach], target, sems.at[HALF + reach]))
        moves[-1].start()
    place_rows(lag_s, 0, s0, None, 0, ev1, n + TRIM)
    place_rows(lag_r, 0, r0, far_r, 0, ev1, 2 * (n + TRIM))
    place_rows(lag_s, 1, s4, None, 0, evs, 0)
    place_rows(lag_r, 1, r4, odr, 0, evr, 0)
    for reach in range(1, HALF + 1):
        for i in range(reach):
            rest[reach * (reach - 1) // 2 + i] = lagged(lag_s, lag_r, (0, 1), far_start(reach) + i, -sign * reach)

    def drain(j, carry):
        move(j).wait()
        return carry

    lax.fori_loop(0, HALF + 1, drain, 0)
    for each in moves:
        each.wait()


def last_image_kernel(s8, r8, evs8, odr8, rest, before, out, lag_s, lag_r, block, sems):
    p, there, sign, far_start, _ = sides()
    n = s8.shape[0]
    lag_s[0, n : 2 * n] = s8[...]
    lag_s[0, pl.ds(2 * n * (1 - p), n)] = evs8[...]
    lag_r[0, n : 2 * n] = r8[...]
    lag_r[0, pl.ds(2 * n * p, n)] = jnp.where(there, odr8[...], 0.0)
    moves = []
    for reach in range(HALF, 0, -1):
        base = reach * (reach - 1) // 2
        for i in range(reach):
            block[base + i] = rest[base + i] + lagged(lag_s, lag_r, (0,), far_start(reach) + i, -sign * reach)
        target = out.at[HALF - sign * reach, pl.ds(far_start(reach), reach)]
        moves.append(pltpu.make_async_copy(block.at[base : base + reach], target, sems.at[reach - 1]))
        moves[-1].start()
    for each in moves:
        each.wait()


def estimate(flops, nbytes):
    return pl.CostEstimate(flops=flops, bytes_accessed=nbytes, transcendentals=0)


def local(source_field, source_prior, receiver_field, receiver_prior, stiffness, buoyancy, wavelet, fire_step, shot_cell, receiver_cell, traces):
    n, ny, nz = source_field.shape
    shots, count = lax.axis_size("shot"), lax.axis_size("gx")
    near = [(i, i ^ 1) for i in range(count)]
    far = [(s * count + i, s * count + i + 1) for s in range(shots) for i in range(1, count - 1, 2)]
    far = far + [(b, a) for a, b in far]
    if shots % 2 == 0:
        far += [(s * count + e, (s ^ 1) * count + e) for s in range(shots) for e in (0, count - 1)]

    def swap_near(x):
        return lax.ppermute(x, "gx", near)

    def swap_far(x):
        return lax.ppermute(x, ("shot", "gx"), far)

    hops = [2, 1] if count > 2 else [1]
    while 2 * max(hops) < count:
        hops.append(2 * max(hops))

    def exchange(x, which):
        return lax.ppermute(x, "gx", [(i, i ^ hops[which]) for i in range(count)])

    far_s0 = swap_far(source_field)
    received = exchange(traces[None], 0)

    small = n + TRIM
    width = traces.shape[1]
    ns = shot_cell.shape[0]
    args = (
        source_field,
        source_prior,
        receiver_field,
        receiver_prior,
        stiffness,
        buoyancy,
        traces[None],
        receiver_cell.reshape(count, width),
        shot_cell.reshape(1, ns),
        fire_step.reshape(1, ns),
        wavelet.T,
    )
    packed = pl.pallas_call(
        functools.partial(pack_kernel, count=len(args)),
        out_shape=[jax.ShapeDtypeStruct(a.shape, a.dtype) for a in args]
        + [shape(n + 2 * TRIM, ny, nz), shape(small, ny, nz), shape(3 * small, ny, nz)],
        in_specs=[pl.BlockSpec(memory_space=pltpu.MemorySpace.HBM)] * len(args),
        out_specs=vmem_specs(len(args) + 3),
        scratch_shapes=[pltpu.SemaphoreType.DMA((len(args),))],
        compiler_params=params(8),
        cost_estimate=estimate(1000, 3000000),
        name="pack",
    )(*(pltpu.with_memory_space_constraint(a, pltpu.MemorySpace.HBM) for a in args))
    source_field, source_prior, receiver_field, receiver_prior, stiffness, buoyancy, gathered, cells, shot_row, fire_row, wave = packed[: len(args)]
    far_coef, far_r, ev1 = packed[len(args) :]
    far_coef = swap_far(far_coef)
    far_r = swap_far(far_r)
    ev1 = swap_near(ev1)

    gathered = jnp.concatenate([gathered, received], axis=0)
    for which in range(1, len(hops)):
        gathered = jnp.concatenate([gathered, exchange(gathered, which)], axis=0)

    plane = shape(STEPS, ny, nz)
    plane_s, *band = pl.pallas_call(
        shots_kernel,
        out_shape=[plane, jax.ShapeDtypeStruct((2 * nz, nz), bf16), jax.ShapeDtypeStruct((8 * ny, 32 * ny), bf16)],
        in_specs=vmem_specs(3),
        out_specs=vmem_specs(3),
        compiler_params=params(8),
        cost_estimate=estimate(1000000, 100000),
        name="shots",
    )(shot_row, fire_row, wave)
    plane_r = pl.pallas_call(
        functools.partial(receivers_kernel, hops=tuple(hops)),
        out_shape=plane,
        in_specs=vmem_specs(2),
        out_specs=pl.BlockSpec(memory_space=pltpu.VMEM),
        scratch_shapes=[pltpu.VMEM((STEPS * ny, nz), f32)],
        compiler_params=params(8),
        cost_estimate=estimate(2 * LANES * STEPS * ny * 2048, 1000000),
        name="receivers",
    )(cells, gathered)

    wide = 3 * n
    scratch = [pltpu.VMEM((wide, ny, nz), f32)] * 2 + [pltpu.VMEM((wide, ny, 2 * nz), bf16)] * 4
    cost = estimate(224 * 8 * 128 * 60, 6000000)
    own, prior = shape(n, ny, nz), shape(n + 2 * REACH, ny, nz)
    s4, s3, ods, evs, buoy, kb, kk, gg = pl.pallas_call(
        first_kernel,
        out_shape=[own, prior, shape(n + THIN, ny, nz), shape(n + THIN, ny, nz)] + [shape(wide, ny, nz)] * 4,
        in_specs=vmem_specs(10),
        out_specs=vmem_specs(8),
        scratch_shapes=scratch,
        compiler_params=params(16),
        cost_estimate=cost,
        name="first_s",
    )(source_field, source_prior, stiffness, buoyancy, far_s0, far_coef, ev1, plane_s, *band)
    coefs = (buoy, kb, kk, gg)
    ods = swap_far(ods)
    evs = swap_near(evs)
    r4, r3, odr, evr = pl.pallas_call(
        functools.partial(block_kernel, base=0, near=2 * small),
        out_shape=[own, prior, shape(n + THIN, ny, nz), shape(n + THIN, ny, nz)],
        in_specs=vmem_specs(11),
        out_specs=vmem_specs(4),
        scratch_shapes=scratch,
        compiler_params=params(16),
        cost_estimate=cost,
        name="first_r",
    )(receiver_field, receiver_prior, far_r, ev1, plane_r, *band, *coefs)
    odr = swap_far(odr)
    evr = swap_near(evr)

    def last():
        return pl.pallas_call(
            functools.partial(last_kernel, base=IMG_EVERY),
            out_shape=own,
            in_specs=vmem_specs(11),
            out_specs=pl.BlockSpec(memory_space=pltpu.VMEM),
            scratch_shapes=scratch,
            compiler_params=params(16),
            cost_estimate=cost,
        )

    s8 = last()(s4, s3, ods, evs, plane_s, *band, *coefs)
    ods8 = swap_far(s8)
    evs8 = swap_near(s8)
    r8 = last()(r4, r3, odr, evr, plane_r, *band, *coefs)
    odr8 = swap_far(r8)
    evr8 = swap_near(r8)
    lags = lambda levels: [pltpu.VMEM((levels, wide, ny, nz), f32)] * 2
    corner = HALF * (HALF + 1) // 2
    hbm = pl.BlockSpec(memory_space=pltpu.MemorySpace.HBM)
    early = pl.pallas_call(
        early_image_kernel,
        out_shape=shape(2 * HALF, n, ny, nz),
        in_specs=vmem_specs(9),
        out_specs=pl.BlockSpec(memory_space=pltpu.VMEM),
        scratch_shapes=lags(2),
        compiler_params=params(8),
        cost_estimate=estimate(NOFF * n * ny * nz * 3, 1000000),
        name="early_image",
    )(source_field, s4, receiver_field, r4, far_s0, ev1, ods, evs, evr)
    image, rest = pl.pallas_call(
        image_kernel,
        out_shape=[shape(NOFF, n, ny, nz), shape(corner, ny, nz)],
        in_specs=vmem_specs(15),
        out_specs=[hbm, pl.BlockSpec(memory_space=pltpu.VMEM)],
        scratch_shapes=lags(3) + [pltpu.VMEM((2 * HALF, n, ny, nz), f32), pltpu.SemaphoreType.DMA((2 * HALF,))],
        compiler_params=params(16),
        cost_estimate=estimate(NOFF * n * ny * nz * 4, 4400000),
        name="image",
    )(source_field, s4, s8, receiver_field, r4, r8, ev1, far_r, evs, odr, evr, ods8, evs8, evr8, early)
    return pl.pallas_call(
        last_image_kernel,
        out_shape=shape(NOFF, n, ny, nz),
        in_specs=vmem_specs(5) + [hbm],
        out_specs=hbm,
        scratch_shapes=lags(1) + [pltpu.VMEM((corner, ny, nz), f32), pltpu.SemaphoreType.DMA((HALF,))],
        input_output_aliases={5: 0},
        compiler_params=params(16),
        cost_estimate=estimate(HALF * n * ny * nz * 2, 2200000),
        name="last_image",
    )(s8, r8, evs8, odr8, rest, image)


def solution(mesh):
    placed = (
        P(("shot", "gx"), None, None),
        P(("shot", "gx"), None, None),
        P(("shot", "gx"), None, None),
        P(("shot", "gx"), None, None),
        P("gx", None, None),
        P("gx", None, None),
        P("shot", None),
        P("shot"),
        P("shot"),
        P("shot"),
        P("shot", "gx"),
    )
    return jax.shard_map(local, mesh=mesh, in_specs=placed, out_specs=P("shot", "gx", None, None), check_vma=False)
```

```python
import functools

import jax
import jax.numpy as jnp
from jax import lax
from jax.experimental import pallas as pl
from jax.experimental.pallas import tpu as pltpu
from jax.sharding import PartitionSpec as P


STEPS = 8
IMG_EVERY = 4
NOFF = 33
SURFACE = 4
HALF = 16
REACH = 4
TRIM = HALF - REACH
THIN = TRIM - REACH
LANES = 48

SCALE = 5040.0
WHOLE = (8064.0, -1008.0, 128.0, -9.0)
CENTRE = 6.0 * sum(WHOLE)

f32 = jnp.float32
bf16 = jnp.bfloat16


def vmem_specs(count):
    return [pl.BlockSpec(memory_space=pltpu.VMEM)] * count


def params(megabytes):
    return pltpu.CompilerParams(vmem_limit_bytes=megabytes * 1024 * 1024)


def shape(*dims):
    return jax.ShapeDtypeStruct(dims, f32)


def place():
    me = lax.axis_index("gx")
    return lax.rem(me, 2), (me > 0) & (me < lax.axis_size("gx") - 1)


def split2(value):
    high = value.astype(bf16)
    low = (value - high.astype(f32)).astype(bf16)
    return high, low


def split3(value):
    high = value.astype(bf16)
    rest = value - high.astype(f32)
    mid = rest.astype(bf16)
    low = (rest - mid.astype(f32)).astype(bf16)
    return high, mid, low


def weights_of(gap):
    value = jnp.zeros(gap.shape, f32)
    for k, weight in enumerate(WHOLE):
        value = jnp.where(gap == k + 1, weight, value)
    return value


def depth_matrix(nz):
    row = lax.broadcasted_iota(jnp.int32, (nz, nz), 0)
    col = lax.broadcasted_iota(jnp.int32, (nz, nz), 1)
    band = weights_of(jnp.abs(row - col)).astype(bf16)
    return jnp.concatenate([band, band], axis=0)


def cross_matrix(ny):
    bits = ny.bit_length() - 1
    row = lax.broadcasted_iota(jnp.int32, (8 * ny, 16 * ny), 0)
    col = lax.broadcasted_iota(jnp.int32, (8 * ny, 16 * ny), 1)
    along = jnp.abs(lax.shift_right_logical(col, bits) - lax.shift_right_logical(row, bits) - REACH)
    aside = jnp.abs(jnp.bitwise_and(col, ny - 1) - jnp.bitwise_and(row, ny - 1))
    band = jnp.where(aside == 0, weights_of(along), 0.0) + jnp.where(along == 0, weights_of(aside), 0.0)
    band = band.astype(bf16)
    return jnp.concatenate([band, band], axis=1)


def neighbours(high, low, r0, depth, cross):
    _, ny, both = high.shape
    nz = both // 2
    h, l = high[r0 : r0 + 8].reshape(8 * ny, both), low[r0 : r0 + 8].reshape(8 * ny, both)
    split = [jnp.concatenate([h[:, cut], l[:, cut]], axis=1) for cut in (slice(0, nz), slice(nz, both))]
    deep = jnp.dot(jnp.concatenate(split, axis=0), depth, preferred_element_type=f32)
    rows = slice(r0 - REACH, r0 + 8 + REACH)
    around = jnp.concatenate([high[rows].reshape(16 * ny, both), low[rows].reshape(16 * ny, both)], axis=0)
    wide = jnp.dot(cross, around, preferred_element_type=f32)
    return wide[:, 0:nz] + deep[0 : 8 * ny], wide[:, nz:] + deep[8 * ny :]


def keep(high, low, rows, plain, scaled):
    pair = jnp.concatenate([plain, scaled], axis=plain.ndim - 1)
    h, l = split2(pair)
    high[rows] = h
    low[rows] = l


def pack_kernel(*refs, count):
    args, copies, sems = refs[:count], refs[count : 2 * count], refs[-1]
    far_coef, far_r, near = refs[2 * count : -1]
    moves = [pltpu.make_async_copy(a, b, sems.at[i]) for i, (a, b) in enumerate(zip(args, copies))]
    for move in moves:
        move.start()
    for move in moves:
        move.wait()
    s0, sp, r0, rp, stiff, buoy = copies[:6]
    p, _ = place()
    n = s0.shape[0]
    far_cut, near_cut = pl.ds(REACH * p, TRIM), pl.ds(REACH * (1 - p), TRIM)
    far_coef[0:n] = buoy[...]
    far_coef[n : n + TRIM] = stiff[far_cut]
    far_coef[n + TRIM :] = sp[far_cut]
    far_r[0:n] = r0[...]
    far_r[n:] = rp[far_cut]
    near[0:n] = buoy[...]
    near[n : n + TRIM] = stiff[near_cut]
    near[n + TRIM : 2 * n + TRIM] = s0[...]
    near[2 * n + TRIM : 2 * (n + TRIM)] = sp[near_cut]
    near[2 * (n + TRIM) : 3 * n + 2 * TRIM] = r0[...]
    near[3 * n + 2 * TRIM :] = rp[near_cut]


def spread(cells, parts, lateral, steps):
    width = cells.shape[1]
    bits = lateral.bit_length() - 1
    crossline = jnp.bitwise_and(cells, lateral - 1)
    inline = lax.shift_right_arithmetic(cells, bits) - (lax.axis_index("gx") * HALF - TRIM)
    here = lax.broadcasted_iota(jnp.int32, (lateral, width), 0) == crossline
    hot = jnp.where(lax.broadcasted_iota(jnp.int32, (LANES, width), 0) == inline, 1.0, 0.0).astype(bf16)
    total = None
    for part in parts:
        part = part.astype(f32)
        rows = [jnp.where(here, part[t : t + 1], 0.0) for t in range(steps)]
        term = lax.dot_general(
            jnp.concatenate(rows, axis=0).astype(bf16), hot, (((1,), (1,)), ((), ())), preferred_element_type=f32
        )
        total = term if total is None else total + term
    return total


def shots_kernel(shots, fire, wavelet, planes, depth, cross):
    steps, lateral, _ = planes.shape
    taps, ns = wavelet.shape
    delay = lax.broadcasted_iota(jnp.int32, (steps, ns), 0) - fire[...]
    amounts = jnp.zeros((steps, ns), f32)
    for d in range(taps):
        amounts = amounts + jnp.where(delay == d, wavelet[d : d + 1, :], 0.0)
    depth[...] = depth_matrix(depth.shape[1])
    cross[...] = cross_matrix(lateral)
    total = spread(shots[...], split3(amounts), lateral, steps)
    planes[:, :, 0:LANES] = total.reshape(steps, lateral, LANES)


def receivers_kernel(cells, traces, planes, acc, hops):
    groups = cells.shape[0]
    steps, lateral, _ = planes.shape
    me = lax.axis_index("gx")

    def owner(q):
        other = me
        for bit, hop in enumerate(hops):
            other = jnp.bitwise_xor(other, hop * jnp.bitwise_and(lax.shift_right_logical(q, bit), 1))
        return other

    acc[...] = jnp.zeros(acc.shape, f32)

    def gather(j, carry):
        row = jnp.concatenate([cells[pl.ds(owner(2 * j + half), 1), :] for half in range(2)], axis=1)
        block = jnp.concatenate([traces[2 * j], traces[2 * j + 1]], axis=1)
        back = jnp.concatenate([block[steps - 1 - t : steps - t] for t in range(steps)], axis=0)
        acc[:, 0:LANES] += spread(row, split3(back), lateral, steps)
        return carry

    lax.fori_loop(0, groups // 2, gather, 0, unroll=8)
    planes[:, :, 0:LANES] = acc[:, 0:LANES].reshape(steps, lateral, LANES)


def load_field(dst, own, od, od_lo, ev, ev_lo, n, full):
    p, there = place()
    rows = own.shape[0]
    dst[rows : 2 * rows] = own[...]
    skip = 0 if full else REACH
    dst[pl.ds(2 * rows * p + skip * (1 - p), n)] = jnp.where(there, od[od_lo : od_lo + n], 0.0)
    dst[pl.ds(2 * rows * (1 - p) + skip * p, n)] = ev[ev_lo : ev_lo + n]


def run_steps(field, parts, coefs, planes, depth, cross, base):
    buoy, kb, kk, gg = coefs
    wide, ny, nz = field[0].shape
    surface = lax.broadcasted_iota(jnp.int32, (8, nz), 1) == SURFACE
    band = depth[...], cross[...]
    for r0 in range(0, wide, 8):
        rows = slice(r0, r0 + 8)
        keep(*parts[0], rows, field[0][rows], buoy[rows] * field[0][rows])
    for step in range(IMG_EVERY):
        old, new = field[step % 2], field[1 - step % 2]
        first = REACH * (step + 1)
        for r0 in range(first, wide - first, 8):
            rows = slice(r0, r0 + 8)
            plain, scaled = neighbours(*parts[step % 2], r0, *band)
            terms = []
            for i in range(8):
                for t in range(ny // 8):
                    term = pltpu.roll(planes[base + step, 8 * t : 8 * t + 8, :], (SURFACE - (r0 + i - REACH)) % nz, axis=1)
                    terms.append(jnp.where(surface, term, 0.0))
            fresh = gg[rows] * old[rows] - new[rows] + jnp.concatenate(terms, axis=0).reshape(8, ny, nz)
            fresh = fresh + kb[rows] * plain.reshape(8, ny, nz) + kk[rows] * scaled.reshape(8, ny, nz)
            new[rows] = fresh
            if step < IMG_EVERY - 1:
                keep(*parts[1 - step % 2], rows, fresh, buoy[rows] * fresh)


def finish(field, n, now_out, before_out, od_out, ev_out):
    last, earlier = field[IMG_EVERY % 2], field[1 - IMG_EVERY % 2]
    value, thin = last[n : 2 * n], earlier[n + REACH : n + REACH + THIN]
    now_out[...] = value
    before_out[...] = earlier[n - REACH : 2 * n + REACH]
    for out in (od_out, ev_out):
        out[0:n] = value
        out[n:] = thin


def first_kernel(own, prior, stiff, buoy_own, far_own, far_coef, ev, planes, depth, cross, now_out, before_out, od_out, ev_out, buoy, kb, kk, gg, f0, f1, h0, l0, h1, l1):
    n, ny, nz = own.shape
    band = depth[...], cross[...]
    load_field(buoy, buoy_own, far_coef, 0, ev, 0, n, True)
    load_field(f1, stiff, far_coef, n, ev, n, TRIM, False)
    load_field(f0, own, far_own, 0, ev, n + TRIM, n, True)
    for r0 in range(0, 3 * n, 8):
        rows = slice(r0, r0 + 8)
        keep(h1, l1, rows, buoy[rows], f0[rows])
    for r0 in range(REACH, 3 * n - REACH, 8):
        rows = slice(r0, r0 + 8)
        around, _ = neighbours(h1, l1, r0, *band)
        b = buoy[rows]
        k = f1[rows] * (0.5 / SCALE)
        kk[rows] = k
        kb[rows] = k * b
        gg[rows] = 2.0 - k * (CENTRE * b + around.reshape(8, ny, nz))
    load_field(f1, prior, far_coef, n + TRIM, ev, 2 * n + TRIM, TRIM, False)
    run_steps((f0, f1), ((h0, l0), (h1, l1)), (buoy, kb, kk, gg), planes, depth, cross, 0)
    finish((f0, f1), n, now_out, before_out, od_out, ev_out)


def block_steps(own, prior, od, ev, planes, depth, cross, coefs, field, parts, base, near=0):
    n = own.shape[0]
    load_field(field[0], own, od, 0, ev, near, n, True)
    if prior.shape[0] == n:
        load_field(field[1], prior, od, n, ev, near + n, TRIM, False)
    else:
        p, there = place()
        field[1][n - REACH : 2 * n + REACH] = prior[...]
        field[1][pl.ds(2 * n * p + REACH, THIN)] = jnp.where(there, od[n:], 0.0)
        field[1][pl.ds(2 * n * (1 - p) + REACH, THIN)] = ev[n:]
    run_steps(field, parts, coefs, planes, depth, cross, base)


def block_kernel(own, prior, od, ev, planes, depth, cross, buoy, kb, kk, gg, now_out, before_out, od_out, ev_out, f0, f1, h0, l0, h1, l1, base, near):
    block_steps(own, prior, od, ev, planes, depth, cross, (buoy, kb, kk, gg), (f0, f1), ((h0, l0), (h1, l1)), base, near)
    finish((f0, f1), own.shape[0], now_out, before_out, od_out, ev_out)


def last_kernel(own, prior, od, ev, planes, depth, cross, buoy, kb, kk, gg, now_out, f0, f1, h0, l0, h1, l1, base):
    block_steps(own, prior, od, ev, planes, depth, cross, (buoy, kb, kk, gg), (f0, f1), ((h0, l0), (h1, l1)), base)
    n = own.shape[0]
    now_out[...] = (f0, f1)[IMG_EVERY % 2][n : 2 * n]


def lagged(lag_s, lag_r, levels, x, lag):
    total = None
    for level in levels:
        term = lag_s[level, HALF + x - lag] * lag_r[level, HALF + x + lag]
        total = term if total is None else total + term
    return total


def sides():
    p, there = place()
    return p, there, 1 - 2 * p, lambda reach: (HALF - reach) * p, lambda reach: reach * (1 - p)


def place_rows(dst, level, own, od, od_lo, ev, ev_lo):
    p, there = place()
    n = own.shape[0]
    dst[level, n : 2 * n] = own[...]
    if od is not None:
        dst[level, pl.ds(2 * n * p, n)] = jnp.where(there, od[od_lo : od_lo + n], 0.0)
    dst[level, pl.ds(2 * n * (1 - p), n)] = ev[ev_lo : ev_lo + n]


def first_image_kernel(s0, r0, far_s0, ev1, block, lag_s, lag_r):
    _, _, sign, _, own_start = sides()
    n = s0.shape[0]
    place_rows(lag_s, 0, s0, far_s0, 0, ev1, n + TRIM)
    place_rows(lag_r, 0, r0, None, 0, ev1, 2 * (n + TRIM))

    def whole(j, carry):
        for x in range(n):
            block[j, x] = lagged(lag_s, lag_r, (0,), x, sign * j)
        return carry

    lax.fori_loop(0, HALF + 1, whole, 0)
    for reach in range(1, HALF):
        for i in range(n - reach):
            block[HALF + reach, i] = lagged(lag_s, lag_r, (0,), own_start(reach) + i, -sign * reach)


def early_image_kernel(s4, r4, ods, evs, evr, before, block, lag_s, lag_r):
    _, _, sign, _, own_start = sides()
    n = s4.shape[0]
    place_rows(lag_s, 0, s4, ods, 0, evs, 0)
    place_rows(lag_r, 0, r4, None, 0, evr, 0)

    def whole(j, carry):
        for x in range(n):
            block[j, x] = before[j, x] + lagged(lag_s, lag_r, (0,), x, sign * j)
        return carry

    lax.fori_loop(0, HALF + 1, whole, 0)
    for reach in range(1, HALF):
        for i in range(n - reach):
            block[HALF + reach, i] = before[HALF + reach, i] + lagged(lag_s, lag_r, (0,), own_start(reach) + i, -sign * reach)


def image_kernel(s0, s4, s8, r0, r4, r8, ev1, far_r, evs, odr, evr, ods8, evs8, evr8, early, out, rest, lag_s, lag_r, block, sems):
    _, _, sign, far_start, own_start = sides()
    n = s0.shape[0]
    place_rows(lag_s, 2, s8, ods8, 0, evs8, 0)
    place_rows(lag_r, 2, r8, None, 0, evr8, 0)
    move = lambda j: pltpu.make_async_copy(block.at[j], out.at[HALF + sign * j], sems.at[j])

    def whole(j, carry):
        for x in range(n):
            block[j, x] = early[j, x] + lagged(lag_s, lag_r, (2,), x, sign * j)
        move(j).start()
        return carry

    lax.fori_loop(0, HALF + 1, whole, 0)
    moves = []
    for reach in range(1, HALF):
        for i in range(n - reach):
            block[HALF + reach, i] = early[HALF + reach, i] + lagged(lag_s, lag_r, (2,), own_start(reach) + i, -sign * reach)
        target = out.at[HALF - sign * reach, pl.ds(own_start(reach), n - reach)]
        moves.append(pltpu.make_async_copy(block.at[HALF + reach, 0 : n - reach], target, sems.at[HALF + reach]))
        moves[-1].start()
    place_rows(lag_s, 0, s0, None, 0, ev1, n + TRIM)
    place_rows(lag_r, 0, r0, far_r, 0, ev1, 2 * (n + TRIM))
    place_rows(lag_s, 1, s4, None, 0, evs, 0)
    place_rows(lag_r, 1, r4, odr, 0, evr, 0)
    for reach in range(1, HALF + 1):
        for i in range(reach):
            rest[reach * (reach - 1) // 2 + i] = lagged(lag_s, lag_r, (0, 1), far_start(reach) + i, -sign * reach)

    def drain(j, carry):
        move(j).wait()
        return carry

    lax.fori_loop(0, HALF + 1, drain, 0)
    for each in moves:
        each.wait()


def last_image_kernel(s8, r8, evs8, odr8, rest, before, out, lag_s, lag_r, block, sems):
    p, there, sign, far_start, _ = sides()
    n = s8.shape[0]
    lag_s[0, n : 2 * n] = s8[...]
    lag_s[0, pl.ds(2 * n * (1 - p), n)] = evs8[...]
    lag_r[0, n : 2 * n] = r8[...]
    lag_r[0, pl.ds(2 * n * p, n)] = jnp.where(there, odr8[...], 0.0)
    moves = []
    for reach in range(HALF, 0, -1):
        base = reach * (reach - 1) // 2
        for i in range(reach):
            block[base + i] = rest[base + i] + lagged(lag_s, lag_r, (0,), far_start(reach) + i, -sign * reach)
        target = out.at[HALF - sign * reach, pl.ds(far_start(reach), reach)]
        moves.append(pltpu.make_async_copy(block.at[base : base + reach], target, sems.at[reach - 1]))
        moves[-1].start()
    for each in moves:
        each.wait()


def estimate(flops, nbytes):
    return pl.CostEstimate(flops=flops, bytes_accessed=nbytes, transcendentals=0)


def local(source_field, source_prior, receiver_field, receiver_prior, stiffness, buoyancy, wavelet, fire_step, shot_cell, receiver_cell, traces):
    n, ny, nz = source_field.shape
    shots, count = lax.axis_size("shot"), lax.axis_size("gx")
    near = [(i, i ^ 1) for i in range(count)]
    far = [(s * count + i, s * count + i + 1) for s in range(shots) for i in range(1, count - 1, 2)]
    far = far + [(b, a) for a, b in far]
    if shots % 2 == 0:
        far += [(s * count + e, (s ^ 1) * count + e) for s in range(shots) for e in (0, count - 1)]

    def swap_near(x):
        return lax.ppermute(x, "gx", near)

    def swap_far(x):
        return lax.ppermute(x, ("shot", "gx"), far)

    hops = [2, 1] if count > 2 else [1]
    hops += [1 << bit for bit in range(count.bit_length() - 2, 1, -1)]

    def exchange(x, which):
        return lax.ppermute(x, "gx", [(i, i ^ hops[which]) for i in range(count)])

    far_s0 = swap_far(source_field)
    received = exchange(traces[None], 0)

    small = n + TRIM
    width = traces.shape[1]
    ns = shot_cell.shape[0]
    args = (
        source_field,
        source_prior,
        receiver_field,
        receiver_prior,
        stiffness,
        buoyancy,
        traces[None],
        receiver_cell.reshape(count, width),
        shot_cell.reshape(1, ns),
        fire_step.reshape(1, ns),
        wavelet.T,
    )
    packed = pl.pallas_call(
        functools.partial(pack_kernel, count=len(args)),
        out_shape=[jax.ShapeDtypeStruct(a.shape, a.dtype) for a in args]
        + [shape(n + 2 * TRIM, ny, nz), shape(small, ny, nz), shape(3 * small, ny, nz)],
        in_specs=[pl.BlockSpec(memory_space=pltpu.MemorySpace.HBM)] * len(args),
        out_specs=vmem_specs(len(args) + 3),
        scratch_shapes=[pltpu.SemaphoreType.DMA((len(args),))],
        compiler_params=params(8),
        cost_estimate=estimate(1000, 3000000),
        name="pack",
    )(*(pltpu.with_memory_space_constraint(a, pltpu.MemorySpace.HBM) for a in args))
    source_field, source_prior, receiver_field, receiver_prior, stiffness, buoyancy, gathered, cells, shot_row, fire_row, wave = packed[: len(args)]
    far_coef, far_r, ev1 = packed[len(args) :]
    far_coef = swap_far(far_coef)
    far_r = swap_far(far_r)
    ev1 = swap_near(ev1)

    gathered = jnp.concatenate([gathered, received], axis=0)
    for which in range(1, len(hops)):
        gathered = jnp.concatenate([gathered, exchange(gathered, which)], axis=0)

    plane = shape(STEPS, ny, nz)
    plane_s, *band = pl.pallas_call(
        shots_kernel,
        out_shape=[plane, jax.ShapeDtypeStruct((2 * nz, nz), bf16), jax.ShapeDtypeStruct((8 * ny, 32 * ny), bf16)],
        in_specs=vmem_specs(3),
        out_specs=vmem_specs(3),
        compiler_params=params(8),
        cost_estimate=estimate(1000000, 100000),
        name="shots",
    )(shot_row, fire_row, wave)
    plane_r = pl.pallas_call(
        functools.partial(receivers_kernel, hops=tuple(hops)),
        out_shape=plane,
        in_specs=vmem_specs(2),
        out_specs=pl.BlockSpec(memory_space=pltpu.VMEM),
        scratch_shapes=[pltpu.VMEM((STEPS * ny, nz), f32)],
        compiler_params=params(8),
        cost_estimate=estimate(2 * LANES * STEPS * ny * 2048, 1000000),
        name="receivers",
    )(cells, gathered)

    wide = 3 * n
    scratch = [pltpu.VMEM((wide, ny, nz), f32)] * 2 + [pltpu.VMEM((wide, ny, 2 * nz), bf16)] * 4
    cost = estimate(224 * 8 * 128 * 60, 6000000)
    own, prior = shape(n, ny, nz), shape(n + 2 * REACH, ny, nz)
    s4, s3, ods, evs, buoy, kb, kk, gg = pl.pallas_call(
        first_kernel,
        out_shape=[own, prior, shape(n + THIN, ny, nz), shape(n + THIN, ny, nz)] + [shape(wide, ny, nz)] * 4,
        in_specs=vmem_specs(10),
        out_specs=vmem_specs(8),
        scratch_shapes=scratch,
        compiler_params=params(16),
        cost_estimate=cost,
        name="first_s",
    )(source_field, source_prior, stiffness, buoyancy, far_s0, far_coef, ev1, plane_s, *band)
    coefs = (buoy, kb, kk, gg)
    ods = swap_far(ods)
    evs = swap_near(evs)
    r4, r3, odr, evr = pl.pallas_call(
        functools.partial(block_kernel, base=0, near=2 * small),
        out_shape=[own, prior, shape(n + THIN, ny, nz), shape(n + THIN, ny, nz)],
        in_specs=vmem_specs(11),
        out_specs=vmem_specs(4),
        scratch_shapes=scratch,
        compiler_params=params(16),
        cost_estimate=cost,
        name="first_r",
    )(receiver_field, receiver_prior, far_r, ev1, plane_r, *band, *coefs)
    odr = swap_far(odr)
    evr = swap_near(evr)

    def last():
        return pl.pallas_call(
            functools.partial(last_kernel, base=IMG_EVERY),
            out_shape=own,
            in_specs=vmem_specs(11),
            out_specs=pl.BlockSpec(memory_space=pltpu.VMEM),
            scratch_shapes=scratch,
            compiler_params=params(16),
            cost_estimate=cost,
        )

    s8 = last()(s4, s3, ods, evs, plane_s, *band, *coefs)
    ods8 = swap_far(s8)
    evs8 = swap_near(s8)
    r8 = last()(r4, r3, odr, evr, plane_r, *band, *coefs)
    odr8 = swap_far(r8)
    evr8 = swap_near(r8)
    lags = lambda levels: [pltpu.VMEM((levels, wide, ny, nz), f32)] * 2
    corner = HALF * (HALF + 1) // 2
    hbm = pl.BlockSpec(memory_space=pltpu.MemorySpace.HBM)

    def products(kernel, *inputs):
        return pl.pallas_call(
            kernel,
            out_shape=shape(2 * HALF, n, ny, nz),
            in_specs=vmem_specs(len(inputs)),
            out_specs=pl.BlockSpec(memory_space=pltpu.VMEM),
            scratch_shapes=lags(1),
            compiler_params=params(8),
            cost_estimate=estimate(NOFF * n * ny * nz * 3, 1000000),
        )(*inputs)

    early = products(first_image_kernel, source_field, receiver_field, far_s0, ev1)
    early = products(early_image_kernel, s4, r4, ods, evs, evr, early)
    image, rest = pl.pallas_call(
        image_kernel,
        out_shape=[shape(NOFF, n, ny, nz), shape(corner, ny, nz)],
        in_specs=vmem_specs(15),
        out_specs=[hbm, pl.BlockSpec(memory_space=pltpu.VMEM)],
        scratch_shapes=lags(3) + [pltpu.VMEM((2 * HALF, n, ny, nz), f32), pltpu.SemaphoreType.DMA((2 * HALF,))],
        compiler_params=params(16),
        cost_estimate=estimate(NOFF * n * ny * nz * 4, 4400000),
        name="image",
    )(source_field, s4, s8, receiver_field, r4, r8, ev1, far_r, evs, odr, evr, ods8, evs8, evr8, early)
    return pl.pallas_call(
        last_image_kernel,
        out_shape=shape(NOFF, n, ny, nz),
        in_specs=vmem_specs(5) + [hbm],
        out_specs=hbm,
        scratch_shapes=lags(1) + [pltpu.VMEM((corner, ny, nz), f32), pltpu.SemaphoreType.DMA((HALF,))],
        input_output_aliases={5: 0},
        compiler_params=params(16),
        cost_estimate=estimate(HALF * n * ny * nz * 2, 2200000),
        name="last_image",
    )(s8, r8, evs8, odr8, rest, image)


def solution(mesh):
    placed = (
        P(("shot", "gx"), None, None),
        P(("shot", "gx"), None, None),
        P(("shot", "gx"), None, None),
        P(("shot", "gx"), None, None),
        P("gx", None, None),
        P("gx", None, None),
        P("shot", None),
        P("shot"),
        P("shot"),
        P("shot"),
        P("shot", "gx"),
    )
    return jax.shard_map(local, mesh=mesh, in_specs=placed, out_specs=P("shot", "gx", None, None), check_vma=False)
```

```python
import functools

import jax
import jax.numpy as jnp
from jax import lax
from jax.experimental import pallas as pl
from jax.experimental.pallas import tpu as pltpu
from jax.sharding import PartitionSpec as P


STEPS = 8
IMG_EVERY = 4
NOFF = 33
SURFACE = 4
HALF = 16
REACH = 4
TRIM = HALF - REACH
THIN = TRIM - REACH
LANES = 48

SCALE = 5040.0
WHOLE = (8064.0, -1008.0, 128.0, -9.0)
CENTRE = 6.0 * sum(WHOLE)

f32 = jnp.float32
bf16 = jnp.bfloat16


def vmem_specs(count):
    return [pl.BlockSpec(memory_space=pltpu.VMEM)] * count


def params(megabytes):
    return pltpu.CompilerParams(vmem_limit_bytes=megabytes * 1024 * 1024)


def shape(*dims):
    return jax.ShapeDtypeStruct(dims, f32)


def place():
    me = lax.axis_index("gx")
    return lax.rem(me, 2), (me > 0) & (me < lax.axis_size("gx") - 1)


def split2(value):
    high = value.astype(bf16)
    low = (value - high.astype(f32)).astype(bf16)
    return high, low


def split3(value):
    high = value.astype(bf16)
    rest = value - high.astype(f32)
    mid = rest.astype(bf16)
    low = (rest - mid.astype(f32)).astype(bf16)
    return high, mid, low


def weights_of(gap):
    value = jnp.zeros(gap.shape, f32)
    for k, weight in enumerate(WHOLE):
        value = jnp.where(gap == k + 1, weight, value)
    return value


def depth_matrix(nz):
    row = lax.broadcasted_iota(jnp.int32, (nz, nz), 0)
    col = lax.broadcasted_iota(jnp.int32, (nz, nz), 1)
    band = weights_of(jnp.abs(row - col)).astype(bf16)
    return jnp.concatenate([band, band], axis=0)


def cross_matrix(ny):
    bits = ny.bit_length() - 1
    row = lax.broadcasted_iota(jnp.int32, (8 * ny, 16 * ny), 0)
    col = lax.broadcasted_iota(jnp.int32, (8 * ny, 16 * ny), 1)
    along = jnp.abs(lax.shift_right_logical(col, bits) - lax.shift_right_logical(row, bits) - REACH)
    aside = jnp.abs(jnp.bitwise_and(col, ny - 1) - jnp.bitwise_and(row, ny - 1))
    band = jnp.where(aside == 0, weights_of(along), 0.0) + jnp.where(along == 0, weights_of(aside), 0.0)
    band = band.astype(bf16)
    return jnp.concatenate([band, band], axis=1)


def neighbours(high, low, r0, depth, cross):
    _, ny, both = high.shape
    nz = both // 2
    h, l = high[r0 : r0 + 8].reshape(8 * ny, both), low[r0 : r0 + 8].reshape(8 * ny, both)
    split = [jnp.concatenate([h[:, cut], l[:, cut]], axis=1) for cut in (slice(0, nz), slice(nz, both))]
    deep = jnp.dot(jnp.concatenate(split, axis=0), depth, preferred_element_type=f32)
    rows = slice(r0 - REACH, r0 + 8 + REACH)
    around = jnp.concatenate([high[rows].reshape(16 * ny, both), low[rows].reshape(16 * ny, both)], axis=0)
    wide = jnp.dot(cross, around, preferred_element_type=f32)
    return wide[:, 0:nz] + deep[0 : 8 * ny], wide[:, nz:] + deep[8 * ny :]


def keep(high, low, rows, plain, scaled):
    pair = jnp.concatenate([plain, scaled], axis=plain.ndim - 1)
    h, l = split2(pair)
    high[rows] = h
    low[rows] = l


def pack_kernel(*refs, count):
    args, copies, sems = refs[:count], refs[count : 2 * count], refs[-1]
    far_coef, far_r, near = refs[2 * count : -1]
    moves = [pltpu.make_async_copy(a, b, sems.at[i]) for i, (a, b) in enumerate(zip(args, copies))]
    for move in moves:
        move.start()
    for move in moves:
        move.wait()
    s0, sp, r0, rp, stiff, buoy = copies[:6]
    p, _ = place()
    n = s0.shape[0]
    far_cut, near_cut = pl.ds(REACH * p, TRIM), pl.ds(REACH * (1 - p), TRIM)
    far_coef[0:n] = buoy[...]
    far_coef[n : n + TRIM] = stiff[far_cut]
    far_coef[n + TRIM :] = sp[far_cut]
    far_r[0:n] = r0[...]
    far_r[n:] = rp[far_cut]
    near[0:n] = buoy[...]
    near[n : n + TRIM] = stiff[near_cut]
    near[n + TRIM : 2 * n + TRIM] = s0[...]
    near[2 * n + TRIM : 2 * (n + TRIM)] = sp[near_cut]
    near[2 * (n + TRIM) : 3 * n + 2 * TRIM] = r0[...]
    near[3 * n + 2 * TRIM :] = rp[near_cut]


def spread(cells, parts, lateral, steps):
    width = cells.shape[1]
    bits = lateral.bit_length() - 1
    crossline = jnp.bitwise_and(cells, lateral - 1)
    inline = lax.shift_right_arithmetic(cells, bits) - (lax.axis_index("gx") * HALF - TRIM)
    here = lax.broadcasted_iota(jnp.int32, (lateral, width), 0) == crossline
    hot = jnp.where(lax.broadcasted_iota(jnp.int32, (LANES, width), 0) == inline, 1.0, 0.0).astype(bf16)
    total = None
    for part in parts:
        part = part.astype(f32)
        rows = [jnp.where(here, part[t : t + 1], 0.0) for t in range(steps)]
        term = lax.dot_general(
            jnp.concatenate(rows, axis=0).astype(bf16), hot, (((1,), (1,)), ((), ())), preferred_element_type=f32
        )
        total = term if total is None else total + term
    return total


def shots_kernel(shots, fire, wavelet, planes, depth, cross):
    steps, lateral, _ = planes.shape
    taps, ns = wavelet.shape
    delay = lax.broadcasted_iota(jnp.int32, (steps, ns), 0) - fire[...]
    amounts = jnp.zeros((steps, ns), f32)
    for d in range(taps):
        amounts = amounts + jnp.where(delay == d, wavelet[d : d + 1, :], 0.0)
    depth[...] = depth_matrix(depth.shape[1])
    cross[...] = cross_matrix(lateral)
    total = spread(shots[...], split3(amounts), lateral, steps)
    planes[:, :, 0:LANES] = total.reshape(steps, lateral, LANES)


def receivers_kernel(cells, traces, received, planes, acc, hops):
    steps, lateral, _ = planes.shape
    me = lax.axis_index("gx")

    def owner(q):
        other = me
        for bit, hop in enumerate(hops):
            other = jnp.bitwise_xor(other, hop * jnp.bitwise_and(lax.shift_right_logical(q, bit), 1))
        return other

    acc[...] = jnp.zeros(acc.shape, f32)
    for source, first in ((traces, 0), (received, traces.shape[0])):

        def gather(j, carry, source=source, first=first):
            row = jnp.concatenate([cells[pl.ds(owner(first + 2 * j + half), 1), :] for half in range(2)], axis=1)
            block = jnp.concatenate([source[2 * j], source[2 * j + 1]], axis=1)
            back = jnp.concatenate([block[steps - 1 - t : steps - t] for t in range(steps)], axis=0)
            acc[:, 0:LANES] += spread(row, split3(back), lateral, steps)
            return carry

        lax.fori_loop(0, source.shape[0] // 2, gather, 0, unroll=4)
    planes[:, :, 0:LANES] = acc[:, 0:LANES].reshape(steps, lateral, LANES)


def load_field(dst, own, od, od_lo, ev, ev_lo, n, full):
    p, there = place()
    rows = own.shape[0]
    dst[rows : 2 * rows] = own[...]
    skip = 0 if full else REACH
    dst[pl.ds(2 * rows * p + skip * (1 - p), n)] = jnp.where(there, od[od_lo : od_lo + n], 0.0)
    dst[pl.ds(2 * rows * (1 - p) + skip * p, n)] = ev[ev_lo : ev_lo + n]


def run_steps(field, parts, coefs, planes, depth, cross, base):
    buoy, kb, kk, gg = coefs
    wide, ny, nz = field[0].shape
    surface = lax.broadcasted_iota(jnp.int32, (8, nz), 1) == SURFACE
    band = depth[...], cross[...]
    for r0 in range(0, wide, 8):
        rows = slice(r0, r0 + 8)
        keep(*parts[0], rows, field[0][rows], buoy[rows] * field[0][rows])
    for step in range(IMG_EVERY):
        old, new = field[step % 2], field[1 - step % 2]
        first = REACH * (step + 1)
        for r0 in range(first, wide - first, 8):
            rows = slice(r0, r0 + 8)
            plain, scaled = neighbours(*parts[step % 2], r0, *band)
            terms = []
            for i in range(8):
                for t in range(ny // 8):
                    term = pltpu.roll(planes[base + step, 8 * t : 8 * t + 8, :], (SURFACE - (r0 + i - REACH)) % nz, axis=1)
                    terms.append(jnp.where(surface, term, 0.0))
            fresh = gg[rows] * old[rows] - new[rows] + jnp.concatenate(terms, axis=0).reshape(8, ny, nz)
            fresh = fresh + kb[rows] * plain.reshape(8, ny, nz) + kk[rows] * scaled.reshape(8, ny, nz)
            new[rows] = fresh
            if step < IMG_EVERY - 1:
                keep(*parts[1 - step % 2], rows, fresh, buoy[rows] * fresh)


def finish(field, n, now_out, before_out, od_out, ev_out):
    last, earlier = field[IMG_EVERY % 2], field[1 - IMG_EVERY % 2]
    value, thin = last[n : 2 * n], earlier[n + REACH : n + REACH + THIN]
    now_out[...] = value
    before_out[...] = earlier[n - REACH : 2 * n + REACH]
    for out in (od_out, ev_out):
        out[0:n] = value
        out[n:] = thin


def first_kernel(own, prior, stiff, buoy_own, far_own, far_coef, ev, planes, depth, cross, now_out, before_out, od_out, ev_out, buoy, kb, kk, gg, f0, f1, h0, l0, h1, l1):
    n, ny, nz = own.shape
    band = depth[...], cross[...]
    load_field(buoy, buoy_own, far_coef, 0, ev, 0, n, True)
    load_field(f1, stiff, far_coef, n, ev, n, TRIM, False)
    load_field(f0, own, far_own, 0, ev, n + TRIM, n, True)
    for r0 in range(0, 3 * n, 8):
        rows = slice(r0, r0 + 8)
        keep(h1, l1, rows, buoy[rows], f0[rows])
    for r0 in range(REACH, 3 * n - REACH, 8):
        rows = slice(r0, r0 + 8)
        around, _ = neighbours(h1, l1, r0, *band)
        b = buoy[rows]
        k = f1[rows] * (0.5 / SCALE)
        kk[rows] = k
        kb[rows] = k * b
        gg[rows] = 2.0 - k * (CENTRE * b + around.reshape(8, ny, nz))
    load_field(f1, prior, far_coef, n + TRIM, ev, 2 * n + TRIM, TRIM, False)
    run_steps((f0, f1), ((h0, l0), (h1, l1)), (buoy, kb, kk, gg), planes, depth, cross, 0)
    finish((f0, f1), n, now_out, before_out, od_out, ev_out)


def block_steps(own, prior, od, ev, planes, depth, cross, coefs, field, parts, base, near=0):
    n = own.shape[0]
    load_field(field[0], own, od, 0, ev, near, n, True)
    if prior.shape[0] == n:
        load_field(field[1], prior, od, n, ev, near + n, TRIM, False)
    else:
        p, there = place()
        field[1][n - REACH : 2 * n + REACH] = prior[...]
        field[1][pl.ds(2 * n * p + REACH, THIN)] = jnp.where(there, od[n:], 0.0)
        field[1][pl.ds(2 * n * (1 - p) + REACH, THIN)] = ev[n:]
    run_steps(field, parts, coefs, planes, depth, cross, base)


def block_kernel(own, prior, od, ev, planes, depth, cross, buoy, kb, kk, gg, now_out, before_out, od_out, ev_out, f0, f1, h0, l0, h1, l1, base, near):
    block_steps(own, prior, od, ev, planes, depth, cross, (buoy, kb, kk, gg), (f0, f1), ((h0, l0), (h1, l1)), base, near)
    finish((f0, f1), own.shape[0], now_out, before_out, od_out, ev_out)


def last_kernel(own, prior, od, ev, planes, depth, cross, buoy, kb, kk, gg, now_out, f0, f1, h0, l0, h1, l1, base):
    block_steps(own, prior, od, ev, planes, depth, cross, (buoy, kb, kk, gg), (f0, f1), ((h0, l0), (h1, l1)), base)
    n = own.shape[0]
    now_out[...] = (f0, f1)[IMG_EVERY % 2][n : 2 * n]


def lagged(lag_s, lag_r, levels, x, lag):
    total = None
    for level in levels:
        term = lag_s[level, HALF + x - lag] * lag_r[level, HALF + x + lag]
        total = term if total is None else total + term
    return total


def sides():
    p, there = place()
    return p, there, 1 - 2 * p, lambda reach: (HALF - reach) * p, lambda reach: reach * (1 - p)


def place_rows(dst, level, own, od, od_lo, ev, ev_lo):
    p, there = place()
    n = own.shape[0]
    dst[level, n : 2 * n] = own[...]
    if od is not None:
        dst[level, pl.ds(2 * n * p, n)] = jnp.where(there, od[od_lo : od_lo + n], 0.0)
    dst[level, pl.ds(2 * n * (1 - p), n)] = ev[ev_lo : ev_lo + n]


def first_image_kernel(s0, r0, far_s0, ev1, block, lag_s, lag_r):
    _, _, sign, _, own_start = sides()
    n = s0.shape[0]
    place_rows(lag_s, 0, s0, far_s0, 0, ev1, n + TRIM)
    place_rows(lag_r, 0, r0, None, 0, ev1, 2 * (n + TRIM))

    def whole(j, carry):
        for x in range(n):
            block[j, x] = lagged(lag_s, lag_r, (0,), x, sign * j)
        return carry

    lax.fori_loop(0, HALF + 1, whole, 0)
    for reach in range(1, HALF):
        for i in range(n - reach):
            block[HALF + reach, i] = lagged(lag_s, lag_r, (0,), own_start(reach) + i, -sign * reach)


def early_image_kernel(s4, r4, ods, evs, evr, before, block, lag_s, lag_r):
    _, _, sign, _, own_start = sides()
    n = s4.shape[0]
    place_rows(lag_s, 0, s4, ods, 0, evs, 0)
    place_rows(lag_r, 0, r4, None, 0, evr, 0)

    def whole(j, carry):
        for x in range(n):
            block[j, x] = before[j, x] + lagged(lag_s, lag_r, (0,), x, sign * j)
        return carry

    lax.fori_loop(0, HALF + 1, whole, 0)
    for reach in range(1, HALF):
        for i in range(n - reach):
            block[HALF + reach, i] = before[HALF + reach, i] + lagged(lag_s, lag_r, (0,), own_start(reach) + i, -sign * reach)


def image_kernel(s0, s4, s8, r0, r4, r8, ev1, far_r, evs, odr, evr, ods8, evs8, evr8, early, out, rest, wide_s, lag_s, lag_r, block, sems):
    _, _, sign, far_start, own_start = sides()
    n = s0.shape[0]
    place_rows(lag_s, 2, s8, ods8, 0, evs8, 0)
    wide_s[...] = lag_s[2]
    place_rows(lag_r, 2, r8, None, 0, evr8, 0)
    move = lambda j: pltpu.make_async_copy(block.at[j], out.at[HALF + sign * j], sems.at[j])

    def whole(j, carry):
        for x in range(n):
            block[j, x] = early[j, x] + lagged(lag_s, lag_r, (2,), x, sign * j)
        move(j).start()
        return carry

    lax.fori_loop(0, HALF + 1, whole, 0)
    moves = []
    for reach in range(1, HALF):
        for i in range(n - reach):
            block[HALF + reach, i] = early[HALF + reach, i] + lagged(lag_s, lag_r, (2,), own_start(reach) + i, -sign * reach)
        target = out.at[HALF - sign * reach, pl.ds(own_start(reach), n - reach)]
        moves.append(pltpu.make_async_copy(block.at[HALF + reach, 0 : n - reach], target, sems.at[HALF + reach]))
        moves[-1].start()
    place_rows(lag_s, 0, s0, None, 0, ev1, n + TRIM)
    place_rows(lag_r, 0, r0, far_r, 0, ev1, 2 * (n + TRIM))
    place_rows(lag_s, 1, s4, None, 0, evs, 0)
    place_rows(lag_r, 1, r4, odr, 0, evr, 0)
    for reach in range(1, HALF + 1):
        for i in range(reach):
            rest[reach * (reach - 1) // 2 + i] = lagged(lag_s, lag_r, (0, 1), far_start(reach) + i, -sign * reach)

    def drain(j, carry):
        move(j).wait()
        return carry

    lax.fori_loop(0, HALF + 1, drain, 0)
    for each in moves:
        each.wait()


def last_image_kernel(wide_s, odr8, rest, before, out, block, sems):
    p, there, sign, far_start, _ = sides()
    n = odr8.shape[0]
    moves = []
    for reach in range(HALF, 0, -1):
        base = reach * (reach - 1) // 2
        for i in range(reach):
            x = far_start(reach) + i
            far = jnp.where(there, odr8[x - sign * reach + n * (1 - 2 * p)], 0.0)
            block[base + i] = rest[base + i] + wide_s[HALF + x + sign * reach] * far
        target = out.at[HALF - sign * reach, pl.ds(far_start(reach), reach)]
        moves.append(pltpu.make_async_copy(block.at[base : base + reach], target, sems.at[reach - 1]))
        moves[-1].start()
    for each in moves:
        each.wait()


def estimate(flops, nbytes):
    return pl.CostEstimate(flops=flops, bytes_accessed=nbytes, transcendentals=0)


def local(source_field, source_prior, receiver_field, receiver_prior, stiffness, buoyancy, wavelet, fire_step, shot_cell, receiver_cell, traces):
    n, ny, nz = source_field.shape
    shots, count = lax.axis_size("shot"), lax.axis_size("gx")
    near = [(i, i ^ 1) for i in range(count)]
    far = [(s * count + i, s * count + i + 1) for s in range(shots) for i in range(1, count - 1, 2)]
    far = far + [(b, a) for a, b in far]
    if shots % 2 == 0:
        far += [(s * count + e, (s ^ 1) * count + e) for s in range(shots) for e in (0, count - 1)]

    def swap_near(x):
        return lax.ppermute(x, "gx", near)

    def swap_far(x):
        return lax.ppermute(x, ("shot", "gx"), far)

    hops = [2, 1] if count > 2 else [1]
    hops += [1 << bit for bit in range(count.bit_length() - 2, 1, -1)]

    def exchange(x, which):
        return lax.ppermute(x, "gx", [(i, i ^ hops[which]) for i in range(count)])

    far_s0 = swap_far(source_field)
    received = exchange(traces[None], 0)

    small = n + TRIM
    width = traces.shape[1]
    ns = shot_cell.shape[0]
    args = (
        source_field,
        source_prior,
        receiver_field,
        receiver_prior,
        stiffness,
        buoyancy,
        traces[None],
        receiver_cell.reshape(count, width),
        shot_cell.reshape(1, ns),
        fire_step.reshape(1, ns),
        wavelet.T,
    )
    packed = pl.pallas_call(
        functools.partial(pack_kernel, count=len(args)),
        out_shape=[jax.ShapeDtypeStruct(a.shape, a.dtype) for a in args]
        + [shape(n + 2 * TRIM, ny, nz), shape(small, ny, nz), shape(3 * small, ny, nz)],
        in_specs=[pl.BlockSpec(memory_space=pltpu.MemorySpace.HBM)] * len(args),
        out_specs=vmem_specs(len(args) + 3),
        scratch_shapes=[pltpu.SemaphoreType.DMA((len(args),))],
        compiler_params=params(8),
        cost_estimate=estimate(1000, 3000000),
        name="pack",
    )(*(pltpu.with_memory_space_constraint(a, pltpu.MemorySpace.HBM) for a in args))
    source_field, source_prior, receiver_field, receiver_prior, stiffness, buoyancy, gathered, cells, shot_row, fire_row, wave = packed[: len(args)]
    far_coef, far_r, ev1 = packed[len(args) :]
    far_coef = swap_far(far_coef)
    far_r = swap_far(far_r)
    ev1 = swap_near(ev1)

    gathered = jnp.concatenate([gathered, received], axis=0)
    for which in range(1, len(hops) - 1):
        gathered = jnp.concatenate([gathered, exchange(gathered, which)], axis=0)
    received = exchange(gathered, len(hops) - 1)

    plane = shape(STEPS, ny, nz)
    plane_s, *band = pl.pallas_call(
        shots_kernel,
        out_shape=[plane, jax.ShapeDtypeStruct((2 * nz, nz), bf16), jax.ShapeDtypeStruct((8 * ny, 32 * ny), bf16)],
        in_specs=vmem_specs(3),
        out_specs=vmem_specs(3),
        compiler_params=params(8),
        cost_estimate=estimate(1000000, 100000),
        name="shots",
    )(shot_row, fire_row, wave)
    plane_r = pl.pallas_call(
        functools.partial(receivers_kernel, hops=tuple(hops)),
        out_shape=plane,
        in_specs=vmem_specs(3),
        out_specs=pl.BlockSpec(memory_space=pltpu.VMEM),
        scratch_shapes=[pltpu.VMEM((STEPS * ny, nz), f32)],
        compiler_params=params(8),
        cost_estimate=estimate(2 * LANES * STEPS * ny * 2048, 1000000),
        name="receivers",
    )(cells, gathered, received)

    wide = 3 * n
    scratch = [pltpu.VMEM((wide, ny, nz), f32)] * 2 + [pltpu.VMEM((wide, ny, 2 * nz), bf16)] * 4
    cost = estimate(224 * 8 * 128 * 60, 6000000)
    own, prior = shape(n, ny, nz), shape(n + 2 * REACH, ny, nz)
    s4, s3, ods, evs, buoy, kb, kk, gg = pl.pallas_call(
        first_kernel,
        out_shape=[own, prior, shape(n + THIN, ny, nz), shape(n + THIN, ny, nz)] + [shape(wide, ny, nz)] * 4,
        in_specs=vmem_specs(10),
        out_specs=vmem_specs(8),
        scratch_shapes=scratch,
        compiler_params=params(16),
        cost_estimate=cost,
        name="first_s",
    )(source_field, source_prior, stiffness, buoyancy, far_s0, far_coef, ev1, plane_s, *band)
    coefs = (buoy, kb, kk, gg)
    ods = swap_far(ods)
    evs = swap_near(evs)
    r4, r3, odr, evr = pl.pallas_call(
        functools.partial(block_kernel, base=0, near=2 * small),
        out_shape=[own, prior, shape(n + THIN, ny, nz), shape(n + THIN, ny, nz)],
        in_specs=vmem_specs(11),
        out_specs=vmem_specs(4),
        scratch_shapes=scratch,
        compiler_params=params(16),
        cost_estimate=cost,
        name="first_r",
    )(receiver_field, receiver_prior, far_r, ev1, plane_r, *band, *coefs)
    odr = swap_far(odr)
    evr = swap_near(evr)

    def last():
        return pl.pallas_call(
            functools.partial(last_kernel, base=IMG_EVERY),
            out_shape=own,
            in_specs=vmem_specs(11),
            out_specs=pl.BlockSpec(memory_space=pltpu.VMEM),
            scratch_shapes=scratch,
            compiler_params=params(16),
            cost_estimate=cost,
        )

    s8 = last()(s4, s3, ods, evs, plane_s, *band, *coefs)
    ods8 = swap_far(s8)
    evs8 = swap_near(s8)
    r8 = last()(r4, r3, odr, evr, plane_r, *band, *coefs)
    odr8 = swap_far(r8)
    evr8 = swap_near(r8)
    lags = lambda levels: [pltpu.VMEM((levels, wide, ny, nz), f32)] * 2
    corner = HALF * (HALF + 1) // 2
    hbm = pl.BlockSpec(memory_space=pltpu.MemorySpace.HBM)

    def products(kernel, *inputs):
        return pl.pallas_call(
            kernel,
            out_shape=shape(2 * HALF, n, ny, nz),
            in_specs=vmem_specs(len(inputs)),
            out_specs=pl.BlockSpec(memory_space=pltpu.VMEM),
            scratch_shapes=lags(1),
            compiler_params=params(8),
            cost_estimate=estimate(NOFF * n * ny * nz * 3, 1000000),
        )(*inputs)

    early = products(first_image_kernel, source_field, receiver_field, far_s0, ev1)
    early = products(early_image_kernel, s4, r4, ods, evs, evr, early)
    image, rest, wide_s = pl.pallas_call(
        image_kernel,
        out_shape=[shape(NOFF, n, ny, nz), shape(corner, ny, nz), shape(wide, ny, nz)],
        in_specs=vmem_specs(15),
        out_specs=[hbm] + vmem_specs(2),
        scratch_shapes=lags(3) + [pltpu.VMEM((2 * HALF, n, ny, nz), f32), pltpu.SemaphoreType.DMA((2 * HALF,))],
        compiler_params=params(16),
        cost_estimate=estimate(NOFF * n * ny * nz * 4, 4400000),
        name="image",
    )(source_field, s4, s8, receiver_field, r4, r8, ev1, far_r, evs, odr, evr, ods8, evs8, evr8, early)
    return pl.pallas_call(
        last_image_kernel,
        out_shape=shape(NOFF, n, ny, nz),
        in_specs=vmem_specs(3) + [hbm],
        out_specs=hbm,
        scratch_shapes=[pltpu.VMEM((corner, ny, nz), f32), pltpu.SemaphoreType.DMA((HALF,))],
        input_output_aliases={3: 0},
        compiler_params=params(16),
        cost_estimate=estimate(HALF * n * ny * nz * 2, 2200000),
        name="last_image",
    )(wide_s, odr8, rest, image)


def solution(mesh):
    placed = (
        P(("shot", "gx"), None, None),
        P(("shot", "gx"), None, None),
        P(("shot", "gx"), None, None),
        P(("shot", "gx"), None, None),
        P("gx", None, None),
        P("gx", None, None),
        P("shot", None),
        P("shot"),
        P("shot"),
        P("shot"),
        P("shot", "gx"),
    )
    return jax.shard_map(local, mesh=mesh, in_specs=placed, out_specs=P("shot", "gx", None, None), check_vma=False)
```

```python
import functools

import jax
import jax.numpy as jnp
from jax import lax
from jax.experimental import pallas as pl
from jax.experimental.pallas import tpu as pltpu
from jax.sharding import PartitionSpec as P


STEPS = 8
IMG_EVERY = 4
NOFF = 33
SURFACE = 4
HALF = 16
REACH = 4
TRIM = HALF - REACH
THIN = TRIM - REACH
LANES = 48

SCALE = 5040.0
WHOLE = (8064.0, -1008.0, 128.0, -9.0)
CENTRE = 6.0 * sum(WHOLE)

f32 = jnp.float32
bf16 = jnp.bfloat16


def vmem_specs(count):
    return [pl.BlockSpec(memory_space=pltpu.VMEM)] * count


def params(megabytes):
    return pltpu.CompilerParams(vmem_limit_bytes=megabytes * 1024 * 1024)


def shape(*dims):
    return jax.ShapeDtypeStruct(dims, f32)


def place():
    me = lax.axis_index("gx")
    return lax.rem(me, 2), (me > 0) & (me < lax.axis_size("gx") - 1)


def split2(value):
    high = value.astype(bf16)
    low = (value - high.astype(f32)).astype(bf16)
    return high, low


def split3(value):
    high = value.astype(bf16)
    rest = value - high.astype(f32)
    mid = rest.astype(bf16)
    low = (rest - mid.astype(f32)).astype(bf16)
    return high, mid, low


def weights_of(gap):
    value = jnp.zeros(gap.shape, f32)
    for k, weight in enumerate(WHOLE):
        value = jnp.where(gap == k + 1, weight, value)
    return value


def depth_matrix(nz):
    row = lax.broadcasted_iota(jnp.int32, (nz, nz), 0)
    col = lax.broadcasted_iota(jnp.int32, (nz, nz), 1)
    band = weights_of(jnp.abs(row - col)).astype(bf16)
    return jnp.concatenate([band, band], axis=0)


def cross_matrix(ny):
    bits = ny.bit_length() - 1
    row = lax.broadcasted_iota(jnp.int32, (8 * ny, 16 * ny), 0)
    col = lax.broadcasted_iota(jnp.int32, (8 * ny, 16 * ny), 1)
    along = jnp.abs(lax.shift_right_logical(col, bits) - lax.shift_right_logical(row, bits) - REACH)
    aside = jnp.abs(jnp.bitwise_and(col, ny - 1) - jnp.bitwise_and(row, ny - 1))
    band = jnp.where(aside == 0, weights_of(along), 0.0) + jnp.where(along == 0, weights_of(aside), 0.0)
    band = band.astype(bf16)
    return jnp.concatenate([band, band], axis=1)


def neighbours(high, low, r0, depth, cross):
    _, ny, both = high.shape
    nz = both // 2
    h, l = high[r0 : r0 + 8].reshape(8 * ny, both), low[r0 : r0 + 8].reshape(8 * ny, both)
    split = [jnp.concatenate([h[:, cut], l[:, cut]], axis=1) for cut in (slice(0, nz), slice(nz, both))]
    deep = jnp.dot(jnp.concatenate(split, axis=0), depth, preferred_element_type=f32)
    rows = slice(r0 - REACH, r0 + 8 + REACH)
    around = jnp.concatenate([high[rows].reshape(16 * ny, both), low[rows].reshape(16 * ny, both)], axis=0)
    wide = jnp.dot(cross, around, preferred_element_type=f32)
    return wide[:, 0:nz] + deep[0 : 8 * ny], wide[:, nz:] + deep[8 * ny :]


def keep(high, low, rows, plain, scaled):
    pair = jnp.concatenate([plain, scaled], axis=plain.ndim - 1)
    h, l = split2(pair)
    high[rows] = h
    low[rows] = l


def pack_kernel(*refs, count):
    args, copies, sems = refs[:count], refs[count : 2 * count], refs[-1]
    far_coef, far_r, near = refs[2 * count : -1]
    moves = [pltpu.make_async_copy(a, b, sems.at[i]) for i, (a, b) in enumerate(zip(args, copies))]
    for move in moves:
        move.start()
    for move in moves:
        move.wait()
    s0, sp, r0, rp, stiff, buoy = copies[:6]
    p, _ = place()
    n = s0.shape[0]
    far_cut, near_cut = pl.ds(REACH * p, TRIM), pl.ds(REACH * (1 - p), TRIM)
    far_coef[0:n] = buoy[...]
    far_coef[n : n + TRIM] = stiff[far_cut]
    far_coef[n + TRIM :] = sp[far_cut]
    far_r[0:n] = r0[...]
    far_r[n:] = rp[far_cut]
    near[0:n] = buoy[...]
    near[n : n + TRIM] = stiff[near_cut]
    near[n + TRIM : 2 * n + TRIM] = s0[...]
    near[2 * n + TRIM : 2 * (n + TRIM)] = sp[near_cut]
    near[2 * (n + TRIM) : 3 * n + 2 * TRIM] = r0[...]
    near[3 * n + 2 * TRIM :] = rp[near_cut]


def spread(cells, parts, lateral, steps):
    width = cells.shape[1]
    bits = lateral.bit_length() - 1
    crossline = jnp.bitwise_and(cells, lateral - 1)
    inline = lax.shift_right_arithmetic(cells, bits) - (lax.axis_index("gx") * HALF - TRIM)
    here = lax.broadcasted_iota(jnp.int32, (lateral, width), 0) == crossline
    hot = jnp.where(lax.broadcasted_iota(jnp.int32, (LANES, width), 0) == inline, 1.0, 0.0).astype(bf16)
    total = None
    for part in parts:
        part = part.astype(f32)
        rows = [jnp.where(here, part[t : t + 1], 0.0) for t in range(steps)]
        term = lax.dot_general(
            jnp.concatenate(rows, axis=0).astype(bf16), hot, (((1,), (1,)), ((), ())), preferred_element_type=f32
        )
        total = term if total is None else total + term
    return total


def shots_kernel(shots, fire, wavelet, planes, depth, cross):
    steps, lateral, _ = planes.shape
    taps, ns = wavelet.shape
    delay = lax.broadcasted_iota(jnp.int32, (steps, ns), 0) - fire[...]
    amounts = jnp.zeros((steps, ns), f32)
    for d in range(taps):
        amounts = amounts + jnp.where(delay == d, wavelet[d : d + 1, :], 0.0)
    depth[...] = depth_matrix(depth.shape[1])
    cross[...] = cross_matrix(lateral)
    total = spread(shots[...], split3(amounts), lateral, steps)
    planes[:, :, 0:LANES] = total.reshape(steps, lateral, LANES)


def receivers_kernel(cells, traces, received, planes, acc, hops):
    steps, lateral, _ = planes.shape
    me = lax.axis_index("gx")

    def owner(q):
        other = me
        for bit, hop in enumerate(hops):
            other = jnp.bitwise_xor(other, hop * jnp.bitwise_and(lax.shift_right_logical(q, bit), 1))
        return other

    acc[...] = jnp.zeros(acc.shape, f32)
    for source, first in ((traces, 0), (received, traces.shape[0])):

        def gather(j, carry, source=source, first=first):
            row = jnp.concatenate([cells[pl.ds(owner(first + 2 * j + half), 1), :] for half in range(2)], axis=1)
            block = jnp.concatenate([source[2 * j], source[2 * j + 1]], axis=1)
            back = jnp.concatenate([block[steps - 1 - t : steps - t] for t in range(steps)], axis=0)
            acc[:, 0:LANES] += spread(row, split3(back), lateral, steps)
            return carry

        lax.fori_loop(0, source.shape[0] // 2, gather, 0, unroll=4)
    planes[:, :, 0:LANES] = acc[:, 0:LANES].reshape(steps, lateral, LANES)


def load_field(dst, own, od, od_lo, ev, ev_lo, n, full):
    p, there = place()
    rows = own.shape[0]
    dst[rows : 2 * rows] = own[...]
    skip = 0 if full else REACH
    dst[pl.ds(2 * rows * p + skip * (1 - p), n)] = jnp.where(there, od[od_lo : od_lo + n], 0.0)
    dst[pl.ds(2 * rows * (1 - p) + skip * p, n)] = ev[ev_lo : ev_lo + n]


def run_steps(field, parts, coefs, planes, depth, cross, base):
    buoy, kb, kk, gg = coefs
    wide, ny, nz = field[0].shape
    surface = lax.broadcasted_iota(jnp.int32, (8, nz), 1) == SURFACE
    band = depth[...], cross[...]
    for r0 in range(0, wide, 8):
        rows = slice(r0, r0 + 8)
        keep(*parts[0], rows, field[0][rows], buoy[rows] * field[0][rows])
    for step in range(IMG_EVERY):
        old, new = field[step % 2], field[1 - step % 2]
        first = REACH * (step + 1)
        for r0 in range(first, wide - first, 8):
            rows = slice(r0, r0 + 8)
            plain, scaled = neighbours(*parts[step % 2], r0, *band)
            terms = []
            for i in range(8):
                for t in range(ny // 8):
                    term = pltpu.roll(planes[base + step, 8 * t : 8 * t + 8, :], (SURFACE - (r0 + i - REACH)) % nz, axis=1)
                    terms.append(jnp.where(surface, term, 0.0))
            fresh = gg[rows] * old[rows] - new[rows] + jnp.concatenate(terms, axis=0).reshape(8, ny, nz)
            fresh = fresh + kb[rows] * plain.reshape(8, ny, nz) + kk[rows] * scaled.reshape(8, ny, nz)
            new[rows] = fresh
            if step < IMG_EVERY - 1:
                keep(*parts[1 - step % 2], rows, fresh, buoy[rows] * fresh)


def finish(field, n, now_out, before_out, od_out, ev_out):
    last, earlier = field[IMG_EVERY % 2], field[1 - IMG_EVERY % 2]
    value, thin = last[n : 2 * n], earlier[n + REACH : n + REACH + THIN]
    now_out[...] = value
    before_out[...] = earlier[n - REACH : 2 * n + REACH]
    for out in (od_out, ev_out):
        out[0:n] = value
        out[n:] = thin


def first_kernel(own, prior, stiff, buoy_own, far_own, far_coef, ev, planes, depth, cross, now_out, before_out, od_out, ev_out, buoy, kb, kk, gg, f0, f1, h0, l0, h1, l1):
    n, ny, nz = own.shape
    band = depth[...], cross[...]
    load_field(buoy, buoy_own, far_coef, 0, ev, 0, n, True)
    load_field(f1, stiff, far_coef, n, ev, n, TRIM, False)
    load_field(f0, own, far_own, 0, ev, n + TRIM, n, True)
    for r0 in range(0, 3 * n, 8):
        rows = slice(r0, r0 + 8)
        keep(h1, l1, rows, buoy[rows], f0[rows])
    for r0 in range(REACH, 3 * n - REACH, 8):
        rows = slice(r0, r0 + 8)
        around, _ = neighbours(h1, l1, r0, *band)
        b = buoy[rows]
        k = f1[rows] * (0.5 / SCALE)
        kk[rows] = k
        kb[rows] = k * b
        gg[rows] = 2.0 - k * (CENTRE * b + around.reshape(8, ny, nz))
    load_field(f1, prior, far_coef, n + TRIM, ev, 2 * n + TRIM, TRIM, False)
    run_steps((f0, f1), ((h0, l0), (h1, l1)), (buoy, kb, kk, gg), planes, depth, cross, 0)
    finish((f0, f1), n, now_out, before_out, od_out, ev_out)


def block_steps(own, prior, od, ev, planes, depth, cross, coefs, field, parts, base, near=0):
    n = own.shape[0]
    load_field(field[0], own, od, 0, ev, near, n, True)
    if prior.shape[0] == n:
        load_field(field[1], prior, od, n, ev, near + n, TRIM, False)
    else:
        p, there = place()
        field[1][n - REACH : 2 * n + REACH] = prior[...]
        field[1][pl.ds(2 * n * p + REACH, THIN)] = jnp.where(there, od[n:], 0.0)
        field[1][pl.ds(2 * n * (1 - p) + REACH, THIN)] = ev[n:]
    run_steps(field, parts, coefs, planes, depth, cross, base)


def block_kernel(own, prior, od, ev, planes, depth, cross, buoy, kb, kk, gg, now_out, before_out, od_out, ev_out, f0, f1, h0, l0, h1, l1, base, near):
    block_steps(own, prior, od, ev, planes, depth, cross, (buoy, kb, kk, gg), (f0, f1), ((h0, l0), (h1, l1)), base, near)
    finish((f0, f1), own.shape[0], now_out, before_out, od_out, ev_out)


def last_kernel(own, prior, od, ev, planes, depth, cross, buoy, kb, kk, gg, now_out, f0, f1, h0, l0, h1, l1, base):
    block_steps(own, prior, od, ev, planes, depth, cross, (buoy, kb, kk, gg), (f0, f1), ((h0, l0), (h1, l1)), base)
    n = own.shape[0]
    now_out[...] = (f0, f1)[IMG_EVERY % 2][n : 2 * n]


def lagged(lag_s, lag_r, levels, x, lag):
    total = None
    for level in levels:
        term = lag_s[level, HALF + x - lag] * lag_r[level, HALF + x + lag]
        total = term if total is None else total + term
    return total


def sides():
    p, there = place()
    return p, there, 1 - 2 * p, lambda reach: (HALF - reach) * p, lambda reach: reach * (1 - p)


def place_rows(dst, level, own, od, od_lo, ev, ev_lo):
    p, there = place()
    n = own.shape[0]
    dst[level, n : 2 * n] = own[...]
    if od is not None:
        dst[level, pl.ds(2 * n * p, n)] = jnp.where(there, od[od_lo : od_lo + n], 0.0)
    dst[level, pl.ds(2 * n * (1 - p), n)] = ev[ev_lo : ev_lo + n]


def first_image_kernel(s0, r0, far_s0, ev1, block, lag_s, lag_r):
    _, _, sign, _, own_start = sides()
    n = s0.shape[0]
    place_rows(lag_s, 0, s0, far_s0, 0, ev1, n + TRIM)
    place_rows(lag_r, 0, r0, None, 0, ev1, 2 * (n + TRIM))

    def whole(j, carry):
        for x in range(n):
            block[j, x] = lagged(lag_s, lag_r, (0,), x, sign * j)
        return carry

    lax.fori_loop(0, HALF + 1, whole, 0)
    for reach in range(1, HALF):
        for i in range(n - reach):
            block[HALF + reach, i] = lagged(lag_s, lag_r, (0,), own_start(reach) + i, -sign * reach)


def early_image_kernel(s4, r4, ods, evs, evr, before, block, lag_s, lag_r):
    _, _, sign, _, own_start = sides()
    n = s4.shape[0]
    place_rows(lag_s, 0, s4, ods, 0, evs, 0)
    place_rows(lag_r, 0, r4, None, 0, evr, 0)

    def whole(j, carry):
        for x in range(n):
            block[j, x] = before[j, x] + lagged(lag_s, lag_r, (0,), x, sign * j)
        return carry

    lax.fori_loop(0, HALF + 1, whole, 0)
    for reach in range(1, HALF):
        for i in range(n - reach):
            block[HALF + reach, i] = before[HALF + reach, i] + lagged(lag_s, lag_r, (0,), own_start(reach) + i, -sign * reach)


def rest_kernel(s0, s4, r0, r4, ev1, far_r, evs, odr, evr, rest, lag_s, lag_r):
    _, _, sign, far_start, _ = sides()
    n = s0.shape[0]
    place_rows(lag_s, 0, s0, None, 0, ev1, n + TRIM)
    place_rows(lag_r, 0, r0, far_r, 0, ev1, 2 * (n + TRIM))
    place_rows(lag_s, 1, s4, None, 0, evs, 0)
    place_rows(lag_r, 1, r4, odr, 0, evr, 0)
    for reach in range(1, HALF + 1):
        for i in range(reach):
            rest[reach * (reach - 1) // 2 + i] = lagged(lag_s, lag_r, (0, 1), far_start(reach) + i, -sign * reach)


def image_kernel(s8, r8, ods8, evs8, evr8, early, out, wide_s, lag_s, lag_r, block, sems):
    _, _, sign, _, own_start = sides()
    n = s8.shape[0]
    place_rows(lag_s, 0, s8, ods8, 0, evs8, 0)
    wide_s[...] = lag_s[0]
    place_rows(lag_r, 0, r8, None, 0, evr8, 0)
    move = lambda j: pltpu.make_async_copy(block.at[j], out.at[HALF + sign * j], sems.at[j])

    def whole(j, carry):
        for x in range(n):
            block[j, x] = early[j, x] + lagged(lag_s, lag_r, (0,), x, sign * j)
        move(j).start()
        return carry

    lax.fori_loop(0, HALF + 1, whole, 0)
    moves = []
    for reach in range(1, HALF):
        for i in range(n - reach):
            block[HALF + reach, i] = early[HALF + reach, i] + lagged(lag_s, lag_r, (0,), own_start(reach) + i, -sign * reach)
        target = out.at[HALF - sign * reach, pl.ds(own_start(reach), n - reach)]
        moves.append(pltpu.make_async_copy(block.at[HALF + reach, 0 : n - reach], target, sems.at[HALF + reach]))
        moves[-1].start()

    def drain(j, carry):
        move(j).wait()
        return carry

    lax.fori_loop(0, HALF + 1, drain, 0)
    for each in moves:
        each.wait()


def last_image_kernel(wide_s, odr8, rest, before, out, block, sems):
    p, there, sign, far_start, _ = sides()
    n = odr8.shape[0]
    moves = []
    for reach in range(HALF, 0, -1):
        base = reach * (reach - 1) // 2
        for i in range(reach):
            x = far_start(reach) + i
            far = jnp.where(there, odr8[x - sign * reach + n * (1 - 2 * p)], 0.0)
            block[base + i] = rest[base + i] + wide_s[HALF + x + sign * reach] * far
        target = out.at[HALF - sign * reach, pl.ds(far_start(reach), reach)]
        moves.append(pltpu.make_async_copy(block.at[base : base + reach], target, sems.at[reach - 1]))
        moves[-1].start()
    for each in moves:
        each.wait()


def estimate(flops, nbytes):
    return pl.CostEstimate(flops=flops, bytes_accessed=nbytes, transcendentals=0)


def local(source_field, source_prior, receiver_field, receiver_prior, stiffness, buoyancy, wavelet, fire_step, shot_cell, receiver_cell, traces):
    n, ny, nz = source_field.shape
    shots, count = lax.axis_size("shot"), lax.axis_size("gx")
    near = [(i, i ^ 1) for i in range(count)]
    far = [(s * count + i, s * count + i + 1) for s in range(shots) for i in range(1, count - 1, 2)]
    far = far + [(b, a) for a, b in far]
    if shots % 2 == 0:
        far += [(s * count + e, (s ^ 1) * count + e) for s in range(shots) for e in (0, count - 1)]

    def swap_near(x):
        return lax.ppermute(x, "gx", near)

    def swap_far(x):
        return lax.ppermute(x, ("shot", "gx"), far)

    hops = [2, 1] if count > 2 else [1]
    hops += [1 << bit for bit in range(count.bit_length() - 2, 1, -1)]

    def exchange(x, which):
        return lax.ppermute(x, "gx", [(i, i ^ hops[which]) for i in range(count)])

    far_s0 = swap_far(source_field)
    received = exchange(traces[None], 0)

    small = n + TRIM
    width = traces.shape[1]
    ns = shot_cell.shape[0]
    args = (
        source_field,
        source_prior,
        receiver_field,
        receiver_prior,
        stiffness,
        buoyancy,
        traces[None],
        receiver_cell.reshape(count, width),
        shot_cell.reshape(1, ns),
        fire_step.reshape(1, ns),
        wavelet.T,
    )
    packed = pl.pallas_call(
        functools.partial(pack_kernel, count=len(args)),
        out_shape=[jax.ShapeDtypeStruct(a.shape, a.dtype) for a in args]
        + [shape(n + 2 * TRIM, ny, nz), shape(small, ny, nz), shape(3 * small, ny, nz)],
        in_specs=[pl.BlockSpec(memory_space=pltpu.MemorySpace.HBM)] * len(args),
        out_specs=vmem_specs(len(args) + 3),
        scratch_shapes=[pltpu.SemaphoreType.DMA((len(args),))],
        compiler_params=params(8),
        cost_estimate=estimate(1000, 3000000),
        name="pack",
    )(*(pltpu.with_memory_space_constraint(a, pltpu.MemorySpace.HBM) for a in args))
    source_field, source_prior, receiver_field, receiver_prior, stiffness, buoyancy, gathered, cells, shot_row, fire_row, wave = packed[: len(args)]
    far_coef, far_r, ev1 = packed[len(args) :]
    far_coef = swap_far(far_coef)
    far_r = swap_far(far_r)
    ev1 = swap_near(ev1)

    gathered = jnp.concatenate([gathered, received], axis=0)
    for which in range(1, len(hops) - 1):
        gathered = jnp.concatenate([gathered, exchange(gathered, which)], axis=0)
    received = exchange(gathered, len(hops) - 1)

    plane = shape(STEPS, ny, nz)
    plane_s, *band = pl.pallas_call(
        shots_kernel,
        out_shape=[plane, jax.ShapeDtypeStruct((2 * nz, nz), bf16), jax.ShapeDtypeStruct((8 * ny, 32 * ny), bf16)],
        in_specs=vmem_specs(3),
        out_specs=vmem_specs(3),
        compiler_params=params(8),
        cost_estimate=estimate(1000000, 100000),
        name="shots",
    )(shot_row, fire_row, wave)
    plane_r = pl.pallas_call(
        functools.partial(receivers_kernel, hops=tuple(hops)),
        out_shape=plane,
        in_specs=vmem_specs(3),
        out_specs=pl.BlockSpec(memory_space=pltpu.VMEM),
        scratch_shapes=[pltpu.VMEM((STEPS * ny, nz), f32)],
        compiler_params=params(8),
        cost_estimate=estimate(2 * LANES * STEPS * ny * 2048, 1000000),
        name="receivers",
    )(cells, gathered, received)

    wide = 3 * n
    scratch = [pltpu.VMEM((wide, ny, nz), f32)] * 2 + [pltpu.VMEM((wide, ny, 2 * nz), bf16)] * 4
    cost = estimate(224 * 8 * 128 * 60, 6000000)
    own, prior = shape(n, ny, nz), shape(n + 2 * REACH, ny, nz)
    s4, s3, ods, evs, buoy, kb, kk, gg = pl.pallas_call(
        first_kernel,
        out_shape=[own, prior, shape(n + THIN, ny, nz), shape(n + THIN, ny, nz)] + [shape(wide, ny, nz)] * 4,
        in_specs=vmem_specs(10),
        out_specs=vmem_specs(8),
        scratch_shapes=scratch,
        compiler_params=params(16),
        cost_estimate=cost,
        name="first_s",
    )(source_field, source_prior, stiffness, buoyancy, far_s0, far_coef, ev1, plane_s, *band)
    coefs = (buoy, kb, kk, gg)
    ods = swap_far(ods)
    evs = swap_near(evs)
    r4, r3, odr, evr = pl.pallas_call(
        functools.partial(block_kernel, base=0, near=2 * small),
        out_shape=[own, prior, shape(n + THIN, ny, nz), shape(n + THIN, ny, nz)],
        in_specs=vmem_specs(11),
        out_specs=vmem_specs(4),
        scratch_shapes=scratch,
        compiler_params=params(16),
        cost_estimate=cost,
        name="first_r",
    )(receiver_field, receiver_prior, far_r, ev1, plane_r, *band, *coefs)
    odr = swap_far(odr)
    evr = swap_near(evr)

    def last():
        return pl.pallas_call(
            functools.partial(last_kernel, base=IMG_EVERY),
            out_shape=own,
            in_specs=vmem_specs(11),
            out_specs=pl.BlockSpec(memory_space=pltpu.VMEM),
            scratch_shapes=scratch,
            compiler_params=params(16),
            cost_estimate=cost,
        )

    s8 = last()(s4, s3, ods, evs, plane_s, *band, *coefs)
    ods8 = swap_far(s8)
    evs8 = swap_near(s8)
    r8 = last()(r4, r3, odr, evr, plane_r, *band, *coefs)
    odr8 = swap_far(r8)
    evr8 = swap_near(r8)
    lags = lambda levels: [pltpu.VMEM((levels, wide, ny, nz), f32)] * 2
    corner = HALF * (HALF + 1) // 2
    hbm = pl.BlockSpec(memory_space=pltpu.MemorySpace.HBM)

    def products(kernel, *inputs):
        return pl.pallas_call(
            kernel,
            out_shape=shape(2 * HALF, n, ny, nz),
            in_specs=vmem_specs(len(inputs)),
            out_specs=pl.BlockSpec(memory_space=pltpu.VMEM),
            scratch_shapes=lags(1),
            compiler_params=params(8),
            cost_estimate=estimate(NOFF * n * ny * nz * 3, 1000000),
        )(*inputs)

    early = products(first_image_kernel, source_field, receiver_field, far_s0, ev1)
    early = products(early_image_kernel, s4, r4, ods, evs, evr, early)
    rest = pl.pallas_call(
        rest_kernel,
        out_shape=shape(corner, ny, nz),
        in_specs=vmem_specs(9),
        out_specs=pl.BlockSpec(memory_space=pltpu.VMEM),
        scratch_shapes=lags(2),
        compiler_params=params(8),
        cost_estimate=estimate(1000000, 1000000),
        name="rest",
    )(source_field, s4, receiver_field, r4, ev1, far_r, evs, odr, evr)
    image, wide_s = pl.pallas_call(
        image_kernel,
        out_shape=[shape(NOFF, n, ny, nz), shape(wide, ny, nz)],
        in_specs=vmem_specs(6),
        out_specs=[hbm, pl.BlockSpec(memory_space=pltpu.VMEM)],
        scratch_shapes=lags(1) + [pltpu.VMEM((2 * HALF, n, ny, nz), f32), pltpu.SemaphoreType.DMA((2 * HALF,))],
        compiler_params=params(16),
        cost_estimate=estimate(NOFF * n * ny * nz * 4, 4400000),
        name="image",
    )(s8, r8, ods8, evs8, evr8, early)
    return pl.pallas_call(
        last_image_kernel,
        out_shape=shape(NOFF, n, ny, nz),
        in_specs=vmem_specs(3) + [hbm],
        out_specs=hbm,
        scratch_shapes=[pltpu.VMEM((corner, ny, nz), f32), pltpu.SemaphoreType.DMA((HALF,))],
        input_output_aliases={3: 0},
        compiler_params=params(16),
        cost_estimate=estimate(HALF * n * ny * nz * 2, 2200000),
        name="last_image",
    )(wide_s, odr8, rest, image)


def solution(mesh):
    placed = (
        P(("shot", "gx"), None, None),
        P(("shot", "gx"), None, None),
        P(("shot", "gx"), None, None),
        P(("shot", "gx"), None, None),
        P("gx", None, None),
        P("gx", None, None),
        P("shot", None),
        P("shot"),
        P("shot"),
        P("shot"),
        P("shot", "gx"),
    )
    return jax.shard_map(local, mesh=mesh, in_specs=placed, out_specs=P("shot", "gx", None, None), check_vma=False)
```
